32 devices in a mesh: dp: 4 (over y, x), seq: 8 (over z, core).
Axes of the slice: x: 2, y: 2, z: 4, core: 2. Of those that a mesh axis runs over, the one named last changes fastest.
Arguments:
- layer_input: bfloat16 [8, 2048, 2048], P('dp', 'seq'), may hold values from -6 to 6
- doc_lengths: int32 [8, 8], P('dp'), may hold values from 1 to 1024, 2048 in all within a row
- attn_norm: float32 [2048], replicated, may hold values from 0.5 to 1.5
- q_norm: float32 [128], replicated, may hold values from 0.5 to 1.5
- k_norm: float32 [128], replicated, may hold values from 0.5 to 1.5
- ffn_norm: float32 [2048], replicated, may hold values from 0.5 to 1.5
- w_qkv: bfloat16 [4096, 2048], P('dp'), may hold values from -0.125 to 0.125
- w_gate: bfloat16 [16, 2048], P('dp'), may hold values from -0.125 to 0.125
- w_out: bfloat16 [2048, 2048], P('dp'), may hold values from -1.5 to 1.5
- w_gu: bfloat16 [12288, 2048], P('dp'), may hold values from -0.125 to 0.125
- w_down: bfloat16 [2048, 6144], P('dp'), may hold values from -0.078125 to 0.078125
- cotangent: bfloat16 [8, 2048, 2048], P('dp', 'seq'), may hold values from -6 to 6
Outputs:
- output: bfloat16 [8, 2048, 2048], P('dp', 'seq')
- grad_input: bfloat16 [8, 2048, 2048], P('dp', 'seq')
- grad_attn_norm: float32 [2048], replicated
- grad_q_norm: float32 [128], replicated
- grad_k_norm: float32 [128], replicated
- grad_ffn_norm: float32 [2048], replicated
- grad_w_qkv: float32 [4096, 2048], P('dp')
- grad_w_gate: float32 [16, 2048], P('dp')
- grad_w_out: float32 [2048, 2048], P('dp')
- grad_w_gu: float32 [12288, 2048], P('dp')
- grad_w_down: float32 [2048, 6144], P('dp')
The draws below stay inside these ranges and needn't reach their ends.
Inputs may be any that keep to these rules, and one draw needn't show every extreme that they name: `doc_lengths`: each row's 8 lengths add up to 2048, and the longest one of each row is exactly 1024.
All inputs are finite; a program needn't handle non-finite values.
Results may differ from the reference program's by a relative error of at most 0.02.
Values may be sent and summed in bfloat16 or wider, within the bound.
No kernel may reach another device: no remote copies, remote signals or barrier semaphores. Data moves between devices by JAX's collectives and lax.ppermute only.
A program may use at most 512 MiB of HBM per device.

```python
import math
import jax
import jax.numpy as jnp
import numpy as np
from jax import lax

D = 2048
QUERY_HEADS = 16
KEY_VALUE_HEADS = 8
HEAD_SIZE = 128
FF = 6144
ROW = 2048
DOCS = 8
MOST_DOC = 1024
ROWS = 8
QKV_ROWS = 4096


def shard_levels(rng, shape, shards, least, high):
    level = 1.0
    for dim, blocks in shards:
        steps = jax.random.uniform(jax.random.fold_in(jax.random.fold_in(rng, 6), dim), (blocks,), jnp.float32, least / len(shards), high / len(shards))
        level = level * jnp.repeat(jnp.exp(steps), shape[dim] // blocks).reshape((-1,) + (1,) * (len(shape) - 1 - dim))
    return level


def profile(amount, total, most, lean):
    loads = [(1 << 20) // math.isqrt(standing ** lean) + 1 for standing in range(2, amount + 1)]
    spare, holding = total - most - (amount - 1), [1] * (amount - 1)
    while spare > 0:
        free = [i for i in range(amount - 1) if holding[i] < most]
        mass, left = sum([loads[i] for i in free]), spare
        for i in free:
            more = min(most - holding[i], max(1, left * loads[i] // mass), spare)
            holding[i] = holding[i] + more
            spare = spare - more
    return np.array([most] + holding)


def uneven(own_key, number_of, total, bound, slope):
    if number_of == 2:
        one = jax.random.randint(own_key, (), max(1, total - bound), min(bound, total - 1) + 1)
        return jnp.stack([one, total - one])
    sizes = jnp.asarray(profile(number_of, total, bound, slope), jnp.int32)
    couples = (number_of - 1) // 2
    source_of, receiver = sizes[1:1 + 2 * couples:2], sizes[2:2 + 2 * couples:2]
    room = jnp.minimum(source_of - 1, bound - receiver)
    shifted = jax.random.randint(jax.random.fold_in(own_key, 1), (couples,), 0, 1 << 20) % (room + 1)
    sizes = sizes.at[1:1 + 2 * couples:2].set(source_of - shifted).at[2:2 + 2 * couples:2].set(receiver + shifted)
    return sizes[jax.random.permutation(jax.random.fold_in(own_key, 2), number_of)]


def noise(key, extent, deviation, bound, shards=(), held_as=jnp.bfloat16):
    factor_of = shard_levels(key, extent, shards, -0.22, 0.18) if shards else 1.0
    entries = jax.random.normal(key, extent, jnp.float32) * deviation * factor_of
    return jnp.minimum(jnp.maximum(entries, -bound), bound).astype(held_as)


def setup_inputs(seed: int = 0) -> dict:
    streams_of = jax.random.split(jax.random.key(seed), 13)
    return {
        "layer_input": noise(streams_of[0], (ROWS, ROW, D), 1.0, 6.0, ((0, 4), (1, 8))),
        "doc_lengths": jax.vmap(lambda own: uneven(own, DOCS, ROW, MOST_DOC, 2))(jax.random.split(streams_of[1], ROWS)).reshape((ROWS, DOCS)).astype(jnp.int32),
        "attn_norm": jnp.clip(1.0 + 0.1 * jax.random.normal(streams_of[2], (D,), jnp.float32), 0.5, 1.5),
        "q_norm": jnp.clip(1.0 + 0.1 * jax.random.normal(streams_of[3], (HEAD_SIZE,), jnp.float32), 0.5, 1.5),
        "k_norm": jnp.clip(1.0 + 0.1 * jax.random.normal(streams_of[4], (HEAD_SIZE,), jnp.float32), 0.5, 1.5),
        "ffn_norm": jnp.clip(1.0 + 0.1 * jax.random.normal(streams_of[5], (D,), jnp.float32), 0.5, 1.5),
        "w_qkv": noise(streams_of[6], (QKV_ROWS, D), D ** -0.5, 0.125, ((0, 4),)),
        "w_gate": noise(streams_of[7], (QUERY_HEADS, D), D ** -0.5, 0.125, ((0, 4),)),
        "w_out": noise(streams_of[8], (D, QUERY_HEADS * HEAD_SIZE), 16 ** -0.5, 1.5, ((0, 4),)),
        "w_gu": noise(streams_of[9], (2 * FF, D), D ** -0.5, 0.125, ((0, 4),)),
        "w_down": noise(streams_of[10], (D, FF), FF ** -0.5, 0.078125, ((0, 4),)),
        "cotangent": noise(streams_of[11], (ROWS, ROW, D), 1.0, 6.0, ((0, 4), (1, 8))),
    }


epsilon = 1e-06
theta_base = 1000000.0
masked_score = -1e+30

@jax.custom_vjp
def low(v):
    return lax.optimization_barrier(v.astype(jnp.bfloat16)).astype(jnp.float32)

@jax.custom_vjp
def low_back(v):
    return v

def low_keep(v):
    return (low(v), None)

def low_pass(kept, grad):
    return (grad,)

def back_keep(v):
    return (v, None)

def back_low(kept, grad):
    return (low(grad),)
low.defvjp(low_keep, low_pass)
low_back.defvjp(back_keep, back_low)

def product(left, right):
    return jnp.dot(left, right.T, precision=lax.Precision.HIGHEST, preferred_element_type=jnp.float32)

def normalize(value, gain):
    return value * lax.rsqrt(lax.optimization_barrier(jnp.mean(value * value, axis=-1, keepdims=True)) + epsilon) * gain

def rotate(value, cosine, sine):
    half = value.shape[-1] // 2
    turned = jnp.concatenate([-value[..., half:], value[..., :half]], axis=-1)
    return value * cosine + turned * sine

def doc_positions(lengths, row_length_tokens):
    ends = jnp.cumsum(lengths, axis=-1).astype(jnp.int32)
    starts = (ends - lengths).astype(jnp.int32)
    places = jnp.arange(row_length_tokens, dtype=jnp.int32)
    segment = lax.optimization_barrier(jnp.sum((places[:, None] >= ends[..., None, :]).astype(jnp.int32), axis=-1)).astype(jnp.int32)
    owners = segment[..., None] == jnp.arange(lengths.shape[-1], dtype=jnp.int32)
    first = lax.optimization_barrier(jnp.sum(jnp.where(owners, starts[..., None, :], 0), axis=-1)).astype(jnp.int32)
    return (segment, (places - first).astype(jnp.int32))

def rope_tables(position):
    freq = jnp.power(theta_base, -(jnp.arange(HEAD_SIZE // 2, dtype=jnp.float32) * 2.0) / HEAD_SIZE)
    angle = position.astype(jnp.float32)[..., None] * freq
    both = jnp.concatenate([angle, angle], axis=-1)
    return (jnp.cos(both), jnp.sin(both))

def attention(queries, keys, values, segment):
    row_length_tokens = queries.shape[0]
    block = min(512, row_length_tokens)
    blocks = row_length_tokens // block
    scale = 1.0 / math.sqrt(HEAD_SIZE)
    places = jnp.arange(row_length_tokens, dtype=jnp.int32)
    query_blocks = queries.reshape(blocks, block, QUERY_HEADS, HEAD_SIZE)
    segment_blocks = segment.reshape(blocks, block)
    place_blocks = places.reshape(blocks, block)

    def one_block(item):
        query_block, segment_block, place_block = item
        scores = jnp.einsum('qhd,khd->hqk', query_block, keys, precision=lax.Precision.HIGHEST) * scale
        scores = low_back(scores)
        allowed = (segment_block[:, None] == segment[None, :]) & (place_block[:, None] >= places[None, :])
        scores = jnp.where(allowed[None], scores, masked_score)
        peak = lax.optimization_barrier(jnp.max(scores, axis=-1, keepdims=True))
        weights = jnp.exp(scores - peak)
        probs = weights / lax.optimization_barrier(jnp.sum(weights, axis=-1, keepdims=True))
        return jnp.einsum('hqk,khd->qhd', low(probs), values, precision=lax.Precision.HIGHEST)
    outs = lax.map(jax.checkpoint(one_block), (query_blocks, segment_blocks, place_blocks))
    return outs.reshape(row_length_tokens, QUERY_HEADS, HEAD_SIZE)

def layer_row(input_row, lengths_row, gains, weights):
    attn_norm, q_norm, k_norm, ffn_norm = gains
    w_qkv, w_gate, w_out, w_gu, w_down = weights
    row_length_tokens = input_row.shape[0]
    group_repeat_count = QUERY_HEADS // KEY_VALUE_HEADS
    segment, position = doc_positions(lengths_row, row_length_tokens)
    cosine, sine = rope_tables(position)
    cosine = cosine[:, None, :]
    sine = sine[:, None, :]
    normed_a = low(normalize(input_row, attn_norm))
    projected_rows = low_back(product(normed_a, w_qkv))
    gate_logit = low_back(product(normed_a, w_gate))
    query_raw = projected_rows[:, :QUERY_HEADS * HEAD_SIZE].reshape(row_length_tokens, QUERY_HEADS, HEAD_SIZE)
    unnormed_key = projected_rows[:, QUERY_HEADS * HEAD_SIZE:(QUERY_HEADS + KEY_VALUE_HEADS) * HEAD_SIZE].reshape(row_length_tokens, KEY_VALUE_HEADS, HEAD_SIZE)
    unnormed_value = projected_rows[:, (QUERY_HEADS + KEY_VALUE_HEADS) * HEAD_SIZE:].reshape(row_length_tokens, KEY_VALUE_HEADS, HEAD_SIZE)
    queries = low(low_back(rotate(normalize(query_raw, q_norm), cosine, sine)))
    keys = low(low_back(jnp.repeat(rotate(normalize(unnormed_key, k_norm), cosine, sine), group_repeat_count, axis=1)))
    values = low(low_back(jnp.repeat(unnormed_value, group_repeat_count, axis=1)))
    attn = low(low_back(attention(queries, keys, values, segment)))
    gated = low(attn * jax.nn.sigmoid(gate_logit)[:, :, None]).reshape(row_length_tokens, QUERY_HEADS * HEAD_SIZE)
    mid = input_row + low_back(product(gated, w_out))
    normed_f = low(normalize(mid, ffn_norm))
    gate_up = low_back(product(normed_f, w_gu))
    hidden = low(jax.nn.silu(gate_up[:, :FF]) * gate_up[:, FF:])
    return mid + low_back(product(hidden, w_down))

def reference(layer_input, doc_lengths, attn_norm, q_norm, k_norm, ffn_norm, w_qkv, w_gate, w_out, w_gu, w_down, cotangent):
    inputs = layer_input.astype(jnp.float32)
    gains = (attn_norm, q_norm, k_norm, ffn_norm)
    weights = (w_qkv.astype(jnp.float32), w_gate.astype(jnp.float32), w_out.astype(jnp.float32), w_gu.astype(jnp.float32), w_down.astype(jnp.float32))

    def forward(inputs, gains, weights):

        def step(carry, item):
            input_row, lengths_row = item
            return (carry, layer_row(input_row, lengths_row, gains, weights))
        unused, result = lax.scan(step, jnp.zeros((), jnp.float32), (inputs, doc_lengths))
        return result
    result, pull = jax.vjp(forward, inputs, gains, weights)
    d_inputs, d_gains, d_weights = pull(cotangent.astype(jnp.float32))
    return (result.astype(jnp.bfloat16), d_inputs.astype(jnp.bfloat16), d_gains[0], d_gains[1], d_gains[2], d_gains[3], d_weights[0], d_weights[1], d_weights[2], d_weights[3], d_weights[4])
```

```python
import functools
import math

import jax
import jax.numpy as jnp
from jax import lax
from jax.experimental import pallas as pl
from jax.experimental.pallas import tpu as pltpu
from jax.sharding import PartitionSpec as P

QUERY_HEADS = 16
KEY_VALUE_HEADS = 8
HEAD = 128
FF = 6144
CORES = 2

GROUP = QUERY_HEADS // KEY_VALUE_HEADS
CORE_Q = QUERY_HEADS // CORES
CORE_KV = KEY_VALUE_HEADS // CORES
epsilon = 1e-06
theta_base = 1000000.0
SCALE = 1.0 / math.sqrt(HEAD)
SCALE2 = SCALE * math.log2(math.e)
BF = jnp.bfloat16
F32 = jnp.float32


def dot_nt(left, right, out=F32):
    return lax.dot_general(left, right, (((1,), (1,)), ((), ())), preferred_element_type=F32).astype(out)


def dot_nn(left, right, out=F32):
    return lax.dot_general(left, right, (((1,), (0,)), ((), ())), preferred_element_type=F32).astype(out)


def dot_tn(left, right, out=F32):
    return lax.dot_general(left, right, (((0,), (0,)), ((), ())), preferred_element_type=F32).astype(out)


def doc_positions(lengths, total):
    ends = jnp.cumsum(lengths, axis=-1)
    starts = ends - lengths
    places = jnp.arange(total, dtype=jnp.int32)
    segment = jnp.sum((places[:, None] >= ends[..., None, :]).astype(jnp.int32), axis=-1)
    owners = segment[..., None] == jnp.arange(lengths.shape[-1], dtype=jnp.int32)
    first = jnp.sum(jnp.where(owners, starts[..., None, :], 0), axis=-1)
    return first, places - first


def pack_kernel(chips, proj_ref, cos_ref, sin_ref, qg_ref, kg_ref, out_ref):
    per = CORE_Q // chips
    copies = max(1, chips // CORE_KV)
    cos = cos_ref[...]
    sin = sin_ref[...]

    def head(index, gain):
        u = proj_ref[:, index * HEAD : (index + 1) * HEAD]
        factor = lax.rsqrt(jnp.mean(u * u, axis=-1, keepdims=True) + epsilon)
        n = u * factor * gain
        return (n * cos + pltpu.roll(n, HEAD // 2, 1) * sin).astype(BF)

    for z in range(chips):
        for h in range(per):
            out_ref[z, :, h * HEAD : (h + 1) * HEAD] = head(z * per + h, qg_ref[...])
        if z % copies == 0:
            kv = z // copies
            key = head(CORE_Q + kv, kg_ref[...])
            base = (CORE_Q + CORE_KV + kv) * HEAD
            value = proj_ref[:, base : base + HEAD].astype(BF)
        out_ref[z, :, per * HEAD : (per + 1) * HEAD] = key
        out_ref[z, :, (per + 1) * HEAD : (per + 2) * HEAD] = value


def pack_heads(proj, cos, sin, q_gain, k_gain, row, chips, chip_tok):
    per = CORE_Q // chips
    lanes = (per + 2) * HEAD
    block = min(256, chip_tok)
    steps = chip_tok // block
    width = proj.shape[1]
    tok = lambda i: (row * steps + i, 0)
    return pl.pallas_call(
        functools.partial(pack_kernel, chips),
        grid=(steps,),
        in_specs=[
            pl.BlockSpec((block, width), tok),
            pl.BlockSpec((block, HEAD), tok),
            pl.BlockSpec((block, HEAD), tok),
            pl.BlockSpec((1, HEAD), lambda i: (0, 0)),
            pl.BlockSpec((1, HEAD), lambda i: (0, 0)),
        ],
        out_specs=pl.BlockSpec((chips, block, lanes), lambda i: (0, i, 0)),
        out_shape=jax.ShapeDtypeStruct((chips, chip_tok, lanes), BF),
        name="pack_heads",
    )(proj, cos, sin, q_gain, k_gain)


def unpack_kernel(chips, grad_ref, proj_ref, cos_ref, sin_ref, qg_ref, kg_ref, out_ref, qs_ref, ks_ref):
    per = CORE_Q // chips
    copies = max(1, chips // CORE_KV)
    cos = cos_ref[...]
    sin = sin_ref[...]

    @pl.when(pl.program_id(0) == 0)
    def _():
        qs_ref[...] = jnp.zeros_like(qs_ref)
        ks_ref[...] = jnp.zeros_like(ks_ref)

    def head(e, index, gain, sum_ref):
        e = e * cos + pltpu.roll(e * sin, HEAD // 2, 1)
        u = proj_ref[:, index * HEAD : (index + 1) * HEAD]
        factor = lax.rsqrt(jnp.mean(u * u, axis=-1, keepdims=True) + epsilon)
        n = u * factor
        sum_ref[...] += jnp.sum((e * n).reshape(-1, 8, HEAD), axis=0)
        weighted = e * gain
        inner = jnp.mean(weighted * n, axis=-1, keepdims=True)
        out_ref[:, index * HEAD : (index + 1) * HEAD] = (factor * (weighted - n * inner)).astype(BF)

    def part(z, lane):
        return grad_ref[z, :, lane * HEAD : (lane + 1) * HEAD].astype(F32)

    for z in range(chips):
        for h in range(per):
            head(part(z, h), z * per + h, qg_ref[...], qs_ref)
    for kv in range(CORE_KV):
        spread = range(kv * copies, (kv + 1) * copies)
        head(sum(part(z, per) for z in spread), CORE_Q + kv, kg_ref[...], ks_ref)
        base = (CORE_Q + CORE_KV + kv) * HEAD
        out_ref[:, base : base + HEAD] = sum(part(z, per + 1) for z in spread).astype(BF)


def unpack_heads(grads, proj, cos, sin, q_gain, k_gain, row, chips, chip_tok):
    lanes = grads.shape[2]
    block = min(256, chip_tok)
    steps = chip_tok // block
    width = proj.shape[1]
    tok = lambda i: (row * steps + i, 0)
    small = pl.BlockSpec((8, HEAD), lambda i: (0, 0))
    return pl.pallas_call(
        functools.partial(unpack_kernel, chips),
        grid=(steps,),
        in_specs=[
            pl.BlockSpec((chips, block, lanes), lambda i: (0, i, 0)),
            pl.BlockSpec((block, width), tok),
            pl.BlockSpec((block, HEAD), tok),
            pl.BlockSpec((block, HEAD), tok),
            pl.BlockSpec((1, HEAD), lambda i: (0, 0)),
            pl.BlockSpec((1, HEAD), lambda i: (0, 0)),
        ],
        out_specs=[pl.BlockSpec((block, width), lambda i: (i, 0)), small, small],
        out_shape=[
            jax.ShapeDtypeStruct((chip_tok, width), BF),
            jax.ShapeDtypeStruct((8, HEAD), F32),
            jax.ShapeDtypeStruct((8, HEAD), F32),
        ],
        name="unpack_heads",
    )(grads, proj, cos, sin, q_gain, k_gain)


def visible(j, size, start, diagonal):
    inner = lax.broadcasted_iota(jnp.int32, (size, size), 0)
    allowed = inner >= start - j * size
    if diagonal:
        allowed = allowed & (inner <= lax.broadcasted_iota(jnp.int32, (size, size), 1))
    return allowed


def attend_kernel(per, low_ref, q_ref, k_ref, v_ref, start_ref, out_ref, log_ref, acc_ref, sum_ref):
    i = pl.program_id(0)
    size = q_ref.shape[1]
    start = start_ref[...]
    acc_ref[...] = jnp.zeros_like(acc_ref)
    sum_ref[...] = jnp.zeros_like(sum_ref)

    def one(j, diagonal):
        key = k_ref[j]
        value = v_ref[j]
        allowed = visible(j, size, start, diagonal)
        for h in range(per):
            scores = dot_nt(key, q_ref[0, :, h * HEAD : (h + 1) * HEAD])
            p = jnp.where(allowed, jnp.exp2(scores * SCALE2), 0.0)
            sum_ref[h : h + 1, :] += jnp.sum(p, axis=0, keepdims=True)
            acc_ref[h] += dot_tn(value, p.astype(BF))

    def step(j, carry):
        one(j, False)
        return carry

    lax.fori_loop(low_ref[i], i, step, 0)
    one(i, True)
    for h in range(per):
        total = sum_ref[h : h + 1, :]
        out_ref[0, :, h * HEAD : (h + 1) * HEAD] = (acc_ref[h] / total).T.astype(BF)
        log_ref[h : h + 1, :] = jnp.log2(total)


def attend(packed, start, low):
    chips, size, lanes = packed.shape
    per = lanes // HEAD - 2
    return pl.pallas_call(
        functools.partial(attend_kernel, per),
        grid_spec=pltpu.PrefetchScalarGridSpec(
            num_scalar_prefetch=1,
            grid=(chips,),
            in_specs=[
                pl.BlockSpec((1, size, per * HEAD), lambda i, low: (i, 0, 0)),
                pl.BlockSpec((chips, size, HEAD), lambda i, low: (0, 0, per)),
                pl.BlockSpec((chips, size, HEAD), lambda i, low: (0, 0, per + 1)),
                pl.BlockSpec((1, size), lambda i, low: (0, i)),
            ],
            out_specs=[
                pl.BlockSpec((1, size, per * HEAD), lambda i, low: (i, 0, 0)),
                pl.BlockSpec((per, size), lambda i, low: (0, i)),
            ],
            scratch_shapes=[pltpu.VMEM((per, HEAD, size), F32), pltpu.VMEM((per, size), F32)],
        ),
        out_shape=[
            jax.ShapeDtypeStruct((chips, size, per * HEAD), BF),
            jax.ShapeDtypeStruct((per, chips * size), F32),
        ],
        name="attend",
    )(low, packed, packed, packed, start)


def attend_back_kernel(
    per, low_ref, q_ref, k_ref, v_ref, grad_ref, res_ref, log_ref, start_ref, out_ref, dq_ref, dk_ref, dv_ref
):
    i = pl.program_id(0)
    size = q_ref.shape[1]
    start = start_ref[...]

    @pl.when(i == 0)
    def _():
        dk_ref[...] = jnp.zeros_like(dk_ref)
        dv_ref[...] = jnp.zeros_like(dv_ref)

    dq_ref[...] = jnp.zeros_like(dq_ref)
    ones = jnp.ones((8, HEAD), F32)
    inner = []
    for h in range(per):
        cols = slice(h * HEAD, (h + 1) * HEAD)
        both = grad_ref[0, :, cols].astype(F32) * res_ref[0, :, cols].astype(F32)
        sums = lax.dot_general(
            ones, both, (((1,), (1,)), ((), ())), precision=lax.Precision.HIGHEST, preferred_element_type=F32
        )
        inner.append(sums[0:1, :])

    def one(j, diagonal):
        key = k_ref[j]
        value = v_ref[j]
        allowed = visible(j, size, start, diagonal)
        for h in range(per):
            query = q_ref[0, :, h * HEAD : (h + 1) * HEAD]
            grad = grad_ref[0, :, h * HEAD : (h + 1) * HEAD]
            scores = dot_nt(key, query)
            p = jnp.where(allowed, jnp.exp2(scores * SCALE2 - log_ref[h : h + 1, :]), 0.0)
            dp = dot_nt(value, grad)
            ds = (p * (dp - inner[h])).astype(BF)
            dv_ref[j] += dot_nn(p.astype(BF), grad)
            dk_ref[j] += dot_nn(ds, query)
            dq_ref[h] += dot_tn(ds, key)

    def step(j, carry):
        one(j, False)
        return carry

    lax.fori_loop(low_ref[i], i, step, 0)
    one(i, True)
    for h in range(per):
        out_ref[i, :, h * HEAD : (h + 1) * HEAD] = (dq_ref[h] * SCALE).astype(BF)

    @pl.when(i == pl.num_programs(0) - 1)
    def _():
        out_ref[:, :, per * HEAD : (per + 1) * HEAD] = (dk_ref[...] * SCALE).astype(BF)
        out_ref[:, :, (per + 1) * HEAD : (per + 2) * HEAD] = dv_ref[...].astype(BF)


def attend_back(packed, grad, result, logs, start, low):
    chips, size, lanes = packed.shape
    per = lanes // HEAD - 2
    one = pl.BlockSpec((1, size, per * HEAD), lambda i, low: (i, 0, 0))
    return pl.pallas_call(
        functools.partial(attend_back_kernel, per),
        grid_spec=pltpu.PrefetchScalarGridSpec(
            num_scalar_prefetch=1,
            grid=(chips,),
            in_specs=[
                one,
                pl.BlockSpec((chips, size, HEAD), lambda i, low: (0, 0, per)),
                pl.BlockSpec((chips, size, HEAD), lambda i, low: (0, 0, per + 1)),
                one,
                one,
                pl.BlockSpec((per, size), lambda i, low: (0, i)),
                pl.BlockSpec((1, size), lambda i, low: (0, i)),
            ],
            out_specs=pl.BlockSpec((chips, size, lanes), lambda i, low: (0, 0, 0)),
            scratch_shapes=[
                pltpu.VMEM((per, size, HEAD), F32),
                pltpu.VMEM((chips, size, HEAD), F32),
                pltpu.VMEM((chips, size, HEAD), F32),
            ],
        ),
        out_shape=jax.ShapeDtypeStruct((chips, size, lanes), BF),
        name="attend_back",
    )(low, packed, packed, packed, grad, result, logs, start)


def gate_kernel(res_ref, logit_ref, out_ref):
    chips, _, lanes = res_ref.shape
    per = lanes // HEAD
    sig = jax.nn.sigmoid(logit_ref[...])
    for z in range(chips):
        for h in range(per):
            head = z * per + h
            value = res_ref[z, :, h * HEAD : (h + 1) * HEAD].astype(F32)
            out_ref[:, head * HEAD : (head + 1) * HEAD] = (value * sig[:, head : head + 1]).astype(BF)


def gate_rows(result, logits, row):
    chips, size, lanes = result.shape
    block = min(256, size)
    steps = size // block
    return pl.pallas_call(
        gate_kernel,
        grid=(steps,),
        in_specs=[
            pl.BlockSpec((chips, block, lanes), lambda i: (0, i, 0)),
            pl.BlockSpec((block, HEAD), lambda i: (row * steps + i, 0)),
        ],
        out_specs=pl.BlockSpec((block, chips * lanes), lambda i: (i, 0)),
        out_shape=jax.ShapeDtypeStruct((size, chips * lanes), BF),
        name="gate_rows",
    )(result, logits)


def gate_back_kernel(grad_ref, res_ref, logit_ref, out_ref, dlogit_ref):
    chips, size, lanes = res_ref.shape
    per = lanes // HEAD
    sig = jax.nn.sigmoid(logit_ref[...])
    lane = lax.broadcasted_iota(jnp.int32, sig.shape, 1)
    sums = jnp.zeros(sig.shape, F32)
    for z in range(chips):
        for h in range(per):
            head = z * per + h
            e = grad_ref[:, head * HEAD : (head + 1) * HEAD]
            value = res_ref[z, :, h * HEAD : (h + 1) * HEAD].astype(F32)
            out_ref[z, :, h * HEAD : (h + 1) * HEAD] = (e * sig[:, head : head + 1]).astype(BF)
            sums = jnp.where(lane == head, jnp.sum(e * value, axis=-1, keepdims=True), sums)
    dlogit_ref[...] = (sums * sig * (1.0 - sig)).astype(BF)


def gate_back(grad, result, logits, row):
    chips, size, lanes = result.shape
    block = min(256, size)
    steps = size // block
    return pl.pallas_call(
        gate_back_kernel,
        grid=(steps,),
        in_specs=[
            pl.BlockSpec((block, chips * lanes), lambda i: (i, 0)),
            pl.BlockSpec((chips, block, lanes), lambda i: (0, i, 0)),
            pl.BlockSpec((block, HEAD), lambda i: (row * steps + i, 0)),
        ],
        out_specs=[
            pl.BlockSpec((chips, block, lanes), lambda i: (0, i, 0)),
            pl.BlockSpec((block, HEAD), lambda i: (i, 0)),
        ],
        out_shape=[jax.ShapeDtypeStruct((chips, size, lanes), BF), jax.ShapeDtypeStruct((size, HEAD), BF)],
        name="gate_back",
    )(grad, result, logits)


def shards(
    layer_input,
    doc_lengths,
    attn_norm,
    q_norm,
    k_norm,
    ffn_norm,
    w_qkv,
    w_gate,
    w_out,
    w_gu,
    w_down,
    cotangent,
):
    rows, tok, width = layer_input.shape
    seq = lax.axis_size("seq")
    dp = lax.axis_size("dp")
    chips = seq // CORES
    place = lax.axis_index("seq")
    core = place % CORES
    chip = place // CORES
    first = core == 0
    chip_tok = tok * CORES
    length = tok * seq
    tokens = rows * chip_tok
    pair = [(s, s ^ 1) for s in range(seq)]
    groups = [[z * CORES + c for z in range(chips)] for c in range(CORES)]
    q_shard = lax.axis_index("dp") * w_qkv.shape[0] < QUERY_HEADS * HEAD

    def swap(x):
        return lax.ppermute(x, "seq", pair)

    def pick(a, b):
        return jnp.where(first, a, b)

    def both(x):
        other = swap(x)
        return jnp.concatenate([pick(x, other), pick(other, x)], axis=1).reshape(tokens, width)

    def own(x):
        x = x.reshape(rows, CORES, tok, width)
        return pick(x[:, 0], x[:, 1])

    def pair_sum(x):
        return x.astype(F32) + swap(x).astype(F32)

    def exchange(x):
        return lax.all_to_all(x, "seq", 0, 0, axis_index_groups=groups, tiled=True)

    def chip_sum(x):
        if chips != 4:
            return lax.psum(x, "seq", axis_index_groups=groups)
        inward = [(c, 2 + c) for c in range(CORES)] + [(6 + c, 4 + c) for c in range(CORES)]
        middle = [(2 + c, 4 + c) for c in range(CORES)] + [(4 + c, 2 + c) for c in range(CORES)]
        outward = [(2 + c, c) for c in range(CORES)] + [(4 + c, 6 + c) for c in range(CORES)]
        half = x + lax.ppermute(x, "seq", inward)
        full = half + lax.ppermute(half, "seq", middle)
        spread = lax.ppermute(full, "seq", outward)
        return jnp.where((chip == 1) | (chip == 2), full, spread)

    def total_sum(x):
        for name, size in (("seq", seq), ("dp", dp)):
            step = 1
            while step < size:
                x = x + lax.ppermute(x, name, [(s, s ^ step) for s in range(size)])
                step *= 2
        return x

    def scatter(x):
        return lax.psum_scatter(x, "dp", scatter_dimension=0, tiled=True)

    def gather(x):
        return lax.all_gather(x, "dp", axis=0, tiled=True)

    def core_rows(w, unit):
        return jnp.concatenate(
            [pick(w[a : a + unit], w[a + unit : a + 2 * unit]) for a in range(0, w.shape[0], 2 * unit)], axis=0
        )

    def core_cols(w, unit):
        return jnp.concatenate(
            [pick(w[:, a : a + unit], w[:, a + unit : a + 2 * unit]) for a in range(0, w.shape[1], 2 * unit)],
            axis=1,
        )

    def join_rows(low, high, unit):
        parts = []
        for a in range(0, low.shape[0], unit):
            parts += [low[a : a + unit], high[a : a + unit]]
        return jnp.concatenate(parts, axis=0)

    def join_cols(low, high, unit):
        parts = []
        for a in range(0, low.shape[1], unit):
            parts += [low[:, a : a + unit], high[:, a : a + unit]]
        return jnp.concatenate(parts, axis=1)

    ff_unit = w_gu.shape[0] // CORES
    qkv_half = jnp.where(q_shard, core_rows(w_qkv, GROUP * HEAD), core_rows(w_qkv, HEAD))
    qkv_full = gather(qkv_half)
    gate_full = gather(w_gate)
    out_full = gather(core_cols(w_out, GROUP * HEAD))
    gu_full = gather(core_rows(w_gu, ff_unit))
    down_full = gather(core_cols(w_down, ff_unit))
    gate_core = jnp.pad(core_rows(gate_full, GROUP), ((0, HEAD - CORE_Q), (0, 0)))

    start, position = doc_positions(doc_lengths, length)
    low = start.reshape(rows, chips, chip_tok)[:, :, 0] // chip_tok
    local = lax.dynamic_slice_in_dim(position, chip * chip_tok, chip_tok, 1).reshape(tokens)
    freq = jnp.power(theta_base, -(jnp.arange(HEAD // 2, dtype=F32) * 2.0) / HEAD)
    angle = local.astype(F32)[:, None] * freq
    cos = jnp.cos(angle)
    sin = jnp.sin(angle)
    cos = jnp.concatenate([cos, cos], axis=1)
    sin = jnp.concatenate([-sin, sin], axis=1)

    inputs_low = both(layer_input)
    d_out = both(cotangent)
    inputs = inputs_low.astype(F32)
    factor_a = lax.rsqrt(jnp.mean(inputs * inputs, axis=-1, keepdims=True) + epsilon)
    normed_a = (inputs * factor_a * attn_norm).astype(BF)
    logits = dot_nt(normed_a, gate_core)
    proj = dot_nt(normed_a, qkv_full)
    q_gain = q_norm[None, :]
    k_gain = k_norm[None, :]

    packed, results, logs, gated, partial = [], [], [], [], []
    for row in range(rows):
        packed.append(exchange(pack_heads(proj, cos, sin, q_gain, k_gain, row, chips, chip_tok)))
    for row in range(rows):
        head_out, log = attend(packed[row], start[row : row + 1], low[row])
        results.append(head_out)
        logs.append(log)
    tok_results = [exchange(r) for r in results]
    for row in range(rows):
        gated.append(gate_rows(tok_results[row], logits, row))
        partial.append(pair_sum(dot_nt(gated[row], out_full, BF)))
    mid = inputs + jnp.concatenate(partial, axis=0)
    gated = jnp.concatenate(gated, axis=0)

    factor_f = lax.rsqrt(jnp.mean(mid * mid, axis=-1, keepdims=True) + epsilon)
    normed_f = (mid * factor_f * ffn_norm).astype(BF)
    gate_up = dot_nt(normed_f, gu_full, BF)
    gate_part = gate_up[:, : FF // CORES].astype(F32)
    up_part = gate_up[:, FF // CORES :].astype(F32)
    gate_act = jax.nn.sigmoid(gate_part)
    silu = gate_part * gate_act
    hidden = (silu * up_part).astype(BF)
    shard_down = scatter(dot_tn(d_out, hidden, BF))
    d_hidden = dot_nn(d_out, down_full)
    d_gate = d_hidden * up_part * gate_act * (1.0 + gate_part * (1.0 - gate_act))
    d_up = d_hidden * silu
    d_gate_up = jnp.concatenate([d_gate.astype(BF), d_up.astype(BF)], axis=1)
    d_normed = pair_sum(dot_nn(d_gate_up, gu_full, BF))
    half_cols = width // 2
    shard_gu = [scatter(dot_tn(d_gate_up, normed_f[:, a : a + half_cols], BF)) for a in (0, half_cols)]
    out_part = dot_nt(hidden, down_full, BF).reshape(rows, CORES, tok, width)
    out_other = swap(pick(out_part[:, 1], out_part[:, 0]))
    output = (own(mid) + pick(out_part[:, 0], out_part[:, 1]).astype(F32) + out_other.astype(F32)).astype(BF)

    part_ffn = 0.5 * jnp.sum(d_normed * mid * factor_f, axis=0)
    weighted = d_normed * ffn_norm
    inner = jnp.mean(weighted * mid, axis=-1, keepdims=True)
    d_mid = d_out.astype(F32) + factor_f * weighted - mid * factor_f**3 * inner
    d_mid_low = d_mid.astype(BF)
    shard_out = scatter(dot_tn(d_mid_low, gated, BF))

    d_proj, d_logit, d_heads = [], [], []
    q_sum = 0.0
    k_sum = 0.0
    for row in range(rows):
        d_gated = dot_nn(d_mid_low[row * chip_tok : (row + 1) * chip_tok], out_full)
        d_attn, dl = gate_back(d_gated, tok_results[row], logits, row)
        d_logit.append(dl)
        d_heads.append(exchange(d_attn))
    for row in range(rows):
        grads = exchange(
            attend_back(packed[row], d_heads[row], results[row], logs[row], start[row : row + 1], low[row])
        )
        dpr, qs, ks = unpack_heads(grads, proj, cos, sin, q_gain, k_gain, row, chips, chip_tok)
        d_proj.append(dpr)
        q_sum = q_sum + qs
        k_sum = k_sum + ks
    d_proj = jnp.concatenate(d_proj, axis=0)
    d_logit = jnp.concatenate(d_logit, axis=0)
    shard_qkv = scatter(dot_tn(d_proj, normed_a, BF))
    d_norm_part = (dot_nn(d_proj, qkv_full) + dot_nn(d_logit, gate_core)).astype(BF)
    d_norm_part = d_norm_part.reshape(rows, CORES, tok, width)
    d_norm_other = swap(pick(d_norm_part[:, 1], d_norm_part[:, 0]))
    d_normed_a = pick(d_norm_part[:, 0], d_norm_part[:, 1]).astype(F32) + d_norm_other.astype(F32)
    own_in = layer_input.astype(F32)
    own_factor = lax.rsqrt(jnp.mean(own_in * own_in, axis=-1, keepdims=True) + epsilon)
    part_attn = jnp.sum(d_normed_a * own_in * own_factor, axis=(0, 1))
    weighted_a = d_normed_a * attn_norm
    inner_a = jnp.mean(weighted_a * own_in, axis=-1, keepdims=True)
    grad_input = (own(d_mid) + own_factor * weighted_a - own_in * own_factor**3 * inner_a).astype(BF)

    part_gate = dot_tn(d_logit, normed_a)[:CORE_Q]
    zero = jnp.zeros_like(part_gate)
    part_gate = join_rows(pick(part_gate, zero), pick(zero, part_gate), GROUP)
    heads = jnp.concatenate([jnp.sum(q_sum, axis=0), jnp.sum(k_sum, axis=0)])
    heads = jnp.pad(heads, (0, width - heads.shape[0]))
    early = total_sum(jnp.concatenate([part_gate, part_ffn[None], jnp.zeros((7, width), F32)], axis=0))
    late = total_sum(jnp.stack([part_attn, heads]))
    gate_count = w_gate.shape[0]
    grad_w_gate = lax.dynamic_slice_in_dim(early, lax.axis_index("dp") * gate_count, gate_count, 0)

    def halves(shard):
        mine = chip_sum(shard)
        other = swap(mine)
        return pick(mine, other).astype(F32), pick(other, mine).astype(F32)

    grad_down = join_cols(*halves(shard_down), ff_unit)
    gu_low, gu_high = zip(*[halves(s) for s in shard_gu])
    grad_gu = jnp.concatenate([jnp.concatenate(gu_low, axis=1), jnp.concatenate(gu_high, axis=1)], axis=0)
    grad_out = join_cols(*halves(shard_out), GROUP * HEAD)
    qkv_low, qkv_high = halves(shard_qkv)
    grad_qkv = jnp.where(
        q_shard, join_rows(qkv_low, qkv_high, GROUP * HEAD), join_rows(qkv_low, qkv_high, HEAD)
    )
    return (
        output,
        grad_input,
        late[0],
        late[1, :HEAD],
        late[1, HEAD : 2 * HEAD],
        early[QUERY_HEADS],
        grad_qkv,
        grad_w_gate,
        grad_out,
        grad_gu,
        grad_down,
    )


def solution(mesh):
    token = P("dp", "seq", None)
    shard = P("dp", None)
    in_specs = (token, shard, P(), P(), P(), P(), shard, shard, shard, shard, shard, token)
    out_specs = (token, token, P(), P(), P(), P(), shard, shard, shard, shard, shard)
    return jax.shard_map(shards, mesh=mesh, in_specs=in_specs, out_specs=out_specs, check_vma=False)
```

```python
import functools
import math

import jax
import jax.numpy as jnp
from jax import lax
from jax.experimental import pallas as pl
from jax.experimental.pallas import tpu as pltpu
from jax.sharding import PartitionSpec as P

QUERY_HEADS = 16
KEY_VALUE_HEADS = 8
HEAD = 128
FF = 6144
CORES = 2

GROUP = QUERY_HEADS // KEY_VALUE_HEADS
CORE_Q = QUERY_HEADS // CORES
CORE_KV = KEY_VALUE_HEADS // CORES
epsilon = 1e-06
theta_base = 1000000.0
SCALE = 1.0 / math.sqrt(HEAD)
SCALE2 = SCALE * math.log2(math.e)
BF = jnp.bfloat16
F32 = jnp.float32


def dot_nt(left, right, out=F32):
    return lax.dot_general(left, right, (((1,), (1,)), ((), ())), preferred_element_type=F32).astype(out)


def dot_nn(left, right, out=F32):
    return lax.dot_general(left, right, (((1,), (0,)), ((), ())), preferred_element_type=F32).astype(out)


def dot_tn(left, right, out=F32):
    return lax.dot_general(left, right, (((0,), (0,)), ((), ())), preferred_element_type=F32).astype(out)


def doc_positions(lengths, total):
    ends = jnp.cumsum(lengths, axis=-1)
    starts = ends - lengths
    places = jnp.arange(total, dtype=jnp.int32)
    segment = jnp.sum((places[:, None] >= ends[..., None, :]).astype(jnp.int32), axis=-1)
    owners = segment[..., None] == jnp.arange(lengths.shape[-1], dtype=jnp.int32)
    first = jnp.sum(jnp.where(owners, starts[..., None, :], 0), axis=-1)
    return first, places - first


def pack_kernel(chips, proj_ref, cos_ref, sin_ref, qg_ref, kg_ref, out_ref):
    per = CORE_Q // chips
    copies = max(1, chips // CORE_KV)
    cos = cos_ref[...]
    sin = sin_ref[...]

    def head(index, gain):
        u = proj_ref[:, index * HEAD : (index + 1) * HEAD]
        factor = lax.rsqrt(jnp.mean(u * u, axis=-1, keepdims=True) + epsilon)
        n = u * factor * gain
        return (n * cos + pltpu.roll(n, HEAD // 2, 1) * sin).astype(BF)

    for z in range(chips):
        for h in range(per):
            out_ref[z, :, h * HEAD : (h + 1) * HEAD] = head(z * per + h, qg_ref[...])
        if z % copies == 0:
            kv = z // copies
            key = head(CORE_Q + kv, kg_ref[...])
            base = (CORE_Q + CORE_KV + kv) * HEAD
            value = proj_ref[:, base : base + HEAD].astype(BF)
        out_ref[z, :, per * HEAD : (per + 1) * HEAD] = key
        out_ref[z, :, (per + 1) * HEAD : (per + 2) * HEAD] = value


def pack_heads(proj, cos, sin, q_gain, k_gain, row, chips, chip_tok):
    per = CORE_Q // chips
    lanes = (per + 2) * HEAD
    block = min(256, chip_tok)
    steps = chip_tok // block
    width = proj.shape[1]
    tok = lambda i: (row * steps + i, 0)
    return pl.pallas_call(
        functools.partial(pack_kernel, chips),
        grid=(steps,),
        in_specs=[
            pl.BlockSpec((block, width), tok),
            pl.BlockSpec((block, HEAD), tok),
            pl.BlockSpec((block, HEAD), tok),
            pl.BlockSpec((1, HEAD), lambda i: (0, 0)),
            pl.BlockSpec((1, HEAD), lambda i: (0, 0)),
        ],
        out_specs=pl.BlockSpec((chips, block, lanes), lambda i: (0, i, 0)),
        out_shape=jax.ShapeDtypeStruct((chips, chip_tok, lanes), BF),
        name="pack_heads",
    )(proj, cos, sin, q_gain, k_gain)


def unpack_kernel(chips, grad_ref, proj_ref, cos_ref, sin_ref, qg_ref, kg_ref, out_ref, qs_ref, ks_ref):
    per = CORE_Q // chips
    copies = max(1, chips // CORE_KV)
    cos = cos_ref[...]
    sin = sin_ref[...]

    @pl.when(pl.program_id(0) == 0)
    def _():
        qs_ref[...] = jnp.zeros_like(qs_ref)
        ks_ref[...] = jnp.zeros_like(ks_ref)

    def head(e, index, gain, sum_ref):
        e = e * cos + pltpu.roll(e * sin, HEAD // 2, 1)
        u = proj_ref[:, index * HEAD : (index + 1) * HEAD]
        factor = lax.rsqrt(jnp.mean(u * u, axis=-1, keepdims=True) + epsilon)
        n = u * factor
        sum_ref[...] += jnp.sum((e * n).reshape(-1, 8, HEAD), axis=0)
        weighted = e * gain
        inner = jnp.mean(weighted * n, axis=-1, keepdims=True)
        out_ref[:, index * HEAD : (index + 1) * HEAD] = (factor * (weighted - n * inner)).astype(BF)

    def part(z, lane):
        return grad_ref[z, :, lane * HEAD : (lane + 1) * HEAD].astype(F32)

    for z in range(chips):
        for h in range(per):
            head(part(z, h), z * per + h, qg_ref[...], qs_ref)
    for kv in range(CORE_KV):
        spread = range(kv * copies, (kv + 1) * copies)
        head(sum(part(z, per) for z in spread), CORE_Q + kv, kg_ref[...], ks_ref)
        base = (CORE_Q + CORE_KV + kv) * HEAD
        out_ref[:, base : base + HEAD] = sum(part(z, per + 1) for z in spread).astype(BF)


def unpack_heads(grads, proj, cos, sin, q_gain, k_gain, row, chips, chip_tok):
    lanes = grads.shape[2]
    block = min(256, chip_tok)
    steps = chip_tok // block
    width = proj.shape[1]
    tok = lambda i: (row * steps + i, 0)
    small = pl.BlockSpec((8, HEAD), lambda i: (0, 0))
    return pl.pallas_call(
        functools.partial(unpack_kernel, chips),
        grid=(steps,),
        in_specs=[
            pl.BlockSpec((chips, block, lanes), lambda i: (0, i, 0)),
            pl.BlockSpec((block, width), tok),
            pl.BlockSpec((block, HEAD), tok),
            pl.BlockSpec((block, HEAD), tok),
            pl.BlockSpec((1, HEAD), lambda i: (0, 0)),
            pl.BlockSpec((1, HEAD), lambda i: (0, 0)),
        ],
        out_specs=[pl.BlockSpec((block, width), lambda i: (i, 0)), small, small],
        out_shape=[
            jax.ShapeDtypeStruct((chip_tok, width), BF),
            jax.ShapeDtypeStruct((8, HEAD), F32),
            jax.ShapeDtypeStruct((8, HEAD), F32),
        ],
        name="unpack_heads",
    )(grads, proj, cos, sin, q_gain, k_gain)


def visible(j, size, start, diagonal):
    inner = lax.broadcasted_iota(jnp.int32, (size, size), 0)
    allowed = inner >= start - j * size
    if diagonal:
        allowed = allowed & (inner <= lax.broadcasted_iota(jnp.int32, (size, size), 1))
    return allowed


def attend_kernel(per, low_ref, q_ref, k_ref, v_ref, start_ref, out_ref, log_ref, acc_ref, sum_ref):
    i = pl.program_id(0)
    size = q_ref.shape[1]
    start = start_ref[...]
    acc_ref[...] = jnp.zeros_like(acc_ref)
    sum_ref[...] = jnp.zeros_like(sum_ref)

    def one(j, diagonal):
        key = k_ref[j]
        value = v_ref[j]
        allowed = visible(j, size, start, diagonal)
        for h in range(per):
            scores = dot_nt(key, q_ref[0, :, h * HEAD : (h + 1) * HEAD])
            p = jnp.where(allowed, jnp.exp2(scores * SCALE2), 0.0)
            sum_ref[h : h + 1, :] += jnp.sum(p, axis=0, keepdims=True)
            acc_ref[h] += dot_tn(value, p.astype(BF))

    def step(j, carry):
        one(j, False)
        return carry

    lax.fori_loop(low_ref[i], i, step, 0)
    one(i, True)
    for h in range(per):
        total = sum_ref[h : h + 1, :]
        out_ref[0, :, h * HEAD : (h + 1) * HEAD] = (acc_ref[h] / total).T.astype(BF)
        log_ref[h : h + 1, :] = jnp.log2(total)


def attend(packed, start, low):
    chips, size, lanes = packed.shape
    per = lanes // HEAD - 2
    return pl.pallas_call(
        functools.partial(attend_kernel, per),
        grid_spec=pltpu.PrefetchScalarGridSpec(
            num_scalar_prefetch=1,
            grid=(chips,),
            in_specs=[
                pl.BlockSpec((1, size, per * HEAD), lambda i, low: (i, 0, 0)),
                pl.BlockSpec((chips, size, HEAD), lambda i, low: (0, 0, per)),
                pl.BlockSpec((chips, size, HEAD), lambda i, low: (0, 0, per + 1)),
                pl.BlockSpec((1, size), lambda i, low: (0, i)),
            ],
            out_specs=[
                pl.BlockSpec((1, size, per * HEAD), lambda i, low: (i, 0, 0)),
                pl.BlockSpec((per, size), lambda i, low: (0, i)),
            ],
            scratch_shapes=[pltpu.VMEM((per, HEAD, size), F32), pltpu.VMEM((per, size), F32)],
        ),
        out_shape=[
            jax.ShapeDtypeStruct((chips, size, per * HEAD), BF),
            jax.ShapeDtypeStruct((per, chips * size), F32),
        ],
        name="attend",
    )(low, packed, packed, packed, start)


def attend_back_kernel(
    per, low_ref, q_ref, k_ref, v_ref, grad_ref, res_ref, log_ref, start_ref, out_ref, dq_ref, dk_ref, dv_ref
):
    i = pl.program_id(0)
    size = q_ref.shape[1]
    start = start_ref[...]

    @pl.when(i == 0)
    def _():
        dk_ref[...] = jnp.zeros_like(dk_ref)
        dv_ref[...] = jnp.zeros_like(dv_ref)

    dq_ref[...] = jnp.zeros_like(dq_ref)
    ones = jnp.ones((8, HEAD), F32)
    inner = []
    for h in range(per):
        cols = slice(h * HEAD, (h + 1) * HEAD)
        both = grad_ref[0, :, cols].astype(F32) * res_ref[0, :, cols].astype(F32)
        sums = lax.dot_general(
            ones, both, (((1,), (1,)), ((), ())), precision=lax.Precision.HIGHEST, preferred_element_type=F32
        )
        inner.append(sums[0:1, :])

    def one(j, diagonal):
        key = k_ref[j]
        value = v_ref[j]
        allowed = visible(j, size, start, diagonal)
        for h in range(per):
            query = q_ref[0, :, h * HEAD : (h + 1) * HEAD]
            grad = grad_ref[0, :, h * HEAD : (h + 1) * HEAD]
            scores = dot_nt(key, query)
            p = jnp.where(allowed, jnp.exp2(scores * SCALE2 - log_ref[h : h + 1, :]), 0.0)
            dp = dot_nt(value, grad)
            ds = (p * (dp - inner[h])).astype(BF)
            dv_ref[j] += dot_nn(p.astype(BF), grad)
            dk_ref[j] += dot_nn(ds, query)
            dq_ref[h] += dot_tn(ds, key)

    def step(j, carry):
        one(j, False)
        return carry

    lax.fori_loop(low_ref[i], i, step, 0)
    one(i, True)
    for h in range(per):
        out_ref[i, :, h * HEAD : (h + 1) * HEAD] = (dq_ref[h] * SCALE).astype(BF)

    @pl.when(i == pl.num_programs(0) - 1)
    def _():
        out_ref[:, :, per * HEAD : (per + 1) * HEAD] = (dk_ref[...] * SCALE).astype(BF)
        out_ref[:, :, (per + 1) * HEAD : (per + 2) * HEAD] = dv_ref[...].astype(BF)


def attend_back(packed, grad, result, logs, start, low):
    chips, size, lanes = packed.shape
    per = lanes // HEAD - 2
    one = pl.BlockSpec((1, size, per * HEAD), lambda i, low: (i, 0, 0))
    return pl.pallas_call(
        functools.partial(attend_back_kernel, per),
        grid_spec=pltpu.PrefetchScalarGridSpec(
            num_scalar_prefetch=1,
            grid=(chips,),
            in_specs=[
                one,
                pl.BlockSpec((chips, size, HEAD), lambda i, low: (0, 0, per)),
                pl.BlockSpec((chips, size, HEAD), lambda i, low: (0, 0, per + 1)),
                one,
                one,
                pl.BlockSpec((per, size), lambda i, low: (0, i)),
                pl.BlockSpec((1, size), lambda i, low: (0, i)),
            ],
            out_specs=pl.BlockSpec((chips, size, lanes), lambda i, low: (0, 0, 0)),
            scratch_shapes=[
                pltpu.VMEM((per, size, HEAD), F32),
                pltpu.VMEM((chips, size, HEAD), F32),
                pltpu.VMEM((chips, size, HEAD), F32),
            ],
        ),
        out_shape=jax.ShapeDtypeStruct((chips, size, lanes), BF),
        name="attend_back",
    )(low, packed, packed, packed, grad, result, logs, start)


def gate_kernel(res_ref, logit_ref, out_ref):
    chips, _, lanes = res_ref.shape
    per = lanes // HEAD
    sig = jax.nn.sigmoid(logit_ref[...])
    for z in range(chips):
        for h in range(per):
            head = z * per + h
            value = res_ref[z, :, h * HEAD : (h + 1) * HEAD].astype(F32)
            out_ref[:, head * HEAD : (head + 1) * HEAD] = (value * sig[:, head : head + 1]).astype(BF)


def gate_rows(result, logits, row):
    chips, size, lanes = result.shape
    block = min(256, size)
    steps = size // block
    return pl.pallas_call(
        gate_kernel,
        grid=(steps,),
        in_specs=[
            pl.BlockSpec((chips, block, lanes), lambda i: (0, i, 0)),
            pl.BlockSpec((block, HEAD), lambda i: (row * steps + i, 0)),
        ],
        out_specs=pl.BlockSpec((block, chips * lanes), lambda i: (i, 0)),
        out_shape=jax.ShapeDtypeStruct((size, chips * lanes), BF),
        name="gate_rows",
    )(result, logits)


def gate_back_kernel(grad_ref, res_ref, logit_ref, out_ref, dlogit_ref):
    chips, size, lanes = res_ref.shape
    per = lanes // HEAD
    sig = jax.nn.sigmoid(logit_ref[...])
    lane = lax.broadcasted_iota(jnp.int32, sig.shape, 1)
    sums = jnp.zeros(sig.shape, F32)
    for z in range(chips):
        for h in range(per):
            head = z * per + h
            e = grad_ref[:, head * HEAD : (head + 1) * HEAD]
            value = res_ref[z, :, h * HEAD : (h + 1) * HEAD].astype(F32)
            out_ref[z, :, h * HEAD : (h + 1) * HEAD] = (e * sig[:, head : head + 1]).astype(BF)
            sums = jnp.where(lane == head, jnp.sum(e * value, axis=-1, keepdims=True), sums)
    dlogit_ref[...] = (sums * sig * (1.0 - sig)).astype(BF)


def gate_back(grad, result, logits, row):
    chips, size, lanes = result.shape
    block = min(256, size)
    steps = size // block
    return pl.pallas_call(
        gate_back_kernel,
        grid=(steps,),
        in_specs=[
            pl.BlockSpec((block, chips * lanes), lambda i: (i, 0)),
            pl.BlockSpec((chips, block, lanes), lambda i: (0, i, 0)),
            pl.BlockSpec((block, HEAD), lambda i: (row * steps + i, 0)),
        ],
        out_specs=[
            pl.BlockSpec((chips, block, lanes), lambda i: (0, i, 0)),
            pl.BlockSpec((block, HEAD), lambda i: (i, 0)),
        ],
        out_shape=[jax.ShapeDtypeStruct((chips, size, lanes), BF), jax.ShapeDtypeStruct((size, HEAD), BF)],
        name="gate_back",
    )(grad, result, logits)


def join_rows_kernel(count, which_ref, *refs):
    out_ref = refs[2 * count]
    size = refs[0].shape[1]
    own_half = pl.program_id(0) == which_ref[0]

    def put(parts):
        for k in range(count):
            out_ref[:, k * size : (k + 1) * size] = parts[k][...].astype(F32)

    pl.when(own_half)(lambda: put(refs[:count]))
    pl.when(jnp.logical_not(own_half))(lambda: put(refs[count : 2 * count]))


def join_rows(mine, other, core, unit, block):
    count = len(mine)
    height, size = mine[0].shape
    steps = height // block
    blocks = unit // block

    def source(side):
        def index(h, i, which):
            active = (h == which[0]) if side == 0 else (h != which[0])
            return (jnp.where(active, i, jnp.where(h == 0, 0, steps - 1)), 0)

        return pl.BlockSpec((block, size), index)

    def target(h, i, which):
        per = which[1]
        return ((i // per) * 2 * per + h * per + i % per, 0)

    return pl.pallas_call(
        functools.partial(join_rows_kernel, count),
        grid_spec=pltpu.PrefetchScalarGridSpec(
            num_scalar_prefetch=1,
            grid=(CORES, steps),
            in_specs=[source(0)] * count + [source(1)] * count,
            out_specs=pl.BlockSpec((block, count * size), target),
        ),
        out_shape=jax.ShapeDtypeStruct((CORES * height, count * size), F32),
        name="join_rows",
    )(jnp.stack([core, jnp.asarray(blocks, jnp.int32)]), *mine, *other)


def join_cols_kernel(count, per, which_ref, *refs):
    out_ref = refs[2 * count]
    u = pl.program_id(0)
    own_half = pl.program_id(1) == which_ref[0]

    def put(ref):
        out_ref[...] = ref[...].astype(F32)

    for k in range(count):
        here = u // per == k
        pl.when(here & own_half)(functools.partial(put, refs[k]))
        pl.when(here & jnp.logical_not(own_half))(functools.partial(put, refs[count + k]))


def join_cols(mine, other, core, unit):
    count = len(mine)
    height, size = mine[0].shape
    per = size // unit

    def source(k):
        return pl.BlockSpec((height, unit), lambda u, h, which: (0, jnp.clip(u - k * per, 0, per - 1)))

    sources = [source(k) for k in range(count)]
    return pl.pallas_call(
        functools.partial(join_cols_kernel, count, per),
        grid_spec=pltpu.PrefetchScalarGridSpec(
            num_scalar_prefetch=1,
            grid=(count * per, CORES),
            in_specs=sources + sources,
            out_specs=pl.BlockSpec((height, unit), lambda u, h, which: (0, u * CORES + h)),
        ),
        out_shape=jax.ShapeDtypeStruct((height, CORES * count * size), F32),
        name="join_cols",
    )(core[None], *mine, *other)


def tie(value, work):
    return lax.optimization_barrier((value, work))


def shards(
    layer_input,
    doc_lengths,
    attn_norm,
    q_norm,
    k_norm,
    ffn_norm,
    w_qkv,
    w_gate,
    w_out,
    w_gu,
    w_down,
    cotangent,
):
    rows, tok, width = layer_input.shape
    seq = lax.axis_size("seq")
    dp = lax.axis_size("dp")
    chips = seq // CORES
    place = lax.axis_index("seq")
    core = place % CORES
    chip = place // CORES
    first = core == 0
    chip_tok = tok * CORES
    length = tok * seq
    tokens = rows * chip_tok
    pair = [(s, s ^ 1) for s in range(seq)]
    groups = [[z * CORES + c for z in range(chips)] for c in range(CORES)]
    q_shard = lax.axis_index("dp") * w_qkv.shape[0] < QUERY_HEADS * HEAD

    def swap(x):
        return lax.ppermute(x, "seq", pair)

    def pick(a, b):
        return jnp.where(first, a, b)

    def both(x):
        other = swap(x)
        return jnp.concatenate([pick(x, other), pick(other, x)], axis=1).reshape(tokens, width)

    def own(x):
        x = x.reshape(rows, CORES, tok, width)
        return pick(x[:, 0], x[:, 1])

    def pair_sum(x):
        return x.astype(F32) + swap(x).astype(F32)

    def exchange(x):
        return lax.all_to_all(x, "seq", 0, 0, axis_index_groups=groups, tiled=True)

    def chip_sum(x):
        if chips != 4:
            return lax.psum(x, "seq", axis_index_groups=groups)
        inward = [(c, 2 + c) for c in range(CORES)] + [(6 + c, 4 + c) for c in range(CORES)]
        middle = [(2 + c, 4 + c) for c in range(CORES)] + [(4 + c, 2 + c) for c in range(CORES)]
        outward = [(2 + c, c) for c in range(CORES)] + [(4 + c, 6 + c) for c in range(CORES)]
        half = x + lax.ppermute(x, "seq", inward)
        full = half + lax.ppermute(half, "seq", middle)
        spread = lax.ppermute(full, "seq", outward)
        return jnp.where((chip == 1) | (chip == 2), full, spread)

    def total_sum(x, names=("seq", "dp")):
        for name in names:
            size = lax.axis_size(name)
            step = 1
            while step < size:
                x = x + lax.ppermute(x, name, [(s, s ^ step) for s in range(size)])
                step *= 2
        return x

    def scatter(x):
        return lax.psum_scatter(x, "dp", scatter_dimension=0, tiled=True)

    def gather(x):
        return lax.all_gather(x, "dp", axis=0, tiled=True)

    def core_rows(w, unit):
        return jnp.concatenate(
            [pick(w[a : a + unit], w[a + unit : a + 2 * unit]) for a in range(0, w.shape[0], 2 * unit)], axis=0
        )

    def core_cols(w, unit):
        return jnp.concatenate(
            [pick(w[:, a : a + unit], w[:, a + unit : a + 2 * unit]) for a in range(0, w.shape[1], 2 * unit)],
            axis=1,
        )

    ff_unit = w_gu.shape[0] // CORES
    qkv_half = jnp.where(q_shard, core_rows(w_qkv, GROUP * HEAD), core_rows(w_qkv, HEAD))
    qkv_full = gather(qkv_half)
    gate_count = w_gate.shape[0]
    gate_full = lax.dynamic_update_slice_in_dim(
        jnp.zeros((QUERY_HEADS, width), BF), w_gate, lax.axis_index("dp") * gate_count, 0
    )
    gate_full = total_sum(gate_full, ("dp",))
    out_full = gather(core_cols(w_out, GROUP * HEAD))
    gu_full = gather(core_rows(w_gu, ff_unit))
    down_full = gather(core_cols(w_down, ff_unit))
    gate_core = jnp.pad(core_rows(gate_full, GROUP), ((0, HEAD - CORE_Q), (0, 0)))

    start, position = doc_positions(doc_lengths, length)
    low = start.reshape(rows, chips, chip_tok)[:, :, 0] // chip_tok
    local = lax.dynamic_slice_in_dim(position, chip * chip_tok, chip_tok, 1).reshape(tokens)
    freq = jnp.power(theta_base, -(jnp.arange(HEAD // 2, dtype=F32) * 2.0) / HEAD)
    angle = local.astype(F32)[:, None] * freq
    cos = jnp.cos(angle)
    sin = jnp.sin(angle)
    cos = jnp.concatenate([cos, cos], axis=1)
    sin = jnp.concatenate([-sin, sin], axis=1)

    inputs_low = both(layer_input)
    d_out = both(cotangent)
    inputs = inputs_low.astype(F32)
    factor_a = lax.rsqrt(jnp.mean(inputs * inputs, axis=-1, keepdims=True) + epsilon)
    normed_a = (inputs * factor_a * attn_norm).astype(BF)
    logits = dot_nt(normed_a, gate_core)
    proj = dot_nt(normed_a, qkv_full)
    q_gain = q_norm[None, :]
    k_gain = k_norm[None, :]

    packed, results, logs, gated, partial = [], [], [], [], []
    for row in range(rows):
        packed.append(exchange(pack_heads(proj, cos, sin, q_gain, k_gain, row, chips, chip_tok)))
    packed[0], logits = tie(packed[0], logits)
    for row in range(rows):
        head_out, log = attend(packed[row], start[row : row + 1], low[row])
        results.append(head_out)
        logs.append(log)
    tok_results = [exchange(r) for r in results]
    for row in range(rows):
        gated.append(gate_rows(tok_results[row], logits, row))
        partial.append(pair_sum(dot_nt(gated[row], out_full, BF)))
    mid = inputs + jnp.concatenate(partial, axis=0)
    gated = jnp.concatenate(gated, axis=0)

    factor_f = lax.rsqrt(jnp.mean(mid * mid, axis=-1, keepdims=True) + epsilon)
    normed_f = (mid * factor_f * ffn_norm).astype(BF)
    gate_up = dot_nt(normed_f, gu_full, BF)
    gate_part = gate_up[:, : FF // CORES].astype(F32)
    up_part = gate_up[:, FF // CORES :].astype(F32)
    gate_act = jax.nn.sigmoid(gate_part)
    silu = gate_part * gate_act
    hidden = (silu * up_part).astype(BF)
    part_down = [dot_tn(d_out, hidden[:, a : a + ff_unit], BF) for a in range(0, FF // CORES, ff_unit)]
    down_full, part_down = tie(down_full, part_down)
    shard_down = [scatter(p) for p in part_down]
    d_hidden = dot_nn(d_out, down_full)
    d_gate = d_hidden * up_part * gate_act * (1.0 + gate_part * (1.0 - gate_act))
    d_up = d_hidden * silu
    d_gate_up = jnp.concatenate([d_gate.astype(BF), d_up.astype(BF)], axis=1)
    d_norm_mine = dot_nn(d_gate_up, gu_full, BF)
    d_norm_pair = swap(d_norm_mine)
    piece = width // 4
    part_gu = [dot_tn(d_gate_up, normed_f[:, a : a + piece], BF) for a in range(0, width, piece)]
    d_norm_pair, part_gu[:2] = tie(d_norm_pair, part_gu[:2])
    d_normed = d_norm_mine.astype(F32) + d_norm_pair.astype(F32)
    out_part = dot_nt(hidden, down_full, BF)

    part_ffn = 0.5 * jnp.sum(d_normed * mid * factor_f, axis=0)
    weighted = d_normed * ffn_norm
    inner = jnp.mean(weighted * mid, axis=-1, keepdims=True)
    d_mid = d_out.astype(F32) + factor_f * weighted - mid * factor_f**3 * inner
    d_mid_low = d_mid.astype(BF)
    part_out = dot_tn(d_mid_low, gated, BF)

    d_proj, d_logit, d_heads = [], [], []
    q_sum = 0.0
    k_sum = 0.0
    for row in range(rows):
        d_gated = dot_nn(d_mid_low[row * chip_tok : (row + 1) * chip_tok], out_full)
        d_attn, dl = gate_back(d_gated, tok_results[row], logits, row)
        d_logit.append(dl)
        d_heads.append(exchange(d_attn))
    d_heads[0], part_gu[2:] = tie(d_heads[0], part_gu[2:])
    d_heads[-1], part_out = tie(d_heads[-1], part_out)
    shard_gu = [scatter(p) for p in part_gu]
    shard_out = [scatter(part_out)]
    back = []
    for row in range(rows):
        back.append(
            exchange(attend_back(packed[row], d_heads[row], results[row], logs[row], start[row : row + 1], low[row]))
        )
    back[0], out_part = tie(back[0], out_part)
    out_part = out_part.reshape(rows, CORES, tok, width)
    out_other = swap(pick(out_part[:, 1], out_part[:, 0]))
    output = (own(mid) + pick(out_part[:, 0], out_part[:, 1]).astype(F32) + out_other.astype(F32)).astype(BF)
    for row in range(rows):
        dpr, qs, ks = unpack_heads(back[row], proj, cos, sin, q_gain, k_gain, row, chips, chip_tok)
        d_proj.append(dpr)
        q_sum = q_sum + qs
        k_sum = k_sum + ks
    d_proj = jnp.concatenate(d_proj, axis=0)
    d_logit = jnp.concatenate(d_logit, axis=0)
    half = width // 2
    shard_qkv = [scatter(dot_tn(d_proj, normed_a[:, a : a + half], BF)) for a in (0, half)]
    d_norm_part = (dot_nn(d_proj, qkv_full) + dot_nn(d_logit, gate_core)).astype(BF)
    d_norm_part = d_norm_part.reshape(rows, CORES, tok, width)
    d_norm_other = swap(pick(d_norm_part[:, 1], d_norm_part[:, 0]))
    d_normed_a = pick(d_norm_part[:, 0], d_norm_part[:, 1]).astype(F32) + d_norm_other.astype(F32)
    own_in = layer_input.astype(F32)
    own_factor = lax.rsqrt(jnp.mean(own_in * own_in, axis=-1, keepdims=True) + epsilon)
    part_attn = jnp.sum(d_normed_a * own_in * own_factor, axis=(0, 1))
    weighted_a = d_normed_a * attn_norm
    inner_a = jnp.mean(weighted_a * own_in, axis=-1, keepdims=True)
    grad_input = (own(d_mid) + own_factor * weighted_a - own_in * own_factor**3 * inner_a).astype(BF)

    part_gate = dot_tn(d_logit, normed_a)[:CORE_Q]
    zero = jnp.zeros_like(part_gate)
    part_gate = jnp.stack([pick(part_gate, zero).reshape(-1, GROUP, width), pick(zero, part_gate).reshape(-1, GROUP, width)], 1)
    part_gate = part_gate.reshape(QUERY_HEADS, width)
    heads = jnp.concatenate([jnp.sum(q_sum, axis=0), jnp.sum(k_sum, axis=0)])
    heads = jnp.pad(heads, (0, width - heads.shape[0]))
    early = total_sum(jnp.concatenate([part_gate, part_ffn[None], jnp.zeros((7, width), F32)], axis=0))
    late = total_sum(jnp.stack([part_attn, heads]))
    grad_w_gate = lax.dynamic_slice_in_dim(early, lax.axis_index("dp") * gate_count, gate_count, 0)

    def halves(parts):
        mine = [chip_sum(p) for p in parts]
        return mine, [swap(p) for p in mine]

    grad_down = join_cols(*halves(shard_down), core, ff_unit)
    grad_gu = join_rows(*halves(shard_gu), core, ff_unit, 256)
    grad_out = join_cols(*halves(shard_out), core, GROUP * HEAD)
    grad_qkv = join_rows(*halves(shard_qkv), core, jnp.where(q_shard, GROUP * HEAD, HEAD), HEAD)
    return (
        output,
        grad_input,
        late[0],
        late[1, :HEAD],
        late[1, HEAD : 2 * HEAD],
        early[QUERY_HEADS],
        grad_qkv,
        grad_w_gate,
        grad_out,
        grad_gu,
        grad_down,
    )


def solution(mesh):
    token = P("dp", "seq", None)
    shard = P("dp", None)
    in_specs = (token, shard, P(), P(), P(), P(), shard, shard, shard, shard, shard, token)
    out_specs = (token, token, P(), P(), P(), P(), shard, shard, shard, shard, shard)
    return jax.shard_map(shards, mesh=mesh, in_specs=in_specs, out_specs=out_specs, check_vma=False)
```

```python
import functools
import math

import jax
import jax.numpy as jnp
from jax import lax
from jax.experimental import pallas as pl
from jax.experimental.pallas import tpu as pltpu
from jax.sharding import PartitionSpec as P

QUERY_HEADS = 16
KEY_VALUE_HEADS = 8
HEAD = 128
FF = 6144
CORES = 2

GROUP = QUERY_HEADS // KEY_VALUE_HEADS
CORE_Q = QUERY_HEADS // CORES
CORE_KV = KEY_VALUE_HEADS // CORES
epsilon = 1e-06
theta_base = 1000000.0
SCALE = 1.0 / math.sqrt(HEAD)
SCALE2 = SCALE * math.log2(math.e)
BF = jnp.bfloat16
F32 = jnp.float32


def dot_nt(left, right, out=F32):
    return lax.dot_general(left, right, (((1,), (1,)), ((), ())), preferred_element_type=F32).astype(out)


def dot_nn(left, right, out=F32):
    return lax.dot_general(left, right, (((1,), (0,)), ((), ())), preferred_element_type=F32).astype(out)


def dot_tn(left, right, out=F32):
    return lax.dot_general(left, right, (((0,), (0,)), ((), ())), preferred_element_type=F32).astype(out)


def doc_positions(lengths, total):
    ends = jnp.cumsum(lengths, axis=-1)
    starts = ends - lengths
    places = jnp.arange(total, dtype=jnp.int32)
    segment = jnp.sum((places[:, None] >= ends[..., None, :]).astype(jnp.int32), axis=-1)
    owners = segment[..., None] == jnp.arange(lengths.shape[-1], dtype=jnp.int32)
    first = jnp.sum(jnp.where(owners, starts[..., None, :], 0), axis=-1)
    return first, places - first


def pack_kernel(chips, proj_ref, cos_ref, sin_ref, qg_ref, kg_ref, out_ref):
    per = CORE_Q // chips
    copies = max(1, chips // CORE_KV)
    cos = cos_ref[...]
    sin = sin_ref[...]

    def head(index, gain):
        u = proj_ref[:, index * HEAD : (index + 1) * HEAD]
        factor = lax.rsqrt(jnp.mean(u * u, axis=-1, keepdims=True) + epsilon)
        n = u * factor * gain
        return (n * cos + pltpu.roll(n, HEAD // 2, 1) * sin).astype(BF)

    for z in range(chips):
        for h in range(per):
            out_ref[z, :, h * HEAD : (h + 1) * HEAD] = head(z * per + h, qg_ref[...])
        if z % copies == 0:
            kv = z // copies
            key = head(CORE_Q + kv, kg_ref[...])
            base = (CORE_Q + CORE_KV + kv) * HEAD
            value = proj_ref[:, base : base + HEAD].astype(BF)
        out_ref[z, :, per * HEAD : (per + 1) * HEAD] = key
        out_ref[z, :, (per + 1) * HEAD : (per + 2) * HEAD] = value


def pack_heads(proj, cos, sin, q_gain, k_gain, row, chips, chip_tok):
    per = CORE_Q // chips
    lanes = (per + 2) * HEAD
    block = min(256, chip_tok)
    steps = chip_tok // block
    width = proj.shape[1]
    tok = lambda i: (row * steps + i, 0)
    return pl.pallas_call(
        functools.partial(pack_kernel, chips),
        grid=(steps,),
        in_specs=[
            pl.BlockSpec((block, width), tok),
            pl.BlockSpec((block, HEAD), tok),
            pl.BlockSpec((block, HEAD), tok),
            pl.BlockSpec((1, HEAD), lambda i: (0, 0)),
            pl.BlockSpec((1, HEAD), lambda i: (0, 0)),
        ],
        out_specs=pl.BlockSpec((chips, block, lanes), lambda i: (0, i, 0)),
        out_shape=jax.ShapeDtypeStruct((chips, chip_tok, lanes), BF),
        name="pack_heads",
    )(proj, cos, sin, q_gain, k_gain)


def unpack_kernel(chips, grad_ref, proj_ref, cos_ref, sin_ref, qg_ref, kg_ref, out_ref, qs_ref, ks_ref):
    per = CORE_Q // chips
    copies = max(1, chips // CORE_KV)
    cos = cos_ref[...]
    sin = sin_ref[...]

    @pl.when(pl.program_id(0) == 0)
    def _():
        qs_ref[...] = jnp.zeros_like(qs_ref)
        ks_ref[...] = jnp.zeros_like(ks_ref)

    def head(e, index, gain, sum_ref):
        e = e * cos + pltpu.roll(e * sin, HEAD // 2, 1)
        u = proj_ref[:, index * HEAD : (index + 1) * HEAD]
        factor = lax.rsqrt(jnp.mean(u * u, axis=-1, keepdims=True) + epsilon)
        n = u * factor
        sum_ref[...] += jnp.sum((e * n).reshape(-1, 8, HEAD), axis=0)
        weighted = e * gain
        inner = jnp.mean(weighted * n, axis=-1, keepdims=True)
        out_ref[:, index * HEAD : (index + 1) * HEAD] = (factor * (weighted - n * inner)).astype(BF)

    def part(z, lane):
        return grad_ref[z, :, lane * HEAD : (lane + 1) * HEAD].astype(F32)

    for z in range(chips):
        for h in range(per):
            head(part(z, h), z * per + h, qg_ref[...], qs_ref)
    for kv in range(CORE_KV):
        spread = range(kv * copies, (kv + 1) * copies)
        head(sum(part(z, per) for z in spread), CORE_Q + kv, kg_ref[...], ks_ref)
        base = (CORE_Q + CORE_KV + kv) * HEAD
        out_ref[:, base : base + HEAD] = sum(part(z, per + 1) for z in spread).astype(BF)


def unpack_heads(grads, proj, cos, sin, q_gain, k_gain, row, chips, chip_tok):
    lanes = grads.shape[2]
    block = min(256, chip_tok)
    steps = chip_tok // block
    width = proj.shape[1]
    tok = lambda i: (row * steps + i, 0)
    small = pl.BlockSpec((8, HEAD), lambda i: (0, 0))
    return pl.pallas_call(
        functools.partial(unpack_kernel, chips),
        grid=(steps,),
        in_specs=[
            pl.BlockSpec((chips, block, lanes), lambda i: (0, i, 0)),
            pl.BlockSpec((block, width), tok),
            pl.BlockSpec((block, HEAD), tok),
            pl.BlockSpec((block, HEAD), tok),
            pl.BlockSpec((1, HEAD), lambda i: (0, 0)),
            pl.BlockSpec((1, HEAD), lambda i: (0, 0)),
        ],
        out_specs=[pl.BlockSpec((block, width), lambda i: (i, 0)), small, small],
        out_shape=[
            jax.ShapeDtypeStruct((chip_tok, width), BF),
            jax.ShapeDtypeStruct((8, HEAD), F32),
            jax.ShapeDtypeStruct((8, HEAD), F32),
        ],
        name="unpack_heads",
    )(grads, proj, cos, sin, q_gain, k_gain)


def visible(j, size, start, diagonal):
    inner = lax.broadcasted_iota(jnp.int32, (size, size), 0)
    allowed = inner >= start - j * size
    if diagonal:
        allowed = allowed & (inner <= lax.broadcasted_iota(jnp.int32, (size, size), 1))
    return allowed


def attend_kernel(per, low_ref, q_ref, k_ref, v_ref, start_ref, out_ref, log_ref, acc_ref, sum_ref):
    i = pl.program_id(0)
    size = q_ref.shape[1]
    start = start_ref[...]
    acc_ref[...] = jnp.zeros_like(acc_ref)
    sum_ref[...] = jnp.zeros_like(sum_ref)

    def one(j, diagonal):
        key = k_ref[j]
        value = v_ref[j]
        allowed = visible(j, size, start, diagonal)
        for h in range(per):
            scores = dot_nt(key, q_ref[0, :, h * HEAD : (h + 1) * HEAD])
            p = jnp.where(allowed, jnp.exp2(scores * SCALE2), 0.0)
            sum_ref[h : h + 1, :] += jnp.sum(p, axis=0, keepdims=True)
            acc_ref[h] += dot_tn(value, p.astype(BF))

    def step(j, carry):
        one(j, False)
        return carry

    lax.fori_loop(low_ref[i], i, step, 0)
    one(i, True)
    for h in range(per):
        total = sum_ref[h : h + 1, :]
        out_ref[0, :, h * HEAD : (h + 1) * HEAD] = (acc_ref[h] / total).T.astype(BF)
        log_ref[h : h + 1, :] = jnp.log2(total)


def attend(packed, start, low):
    chips, size, lanes = packed.shape
    per = lanes // HEAD - 2
    return pl.pallas_call(
        functools.partial(attend_kernel, per),
        grid_spec=pltpu.PrefetchScalarGridSpec(
            num_scalar_prefetch=1,
            grid=(chips,),
            in_specs=[
                pl.BlockSpec((1, size, per * HEAD), lambda i, low: (i, 0, 0)),
                pl.BlockSpec((chips, size, HEAD), lambda i, low: (0, 0, per)),
                pl.BlockSpec((chips, size, HEAD), lambda i, low: (0, 0, per + 1)),
                pl.BlockSpec((1, size), lambda i, low: (0, i)),
            ],
            out_specs=[
                pl.BlockSpec((1, size, per * HEAD), lambda i, low: (i, 0, 0)),
                pl.BlockSpec((per, size), lambda i, low: (0, i)),
            ],
            scratch_shapes=[pltpu.VMEM((per, HEAD, size), F32), pltpu.VMEM((per, size), F32)],
        ),
        out_shape=[
            jax.ShapeDtypeStruct((chips, size, per * HEAD), BF),
            jax.ShapeDtypeStruct((per, chips * size), F32),
        ],
        name="attend",
    )(low, packed, packed, packed, start)


def attend_back_kernel(
    per, low_ref, q_ref, k_ref, v_ref, grad_ref, res_ref, log_ref, start_ref, out_ref, dq_ref, dk_ref, dv_ref
):
    i = pl.program_id(0)
    size = q_ref.shape[1]
    start = start_ref[...]

    @pl.when(i == 0)
    def _():
        dk_ref[...] = jnp.zeros_like(dk_ref)
        dv_ref[...] = jnp.zeros_like(dv_ref)

    dq_ref[...] = jnp.zeros_like(dq_ref)
    ones = jnp.ones((8, HEAD), F32)
    inner = []
    for h in range(per):
        cols = slice(h * HEAD, (h + 1) * HEAD)
        both = grad_ref[0, :, cols].astype(F32) * res_ref[0, :, cols].astype(F32)
        sums = lax.dot_general(
            ones, both, (((1,), (1,)), ((), ())), precision=lax.Precision.HIGHEST, preferred_element_type=F32
        )
        inner.append(sums[0:1, :])

    def one(j, diagonal):
        key = k_ref[j]
        value = v_ref[j]
        allowed = visible(j, size, start, diagonal)
        for h in range(per):
            query = q_ref[0, :, h * HEAD : (h + 1) * HEAD]
            grad = grad_ref[0, :, h * HEAD : (h + 1) * HEAD]
            scores = dot_nt(key, query)
            p = jnp.where(allowed, jnp.exp2(scores * SCALE2 - log_ref[h : h + 1, :]), 0.0)
            dp = dot_nt(value, grad)
            ds = (p * (dp - inner[h])).astype(BF)
            dv_ref[j] += dot_nn(p.astype(BF), grad)
            dk_ref[j] += dot_nn(ds, query)
            dq_ref[h] += dot_tn(ds, key)

    def step(j, carry):
        one(j, False)
        return carry

    lax.fori_loop(low_ref[i], i, step, 0)
    one(i, True)
    for h in range(per):
        out_ref[i, :, h * HEAD : (h + 1) * HEAD] = (dq_ref[h] * SCALE).astype(BF)

    @pl.when(i == pl.num_programs(0) - 1)
    def _():
        out_ref[:, :, per * HEAD : (per + 1) * HEAD] = (dk_ref[...] * SCALE).astype(BF)
        out_ref[:, :, (per + 1) * HEAD : (per + 2) * HEAD] = dv_ref[...].astype(BF)


def attend_back(packed, grad, result, logs, start, low):
    chips, size, lanes = packed.shape
    per = lanes // HEAD - 2
    one = pl.BlockSpec((1, size, per * HEAD), lambda i, low: (i, 0, 0))
    return pl.pallas_call(
        functools.partial(attend_back_kernel, per),
        grid_spec=pltpu.PrefetchScalarGridSpec(
            num_scalar_prefetch=1,
            grid=(chips,),
            in_specs=[
                one,
                pl.BlockSpec((chips, size, HEAD), lambda i, low: (0, 0, per)),
                pl.BlockSpec((chips, size, HEAD), lambda i, low: (0, 0, per + 1)),
                one,
                one,
                pl.BlockSpec((per, size), lambda i, low: (0, i)),
                pl.BlockSpec((1, size), lambda i, low: (0, i)),
            ],
            out_specs=pl.BlockSpec((chips, size, lanes), lambda i, low: (0, 0, 0)),
            scratch_shapes=[
                pltpu.VMEM((per, size, HEAD), F32),
                pltpu.VMEM((chips, size, HEAD), F32),
                pltpu.VMEM((chips, size, HEAD), F32),
            ],
        ),
        out_shape=jax.ShapeDtypeStruct((chips, size, lanes), BF),
        name="attend_back",
    )(low, packed, packed, packed, grad, result, logs, start)


def gate_kernel(res_ref, logit_ref, out_ref):
    chips, _, lanes = res_ref.shape
    per = lanes // HEAD
    sig = jax.nn.sigmoid(logit_ref[...])
    for z in range(chips):
        for h in range(per):
            head = z * per + h
            value = res_ref[z, :, h * HEAD : (h + 1) * HEAD].astype(F32)
            out_ref[:, head * HEAD : (head + 1) * HEAD] = (value * sig[:, head : head + 1]).astype(BF)


def gate_rows(result, logits, row):
    chips, size, lanes = result.shape
    block = min(256, size)
    steps = size // block
    return pl.pallas_call(
        gate_kernel,
        grid=(steps,),
        in_specs=[
            pl.BlockSpec((chips, block, lanes), lambda i: (0, i, 0)),
            pl.BlockSpec((block, HEAD), lambda i: (row * steps + i, 0)),
        ],
        out_specs=pl.BlockSpec((block, chips * lanes), lambda i: (i, 0)),
        out_shape=jax.ShapeDtypeStruct((size, chips * lanes), BF),
        name="gate_rows",
    )(result, logits)


def gate_back_kernel(grad_ref, res_ref, logit_ref, out_ref, dlogit_ref):
    chips, size, lanes = res_ref.shape
    per = lanes // HEAD
    sig = jax.nn.sigmoid(logit_ref[...])
    lane = lax.broadcasted_iota(jnp.int32, sig.shape, 1)
    sums = jnp.zeros(sig.shape, F32)
    for z in range(chips):
        for h in range(per):
            head = z * per + h
            e = grad_ref[:, head * HEAD : (head + 1) * HEAD]
            value = res_ref[z, :, h * HEAD : (h + 1) * HEAD].astype(F32)
            out_ref[z, :, h * HEAD : (h + 1) * HEAD] = (e * sig[:, head : head + 1]).astype(BF)
            sums = jnp.where(lane == head, jnp.sum(e * value, axis=-1, keepdims=True), sums)
    dlogit_ref[...] = (sums * sig * (1.0 - sig)).astype(BF)


def gate_back(grad, result, logits, row):
    chips, size, lanes = result.shape
    block = min(256, size)
    steps = size // block
    return pl.pallas_call(
        gate_back_kernel,
        grid=(steps,),
        in_specs=[
            pl.BlockSpec((block, chips * lanes), lambda i: (i, 0)),
            pl.BlockSpec((chips, block, lanes), lambda i: (0, i, 0)),
            pl.BlockSpec((block, HEAD), lambda i: (row * steps + i, 0)),
        ],
        out_specs=[
            pl.BlockSpec((chips, block, lanes), lambda i: (0, i, 0)),
            pl.BlockSpec((block, HEAD), lambda i: (i, 0)),
        ],
        out_shape=[jax.ShapeDtypeStruct((chips, size, lanes), BF), jax.ShapeDtypeStruct((size, HEAD), BF)],
        name="gate_back",
    )(grad, result, logits)


def join_rows_kernel(count, which_ref, *refs):
    out_ref = refs[2 * count]
    size = refs[0].shape[1]
    own_half = pl.program_id(0) == which_ref[0]

    def put(parts):
        for k in range(count):
            out_ref[:, k * size : (k + 1) * size] = parts[k][...].astype(F32)

    pl.when(own_half)(lambda: put(refs[:count]))
    pl.when(jnp.logical_not(own_half))(lambda: put(refs[count : 2 * count]))


def join_rows(mine, other, core, blocks, block):
    count = len(mine)
    height, size = mine[0].shape
    steps = height // block

    def source(side):
        def index(h, i, which):
            active = (h == which[0]) if side == 0 else (h != which[0])
            return (jnp.where(active, i, jnp.where(h == 0, 0, steps - 1)), 0)

        return pl.BlockSpec((block, size), index)

    def target(h, i, which):
        per = which[1]
        return ((i // per) * 2 * per + h * per + i % per, 0)

    return pl.pallas_call(
        functools.partial(join_rows_kernel, count),
        grid_spec=pltpu.PrefetchScalarGridSpec(
            num_scalar_prefetch=1,
            grid=(CORES, steps),
            in_specs=[source(0)] * count + [source(1)] * count,
            out_specs=pl.BlockSpec((block, count * size), target),
        ),
        out_shape=jax.ShapeDtypeStruct((CORES * height, count * size), F32),
        name="join_rows",
    )(jnp.stack([core, blocks.astype(jnp.int32)]), *mine, *other)


def join_cols_kernel(count, per, which_ref, *refs):
    out_ref = refs[2 * count]
    u = pl.program_id(0)
    own_half = pl.program_id(1) == which_ref[0]

    def put(ref):
        out_ref[...] = ref[...].astype(F32)

    for k in range(count):
        here = u // per == k
        pl.when(here & own_half)(functools.partial(put, refs[k]))
        pl.when(here & jnp.logical_not(own_half))(functools.partial(put, refs[count + k]))


def join_cols(mine, other, core, unit):
    count = len(mine)
    height, size = mine[0].shape
    per = size // unit

    def source(k):
        return pl.BlockSpec((height, unit), lambda u, h, which: (0, jnp.clip(u - k * per, 0, per - 1)))

    sources = [source(k) for k in range(count)]
    return pl.pallas_call(
        functools.partial(join_cols_kernel, count, per),
        grid_spec=pltpu.PrefetchScalarGridSpec(
            num_scalar_prefetch=1,
            grid=(count * per, CORES),
            in_specs=sources + sources,
            out_specs=pl.BlockSpec((height, unit), lambda u, h, which: (0, u * CORES + h)),
        ),
        out_shape=jax.ShapeDtypeStruct((height, CORES * count * size), F32),
        name="join_cols",
    )(core[None], *mine, *other)


def join_units_kernel(which_ref, keep_ref, keep_other_ref, sent_ref, sent_other_ref, out_ref):
    kept = pl.program_id(0) == which_ref[1]
    mine = pl.program_id(1) == which_ref[0]
    for side, pair in ((True, (keep_ref, keep_other_ref)), (False, (sent_ref, sent_other_ref))):
        for here, ref in ((True, pair[0]), (False, pair[1])):

            @pl.when((kept == side) & (mine == here))
            def _(ref=ref):
                out_ref[...] = ref[...].astype(F32)


def join_units(mine, other, core, upper):
    height, width = mine[0].shape
    block = 256
    steps = height // block
    sources = []
    for side in (0, 1):
        for half in (0, 1):

            def index(p, h, i, which, side=side, half=half):
                at_side = (p == which[1]) if side == 0 else (p != which[1])
                at_half = (h == which[0]) if half == 0 else (h != which[0])
                side_p = which[1] if side == 0 else 1 - which[1]
                side_h = which[0] if half == 0 else 1 - which[0]
                before = (p * 2 + h) < (side_p * 2 + side_h)
                return (jnp.where(at_side & at_half, i, jnp.where(before, 0, steps - 1)), 0)

            sources.append(pl.BlockSpec((block, width), index))
    return pl.pallas_call(
        join_units_kernel,
        grid_spec=pltpu.PrefetchScalarGridSpec(
            num_scalar_prefetch=1,
            grid=(2, CORES, steps),
            in_specs=sources,
            out_specs=pl.BlockSpec((block, width), lambda p, h, i, which: ((p * CORES + h) * steps + i, 0)),
        ),
        out_shape=jax.ShapeDtypeStruct((2 * CORES * height, width), F32),
        name="join_units",
    )(jnp.stack([core, upper]), mine[0], other[0], mine[1], other[1])


def join_blocks_kernel(which_ref, mine_ref, other_ref, out_ref):
    own_half = pl.program_id(0) == which_ref[0]
    for here, ref in ((True, mine_ref), (False, other_ref)):

        @pl.when(own_half == here)
        def _(ref=ref):
            out_ref[...] = ref[0].astype(F32)


def join_blocks(mine, other, core, order):
    count, height, size = mine.shape
    source = pl.BlockSpec((1, height, size), lambda h, b, which, where: (where[b], 0, 0))
    inverse = [order.index(b) for b in range(count)]
    return pl.pallas_call(
        lambda which_ref, where_ref, *refs: join_blocks_kernel(which_ref, *refs),
        grid_spec=pltpu.PrefetchScalarGridSpec(
            num_scalar_prefetch=2,
            grid=(CORES, count),
            in_specs=[source, source],
            out_specs=pl.BlockSpec((height, size), lambda h, b, which, where: (h, b)),
        ),
        out_shape=jax.ShapeDtypeStruct((CORES * height, count * size), F32),
        name="join_blocks",
    )(core[None], jnp.asarray(inverse, jnp.int32), mine, other)


class Line:
    def __init__(self, chips, chip):
        self.chips = chips
        self.inner = (chip == 1) | (chip == 2)
        ends = lambda pairs: [(a * CORES + c, b * CORES + c) for a, b in pairs for c in range(CORES)]
        self.stages = [ends([(0, 1), (3, 2)]), ends([(1, 2), (2, 1)]), ends([(1, 0), (2, 3)])]
        self.groups = [[z * CORES + c for z in range(chips)] for c in range(CORES)]

    def send(self, x, stage):
        if self.chips != 4:
            return (x, lax.psum(x, "seq", axis_index_groups=self.groups) if stage == 0 else x)
        return (x, lax.ppermute(x, "seq", self.stages[stage]))

    def begin(self, x):
        return (0,) + self.send(x, 0)

    def next(self, state):
        stage, x, moved = state
        if self.chips != 4:
            return (stage + 1, moved, moved)
        return (stage + 1,) + self.send(x + moved, stage + 1)

    def end(self, state):
        stage, x, moved = state
        return moved if self.chips != 4 else jnp.where(self.inner, x, moved)

    def run(self, x):
        return self.end(self.next(self.next(self.begin(x))))


def tie(value, work):
    leaves, tree = jax.tree.flatten(work)
    moving = [x for x in leaves if not isinstance(x, int)]
    value, *moving = lax.optimization_barrier((value, *moving))
    moving = iter(moving)
    return value, jax.tree.unflatten(tree, [x if isinstance(x, int) else next(moving) for x in leaves])


def shards(
    layer_input,
    doc_lengths,
    attn_norm,
    q_norm,
    k_norm,
    ffn_norm,
    w_qkv,
    w_gate,
    w_out,
    w_gu,
    w_down,
    cotangent,
):
    rows, tok, width = layer_input.shape
    seq = lax.axis_size("seq")
    dp = lax.axis_size("dp")
    chips = seq // CORES
    place = lax.axis_index("seq")
    core = place % CORES
    chip = place // CORES
    first = core == 0
    chip_tok = tok * CORES
    length = tok * seq
    tokens = rows * chip_tok
    pair = [(s, s ^ 1) for s in range(seq)]
    groups = [[z * CORES + c for z in range(chips)] for c in range(CORES)]
    q_shard = lax.axis_index("dp") * w_qkv.shape[0] < QUERY_HEADS * HEAD

    def swap(x):
        return lax.ppermute(x, "seq", pair)

    def pick(a, b):
        return jnp.where(first, a, b)

    def both(x):
        other = swap(x)
        return jnp.concatenate([pick(x, other), pick(other, x)], axis=1).reshape(tokens, width)

    def exchange(x):
        return lax.all_to_all(x, "seq", 0, 0, axis_index_groups=groups, tiled=True)

    def total_sum(x, names=("seq", "dp")):
        for name in names:
            size = lax.axis_size(name)
            step = 1
            while step < size:
                x = x + lax.ppermute(x, name, [(s, s ^ step) for s in range(size)])
                step *= 2
        return x

    def scatter(x):
        return lax.psum_scatter(x, "dp", scatter_dimension=0, tiled=True)

    def gather(x):
        return lax.all_gather(x, "dp", axis=0, tiled=True)

    def core_rows(w, unit):
        return jnp.concatenate(
            [pick(w[a : a + unit], w[a + unit : a + 2 * unit]) for a in range(0, w.shape[0], 2 * unit)], axis=0
        )

    def core_cols(w, unit):
        return jnp.concatenate(
            [pick(w[:, a : a + unit], w[:, a + unit : a + 2 * unit]) for a in range(0, w.shape[1], 2 * unit)],
            axis=1,
        )

    half_dp = dp // 2
    me = lax.axis_index("dp")
    upper = me >= half_dp
    trade = [(d, d ^ half_dp) for d in range(dp)]
    units = w_gu.shape[0] // 2
    owned = rows * tok

    qkv_half = jnp.where(q_shard, core_rows(w_qkv, GROUP * HEAD), core_rows(w_qkv, HEAD))
    qkv_full = gather(qkv_half)
    out_full = gather(core_cols(w_out, GROUP * HEAD))
    ctg = cotangent.reshape(owned, width)
    ctg_all = gather(ctg)
    gate_count = w_gate.shape[0]
    gate_full = lax.dynamic_update_slice_in_dim(jnp.zeros((QUERY_HEADS, width), BF), w_gate, me * gate_count, 0)
    gate_full = total_sum(gate_full, ("dp",))
    gate_core = jnp.pad(core_rows(gate_full, GROUP), ((0, HEAD - CORE_Q), (0, 0)))

    gu_keep = jnp.where(upper, w_gu[units:], w_gu[:units])
    quarter = units // 2
    gu_send = jnp.where(
        upper, pick(w_gu[:quarter], w_gu[quarter:units]), pick(w_gu[units : units + quarter], w_gu[units + quarter :])
    )
    out_rows = w_down.shape[0] // 2
    down_core = pick(w_down[:out_rows], w_down[out_rows:])
    unit_block = [(d % half_dp) * 2 + d // half_dp for d in range(dp)]
    down_send = jnp.stack([down_core[:, b * units : (b + 1) * units] for b in unit_block])
    (qkv_full, gu_send, down_send) = lax.optimization_barrier((qkv_full, gu_send, down_send))
    gu_half = lax.ppermute(gu_send, "dp", trade)
    down_half = lax.all_to_all(down_send, "dp", 0, 0, tiled=True)

    start, position = doc_positions(doc_lengths, length)
    low = start.reshape(rows, chips, chip_tok)[:, :, 0] // chip_tok
    local = lax.dynamic_slice_in_dim(position, chip * chip_tok, chip_tok, 1).reshape(tokens)
    freq = jnp.power(theta_base, -(jnp.arange(HEAD // 2, dtype=F32) * 2.0) / HEAD)
    angle = local.astype(F32)[:, None] * freq
    cos = jnp.cos(angle)
    sin = jnp.sin(angle)
    cos = jnp.concatenate([cos, cos], axis=1)
    sin = jnp.concatenate([-sin, sin], axis=1)

    inputs = both(layer_input).astype(F32)
    factor_a = lax.rsqrt(jnp.mean(inputs * inputs, axis=-1, keepdims=True) + epsilon)
    normed_a = (inputs * factor_a * attn_norm).astype(BF)
    logits = dot_nt(normed_a, gate_core)
    proj = dot_nt(normed_a, qkv_full)
    q_gain = q_norm[None, :]
    k_gain = k_norm[None, :]

    packed, results, logs, gated, mid = [], [], [], [], []
    for row in range(rows):
        packed.append(exchange(pack_heads(proj, cos, sin, q_gain, k_gain, row, chips, chip_tok)))
    packed[0], logits = tie(packed[0], logits)
    for row in range(rows):
        head_out, log = attend(packed[row], start[row : row + 1], low[row])
        results.append(head_out)
        logs.append(log)
    tok_results = [exchange(r) for r in results]
    tok_results[0], (gu_half, down_half) = tie(tok_results[0], (gu_half, down_half))
    gu_other = swap(gu_half)
    down_other = swap(down_half)
    for row in range(rows):
        gated.append(gate_rows(tok_results[row], logits, row))
        part = dot_nt(gated[row], out_full, BF).reshape(CORES, tok, width)
        other = swap(pick(part[1], part[0]))
        mid.append(layer_input[row].astype(F32) + pick(part[0], part[1]).astype(F32) + other.astype(F32))
    mid = jnp.concatenate(mid, axis=0)
    gated = jnp.concatenate(gated, axis=0)

    factor_f = lax.rsqrt(jnp.mean(mid * mid, axis=-1, keepdims=True) + epsilon)
    normed_f = (mid * factor_f * ffn_norm).astype(BF)
    normed_all = gather(normed_f)
    gu_recv = jnp.concatenate([pick(gu_half, gu_other), pick(gu_other, gu_half)], axis=0)
    down_full = jnp.concatenate([pick(down_half, down_other), pick(down_other, down_half)], axis=1)
    down_full = down_full.reshape(width, units)
    d_hidden = dot_nn(ctg_all, down_full, BF)
    normed_all, (d_hidden, gu_recv) = tie(normed_all, (d_hidden, gu_recv))
    keep_part = dot_nt(normed_all, gu_keep, BF)
    recv_part = dot_nt(normed_all, gu_recv, BF)
    gate_part = jnp.where(upper, recv_part, keep_part).astype(F32)
    up_part = jnp.where(upper, keep_part, recv_part).astype(F32)
    d_hid = d_hidden.astype(F32)
    gate_act = jax.nn.sigmoid(gate_part)
    silu = gate_part * gate_act
    hidden = (silu * up_part).astype(BF)
    d_gate = d_hid * up_part * gate_act * (1.0 + gate_part * (1.0 - gate_act))
    d_up = d_hid * silu
    d_keep = jnp.where(upper, d_up, d_gate).astype(BF)
    d_recv = jnp.where(upper, d_gate, d_up).astype(BF)
    d_normed = scatter((dot_nn(d_keep, gu_keep) + dot_nn(d_recv, gu_recv)).astype(BF))

    part_keep = dot_tn(d_keep, normed_all, BF)
    part_recv = dot_tn(d_recv, normed_all, BF)
    part_down = dot_tn(ctg_all, hidden, BF).reshape(dp, CORES, out_rows, units)
    out_part = dot_nt(hidden, down_full, BF)
    keep_swap = swap(pick(part_keep[quarter:], part_keep[:quarter]))
    recv_swap = swap(pick(part_recv[quarter:], part_recv[:quarter]))
    down_swap = swap(pick(part_down[:, 1], part_down[:, 0]))
    d_normed, (part_keep, part_recv, part_down, out_part) = tie(
        d_normed, (part_keep, part_recv, part_down, out_part)
    )
    output = (mid + scatter(out_part).astype(F32)).astype(BF).reshape(rows, tok, width)

    d_normed = d_normed.astype(F32)
    part_ffn = jnp.sum(d_normed * mid * factor_f, axis=0)
    weighted = d_normed * ffn_norm
    inner = jnp.mean(weighted * mid, axis=-1, keepdims=True)
    d_mid = ctg.astype(F32) + factor_f * weighted - mid * factor_f**3 * inner
    low_mine = d_mid.astype(BF).reshape(rows, tok, width)
    low_other = swap(low_mine)
    low_other, (keep_swap, recv_swap, down_swap) = tie(low_other, (keep_swap, recv_swap, down_swap))
    keep_sum = pick(part_keep[:quarter], part_keep[quarter:]) + keep_swap
    recv_sum = pick(part_recv[:quarter], part_recv[quarter:]) + recv_swap
    down_sum = pick(part_down[:, 0], part_down[:, 1]) + down_swap
    sent_sum = lax.ppermute(recv_sum, "dp", trade)
    down_sum = lax.all_to_all(down_sum, "dp", 0, 0, tiled=True)
    line = Line(chips, chip)
    keep_line = line.begin(keep_sum)

    d_mid_low = jnp.concatenate([pick(low_mine, low_other), pick(low_other, low_mine)], axis=1).reshape(tokens, width)
    part_out = dot_tn(d_mid_low, gated, BF)
    d_proj, d_logit, d_heads = [], [], []
    q_sum = 0.0
    k_sum = 0.0
    for row in range(rows):
        d_gated = dot_nn(d_mid_low[row * chip_tok : (row + 1) * chip_tok], out_full)
        d_attn, dl = gate_back(d_gated, tok_results[row], logits, row)
        d_logit.append(dl)
        d_heads.append(exchange(d_attn))
    d_heads[0], (keep_line, sent_sum, down_sum, part_out) = tie(d_heads[0], (keep_line, sent_sum, down_sum, part_out))
    shard_out = scatter(part_out)
    keep_line = line.next(keep_line)
    down_line = line.begin(down_sum)
    back = []
    for row in range(rows):
        grad = d_heads[row]
        if row:
            grad, (keep_line, down_line) = tie(grad, (keep_line, down_line))
            keep_line = line.next(keep_line)
            down_line = line.next(down_line)
            sent_line = line.begin(sent_sum)
        back.append(exchange(attend_back(packed[row], grad, results[row], logs[row], start[row : row + 1], low[row])))
    back[0], (keep_line, down_line, sent_line) = tie(back[0], (keep_line, down_line, sent_line))
    keep_done = line.end(keep_line)
    down_line = line.next(down_line)
    sent_line = line.next(sent_line)
    keep_other = swap(keep_done)
    for row in range(rows):
        grads = back[row]
        if row:
            grads, (down_line, sent_line) = tie(grads, (down_line, sent_line))
            down_done = line.end(down_line)
            sent_line = line.next(sent_line)
            down_other = swap(down_done)
        dpr, qs, ks = unpack_heads(grads, proj, cos, sin, q_gain, k_gain, row, chips, chip_tok)
        d_proj.append(dpr)
        q_sum = q_sum + qs
        k_sum = k_sum + ks
    d_proj = jnp.concatenate(d_proj, axis=0)
    d_logit = jnp.concatenate(d_logit, axis=0)
    half = width // 2
    shard_qkv = [scatter(dot_tn(d_proj, normed_a[:, a : a + half], BF)) for a in (0, half)]
    d_norm_part = (dot_nn(d_proj, qkv_full) + dot_nn(d_logit, gate_core)).astype(BF)
    d_norm_part = d_norm_part.reshape(rows, CORES, tok, width)
    d_norm_other = swap(pick(d_norm_part[:, 1], d_norm_part[:, 0]))
    sent_done = line.end(sent_line)
    sent_other = swap(sent_done)
    d_normed_a = pick(d_norm_part[:, 0], d_norm_part[:, 1]).astype(F32) + d_norm_other.astype(F32)
    own_in = layer_input.astype(F32)
    own_factor = lax.rsqrt(jnp.mean(own_in * own_in, axis=-1, keepdims=True) + epsilon)
    part_attn = jnp.sum(d_normed_a * own_in * own_factor, axis=(0, 1))
    weighted_a = d_normed_a * attn_norm
    inner_a = jnp.mean(weighted_a * own_in, axis=-1, keepdims=True)
    grad_input = (
        d_mid.reshape(rows, tok, width) + own_factor * weighted_a - own_in * own_factor**3 * inner_a
    ).astype(BF)

    part_gate = dot_tn(d_logit, normed_a)[:CORE_Q]
    zero = jnp.zeros_like(part_gate)
    part_gate = jnp.stack(
        [pick(part_gate, zero).reshape(-1, GROUP, width), pick(zero, part_gate).reshape(-1, GROUP, width)], 1
    )
    part_gate = part_gate.reshape(QUERY_HEADS, width)
    heads = jnp.concatenate([jnp.sum(q_sum, axis=0), jnp.sum(k_sum, axis=0)])
    heads = jnp.pad(heads, (0, width - heads.shape[0]))
    early = total_sum(jnp.concatenate([part_gate, part_ffn[None], jnp.zeros((7, width), F32)], axis=0))
    late = total_sum(jnp.stack([part_attn, heads]))
    grad_w_gate = lax.dynamic_slice_in_dim(early, me * gate_count, gate_count, 0)

    grad_gu = join_units([keep_done, sent_done], [keep_other, sent_other], core, upper.astype(jnp.int32))
    grad_down = join_blocks(down_done, down_other, core, unit_block)
    out_sum = line.run(shard_out)
    grad_out = join_cols([out_sum], [swap(out_sum)], core, GROUP * HEAD)
    qkv_sum = [line.run(p) for p in shard_qkv]
    grad_qkv = join_rows(
        qkv_sum, [swap(p) for p in qkv_sum], core, jnp.where(q_shard, GROUP * HEAD // HEAD, 1), HEAD
    )
    return (
        output,
        grad_input,
        late[0],
        late[1, :HEAD],
        late[1, HEAD : 2 * HEAD],
        early[QUERY_HEADS],
        grad_qkv,
        grad_w_gate,
        grad_out,
        grad_gu,
        grad_down,
    )


def solution(mesh):
    token = P("dp", "seq", None)
    shard = P("dp", None)
    in_specs = (token, shard, P(), P(), P(), P(), shard, shard, shard, shard, shard, token)
    out_specs = (token, token, P(), P(), P(), P(), shard, shard, shard, shard, shard)
    return jax.shard_map(shards, mesh=mesh, in_specs=in_specs, out_specs=out_specs, check_vma=False)
```

```python
import functools
import math

import jax
import jax.numpy as jnp
from jax import lax
from jax.experimental import pallas as pl
from jax.experimental.pallas import tpu as pltpu
from jax.sharding import PartitionSpec as P

QUERY_HEADS = 16
KEY_VALUE_HEADS = 8
HEAD = 128
FF = 6144
CORES = 2

GROUP = QUERY_HEADS // KEY_VALUE_HEADS
CORE_Q = QUERY_HEADS // CORES
CORE_KV = KEY_VALUE_HEADS // CORES
epsilon = 1e-06
theta_base = 1000000.0
SCALE = 1.0 / math.sqrt(HEAD)
SCALE2 = SCALE * math.log2(math.e)
BF = jnp.bfloat16
F32 = jnp.float32


def dot_nt(left, right, out=F32):
    return lax.dot_general(left, right, (((1,), (1,)), ((), ())), preferred_element_type=F32).astype(out)


def dot_nn(left, right, out=F32):
    return lax.dot_general(left, right, (((1,), (0,)), ((), ())), preferred_element_type=F32).astype(out)


def dot_tn(left, right, out=F32):
    return lax.dot_general(left, right, (((0,), (0,)), ((), ())), preferred_element_type=F32).astype(out)


def doc_positions(lengths, total):
    ends = jnp.cumsum(lengths, axis=-1)
    starts = ends - lengths
    places = jnp.arange(total, dtype=jnp.int32)
    segment = jnp.sum((places[:, None] >= ends[..., None, :]).astype(jnp.int32), axis=-1)
    owners = segment[..., None] == jnp.arange(lengths.shape[-1], dtype=jnp.int32)
    first = jnp.sum(jnp.where(owners, starts[..., None, :], 0), axis=-1)
    return first, places - first


def pack_kernel(chips, proj_ref, cos_ref, sin_ref, qg_ref, kg_ref, out_ref):
    per = CORE_Q // chips
    copies = max(1, chips // CORE_KV)
    cos = cos_ref[...]
    sin = sin_ref[...]

    def head(index, gain):
        u = proj_ref[:, index * HEAD : (index + 1) * HEAD]
        factor = lax.rsqrt(jnp.mean(u * u, axis=-1, keepdims=True) + epsilon)
        n = u * factor * gain
        return (n * cos + pltpu.roll(n, HEAD // 2, 1) * sin).astype(BF)

    for z in range(chips):
        for h in range(per):
            out_ref[z, :, h * HEAD : (h + 1) * HEAD] = head(z * per + h, qg_ref[...])
        if z % copies == 0:
            kv = z // copies
            key = head(CORE_Q + kv, kg_ref[...])
            base = (CORE_Q + CORE_KV + kv) * HEAD
            value = proj_ref[:, base : base + HEAD].astype(BF)
        out_ref[z, :, per * HEAD : (per + 1) * HEAD] = key
        out_ref[z, :, (per + 1) * HEAD : (per + 2) * HEAD] = value


def pack_heads(proj, cos, sin, q_gain, k_gain, row, chips, chip_tok):
    per = CORE_Q // chips
    lanes = (per + 2) * HEAD
    block = min(256, chip_tok)
    steps = chip_tok // block
    width = proj.shape[1]
    tok = lambda i: (row * steps + i, 0)
    return pl.pallas_call(
        functools.partial(pack_kernel, chips),
        grid=(steps,),
        in_specs=[
            pl.BlockSpec((block, width), tok),
            pl.BlockSpec((block, HEAD), tok),
            pl.BlockSpec((block, HEAD), tok),
            pl.BlockSpec((1, HEAD), lambda i: (0, 0)),
            pl.BlockSpec((1, HEAD), lambda i: (0, 0)),
        ],
        out_specs=pl.BlockSpec((chips, block, lanes), lambda i: (0, i, 0)),
        out_shape=jax.ShapeDtypeStruct((chips, chip_tok, lanes), BF),
        name="pack_heads",
    )(proj, cos, sin, q_gain, k_gain)


def unpack_kernel(chips, grad_ref, proj_ref, cos_ref, sin_ref, qg_ref, kg_ref, out_ref, qs_ref, ks_ref):
    per = CORE_Q // chips
    copies = max(1, chips // CORE_KV)
    cos = cos_ref[...]
    sin = sin_ref[...]

    @pl.when(pl.program_id(0) == 0)
    def _():
        qs_ref[...] = jnp.zeros_like(qs_ref)
        ks_ref[...] = jnp.zeros_like(ks_ref)

    def head(e, index, gain, sum_ref):
        e = e * cos + pltpu.roll(e * sin, HEAD // 2, 1)
        u = proj_ref[:, index * HEAD : (index + 1) * HEAD]
        factor = lax.rsqrt(jnp.mean(u * u, axis=-1, keepdims=True) + epsilon)
        n = u * factor
        sum_ref[...] += jnp.sum((e * n).reshape(-1, 8, HEAD), axis=0)
        weighted = e * gain
        inner = jnp.mean(weighted * n, axis=-1, keepdims=True)
        out_ref[:, index * HEAD : (index + 1) * HEAD] = (factor * (weighted - n * inner)).astype(BF)

    def part(z, lane):
        return grad_ref[z, :, lane * HEAD : (lane + 1) * HEAD].astype(F32)

    for z in range(chips):
        for h in range(per):
            head(part(z, h), z * per + h, qg_ref[...], qs_ref)
    for kv in range(CORE_KV):
        spread = range(kv * copies, (kv + 1) * copies)
        head(sum(part(z, per) for z in spread), CORE_Q + kv, kg_ref[...], ks_ref)
        base = (CORE_Q + CORE_KV + kv) * HEAD
        out_ref[:, base : base + HEAD] = sum(part(z, per + 1) for z in spread).astype(BF)


def unpack_heads(grads, proj, cos, sin, q_gain, k_gain, row, chips, chip_tok):
    lanes = grads.shape[2]
    block = min(256, chip_tok)
    steps = chip_tok // block
    width = proj.shape[1]
    tok = lambda i: (row * steps + i, 0)
    small = pl.BlockSpec((8, HEAD), lambda i: (0, 0))
    return pl.pallas_call(
        functools.partial(unpack_kernel, chips),
        grid=(steps,),
        in_specs=[
            pl.BlockSpec((chips, block, lanes), lambda i: (0, i, 0)),
            pl.BlockSpec((block, width), tok),
            pl.BlockSpec((block, HEAD), tok),
            pl.BlockSpec((block, HEAD), tok),
            pl.BlockSpec((1, HEAD), lambda i: (0, 0)),
            pl.BlockSpec((1, HEAD), lambda i: (0, 0)),
        ],
        out_specs=[pl.BlockSpec((block, width), lambda i: (i, 0)), small, small],
        out_shape=[
            jax.ShapeDtypeStruct((chip_tok, width), BF),
            jax.ShapeDtypeStruct((8, HEAD), F32),
            jax.ShapeDtypeStruct((8, HEAD), F32),
        ],
        name="unpack_heads",
    )(grads, proj, cos, sin, q_gain, k_gain)


def visible(j, size, start, diagonal):
    inner = lax.broadcasted_iota(jnp.int32, (size, size), 0)
    allowed = inner >= start - j * size
    if diagonal:
        allowed = allowed & (inner <= lax.broadcasted_iota(jnp.int32, (size, size), 1))
    return allowed


def attend_kernel(per, low_ref, q_ref, k_ref, v_ref, start_ref, out_ref, log_ref, acc_ref, sum_ref):
    i = pl.program_id(0)
    size = q_ref.shape[1]
    start = start_ref[...]
    acc_ref[...] = jnp.zeros_like(acc_ref)
    sum_ref[...] = jnp.zeros_like(sum_ref)

    def one(j, diagonal):
        key = k_ref[j]
        value = v_ref[j]
        allowed = visible(j, size, start, diagonal)
        for h in range(per):
            scores = dot_nt(key, q_ref[0, :, h * HEAD : (h + 1) * HEAD])
            p = jnp.where(allowed, jnp.exp2(scores * SCALE2), 0.0)
            sum_ref[h : h + 1, :] += jnp.sum(p, axis=0, keepdims=True)
            acc_ref[h] += dot_tn(value, p.astype(BF))

    def step(j, carry):
        one(j, False)
        return carry

    lax.fori_loop(low_ref[i], i, step, 0)
    one(i, True)
    for h in range(per):
        total = sum_ref[h : h + 1, :]
        out_ref[0, :, h * HEAD : (h + 1) * HEAD] = (acc_ref[h] / total).T.astype(BF)
        log_ref[h : h + 1, :] = jnp.log2(total)


def attend(packed, start, low):
    chips, size, lanes = packed.shape
    per = lanes // HEAD - 2
    return pl.pallas_call(
        functools.partial(attend_kernel, per),
        grid_spec=pltpu.PrefetchScalarGridSpec(
            num_scalar_prefetch=1,
            grid=(chips,),
            in_specs=[
                pl.BlockSpec((1, size, per * HEAD), lambda i, low: (i, 0, 0)),
                pl.BlockSpec((chips, size, HEAD), lambda i, low: (0, 0, per)),
                pl.BlockSpec((chips, size, HEAD), lambda i, low: (0, 0, per + 1)),
                pl.BlockSpec((1, size), lambda i, low: (0, i)),
            ],
            out_specs=[
                pl.BlockSpec((1, size, per * HEAD), lambda i, low: (i, 0, 0)),
                pl.BlockSpec((per, size), lambda i, low: (0, i)),
            ],
            scratch_shapes=[pltpu.VMEM((per, HEAD, size), F32), pltpu.VMEM((per, size), F32)],
        ),
        out_shape=[
            jax.ShapeDtypeStruct((chips, size, per * HEAD), BF),
            jax.ShapeDtypeStruct((per, chips * size), F32),
        ],
        name="attend",
    )(low, packed, packed, packed, start)


def attend_back_kernel(
    per, low_ref, q_ref, k_ref, v_ref, grad_ref, res_ref, log_ref, start_ref, out_ref, dq_ref, dk_ref, dv_ref
):
    i = pl.program_id(0)
    size = q_ref.shape[1]
    start = start_ref[...]

    @pl.when(i == 0)
    def _():
        dk_ref[...] = jnp.zeros_like(dk_ref)
        dv_ref[...] = jnp.zeros_like(dv_ref)

    dq_ref[...] = jnp.zeros_like(dq_ref)
    ones = jnp.ones((8, HEAD), F32)
    inner = []
    for h in range(per):
        cols = slice(h * HEAD, (h + 1) * HEAD)
        both = grad_ref[0, :, cols].astype(F32) * res_ref[0, :, cols].astype(F32)
        sums = lax.dot_general(
            ones, both, (((1,), (1,)), ((), ())), precision=lax.Precision.HIGHEST, preferred_element_type=F32
        )
        inner.append(sums[0:1, :])

    def one(j, diagonal):
        key = k_ref[j]
        value = v_ref[j]
        allowed = visible(j, size, start, diagonal)
        for h in range(per):
            query = q_ref[0, :, h * HEAD : (h + 1) * HEAD]
            grad = grad_ref[0, :, h * HEAD : (h + 1) * HEAD]
            scores = dot_nt(key, query)
            p = jnp.where(allowed, jnp.exp2(scores * SCALE2 - log_ref[h : h + 1, :]), 0.0)
            dp = dot_nt(value, grad)
            ds = (p * (dp - inner[h])).astype(BF)
            dv_ref[j] += dot_nn(p.astype(BF), grad)
            dk_ref[j] += dot_nn(ds, query)
            dq_ref[h] += dot_tn(ds, key)

    def step(j, carry):
        one(j, False)
        return carry

    lax.fori_loop(low_ref[i], i, step, 0)
    one(i, True)
    for h in range(per):
        out_ref[i, :, h * HEAD : (h + 1) * HEAD] = (dq_ref[h] * SCALE).astype(BF)

    @pl.when(i == pl.num_programs(0) - 1)
    def _():
        out_ref[:, :, per * HEAD : (per + 1) * HEAD] = (dk_ref[...] * SCALE).astype(BF)
        out_ref[:, :, (per + 1) * HEAD : (per + 2) * HEAD] = dv_ref[...].astype(BF)


def attend_back(packed, grad, result, logs, start, low):
    chips, size, lanes = packed.shape
    per = lanes // HEAD - 2
    one = pl.BlockSpec((1, size, per * HEAD), lambda i, low: (i, 0, 0))
    return pl.pallas_call(
        functools.partial(attend_back_kernel, per),
        grid_spec=pltpu.PrefetchScalarGridSpec(
            num_scalar_prefetch=1,
            grid=(chips,),
            in_specs=[
                one,
                pl.BlockSpec((chips, size, HEAD), lambda i, low: (0, 0, per)),
                pl.BlockSpec((chips, size, HEAD), lambda i, low: (0, 0, per + 1)),
                one,
                one,
                pl.BlockSpec((per, size), lambda i, low: (0, i)),
                pl.BlockSpec((1, size), lambda i, low: (0, i)),
            ],
            out_specs=pl.BlockSpec((chips, size, lanes), lambda i, low: (0, 0, 0)),
            scratch_shapes=[
                pltpu.VMEM((per, size, HEAD), F32),
                pltpu.VMEM((chips, size, HEAD), F32),
                pltpu.VMEM((chips, size, HEAD), F32),
            ],
        ),
        out_shape=jax.ShapeDtypeStruct((chips, size, lanes), BF),
        name="attend_back",
    )(low, packed, packed, packed, grad, result, logs, start)


def gate_kernel(res_ref, logit_ref, out_ref):
    chips, _, lanes = res_ref.shape
    per = lanes // HEAD
    sig = jax.nn.sigmoid(logit_ref[...])
    for z in range(chips):
        for h in range(per):
            head = z * per + h
            value = res_ref[z, :, h * HEAD : (h + 1) * HEAD].astype(F32)
            out_ref[:, head * HEAD : (head + 1) * HEAD] = (value * sig[:, head : head + 1]).astype(BF)


def gate_rows(result, logits, row):
    chips, size, lanes = result.shape
    block = min(256, size)
    steps = size // block
    return pl.pallas_call(
        gate_kernel,
        grid=(steps,),
        in_specs=[
            pl.BlockSpec((chips, block, lanes), lambda i: (0, i, 0)),
            pl.BlockSpec((block, HEAD), lambda i: (row * steps + i, 0)),
        ],
        out_specs=pl.BlockSpec((block, chips * lanes), lambda i: (i, 0)),
        out_shape=jax.ShapeDtypeStruct((size, chips * lanes), BF),
        name="gate_rows",
    )(result, logits)


def gate_back_kernel(grad_ref, res_ref, logit_ref, out_ref, dlogit_ref):
    chips, size, lanes = res_ref.shape
    per = lanes // HEAD
    sig = jax.nn.sigmoid(logit_ref[...])
    lane = lax.broadcasted_iota(jnp.int32, sig.shape, 1)
    sums = jnp.zeros(sig.shape, F32)
    for z in range(chips):
        for h in range(per):
            head = z * per + h
            e = grad_ref[:, head * HEAD : (head + 1) * HEAD]
            value = res_ref[z, :, h * HEAD : (h + 1) * HEAD].astype(F32)
            out_ref[z, :, h * HEAD : (h + 1) * HEAD] = (e * sig[:, head : head + 1]).astype(BF)
            sums = jnp.where(lane == head, jnp.sum(e * value, axis=-1, keepdims=True), sums)
    dlogit_ref[...] = (sums * sig * (1.0 - sig)).astype(BF)


def gate_back(grad, result, logits, row):
    chips, size, lanes = result.shape
    block = min(256, size)
    steps = size // block
    return pl.pallas_call(
        gate_back_kernel,
        grid=(steps,),
        in_specs=[
            pl.BlockSpec((block, chips * lanes), lambda i: (i, 0)),
            pl.BlockSpec((chips, block, lanes), lambda i: (0, i, 0)),
            pl.BlockSpec((block, HEAD), lambda i: (row * steps + i, 0)),
        ],
        out_specs=[
            pl.BlockSpec((chips, block, lanes), lambda i: (0, i, 0)),
            pl.BlockSpec((block, HEAD), lambda i: (i, 0)),
        ],
        out_shape=[jax.ShapeDtypeStruct((chips, size, lanes), BF), jax.ShapeDtypeStruct((size, HEAD), BF)],
        name="gate_back",
    )(grad, result, logits)


def join_rows_kernel(count, which_ref, *refs):
    out_ref = refs[2 * count]
    size = refs[0].shape[1]
    own_half = pl.program_id(0) == which_ref[0]

    def put(parts):
        for k in range(count):
            out_ref[:, k * size : (k + 1) * size] = parts[k][...].astype(F32)

    pl.when(own_half)(lambda: put(refs[:count]))
    pl.when(jnp.logical_not(own_half))(lambda: put(refs[count : 2 * count]))


def join_rows(mine, other, core, blocks, block):
    count = len(mine)
    height, size = mine[0].shape
    steps = height // block

    def source(side):
        def index(h, i, which):
            active = (h == which[0]) if side == 0 else (h != which[0])
            return (jnp.where(active, i, jnp.where(h == 0, 0, steps - 1)), 0)

        return pl.BlockSpec((block, size), index)

    def target(h, i, which):
        per = which[1]
        return ((i // per) * 2 * per + h * per + i % per, 0)

    return pl.pallas_call(
        functools.partial(join_rows_kernel, count),
        grid_spec=pltpu.PrefetchScalarGridSpec(
            num_scalar_prefetch=1,
            grid=(CORES, steps),
            in_specs=[source(0)] * count + [source(1)] * count,
            out_specs=pl.BlockSpec((block, count * size), target),
        ),
        out_shape=jax.ShapeDtypeStruct((CORES * height, count * size), F32),
        name="join_rows",
    )(jnp.stack([core, blocks.astype(jnp.int32)]), *mine, *other)


def join_cols_kernel(count, per, which_ref, *refs):
    out_ref = refs[2 * count]
    u = pl.program_id(0)
    own_half = pl.program_id(1) == which_ref[0]

    def put(ref):
        out_ref[...] = ref[...].astype(F32)

    for k in range(count):
        here = u // per == k
        pl.when(here & own_half)(functools.partial(put, refs[k]))
        pl.when(here & jnp.logical_not(own_half))(functools.partial(put, refs[count + k]))


def join_cols(mine, other, core, unit):
    count = len(mine)
    height, size = mine[0].shape
    per = size // unit

    def source(k):
        return pl.BlockSpec((height, unit), lambda u, h, which: (0, jnp.clip(u - k * per, 0, per - 1)))

    sources = [source(k) for k in range(count)]
    return pl.pallas_call(
        functools.partial(join_cols_kernel, count, per),
        grid_spec=pltpu.PrefetchScalarGridSpec(
            num_scalar_prefetch=1,
            grid=(count * per, CORES),
            in_specs=sources + sources,
            out_specs=pl.BlockSpec((height, unit), lambda u, h, which: (0, u * CORES + h)),
        ),
        out_shape=jax.ShapeDtypeStruct((height, CORES * count * size), F32),
        name="join_cols",
    )(core[None], *mine, *other)


def join_units_kernel(which_ref, keep_ref, keep_other_ref, sent_ref, sent_other_ref, out_ref):
    kept = pl.program_id(0) == which_ref[1]
    mine = pl.program_id(1) == which_ref[0]
    for side, pair in ((True, (keep_ref, keep_other_ref)), (False, (sent_ref, sent_other_ref))):
        for here, ref in ((True, pair[0]), (False, pair[1])):

            @pl.when((kept == side) & (mine == here))
            def _(ref=ref):
                out_ref[...] = ref[...].astype(F32)


def join_units(mine, other, core, upper):
    height, width = mine[0].shape
    block = 256
    steps = height // block
    sources = []
    for side in (0, 1):
        for half in (0, 1):

            def index(p, h, i, which, side=side, half=half):
                at_side = (p == which[1]) if side == 0 else (p != which[1])
                at_half = (h == which[0]) if half == 0 else (h != which[0])
                side_p = which[1] if side == 0 else 1 - which[1]
                side_h = which[0] if half == 0 else 1 - which[0]
                before = (p * 2 + h) < (side_p * 2 + side_h)
                return (jnp.where(at_side & at_half, i, jnp.where(before, 0, steps - 1)), 0)

            sources.append(pl.BlockSpec((block, width), index))
    return pl.pallas_call(
        join_units_kernel,
        grid_spec=pltpu.PrefetchScalarGridSpec(
            num_scalar_prefetch=1,
            grid=(2, CORES, steps),
            in_specs=sources,
            out_specs=pl.BlockSpec((block, width), lambda p, h, i, which: ((p * CORES + h) * steps + i, 0)),
        ),
        out_shape=jax.ShapeDtypeStruct((2 * CORES * height, width), F32),
        name="join_units",
    )(jnp.stack([core, upper]), mine[0], other[0], mine[1], other[1])


def join_blocks_kernel(which_ref, mine_ref, other_ref, out_ref):
    own_half = pl.program_id(0) == which_ref[0]
    for here, ref in ((True, mine_ref), (False, other_ref)):

        @pl.when(own_half == here)
        def _(ref=ref):
            out_ref[...] = ref[0].astype(F32)


def join_blocks(mine, other, core, order):
    count, height, size = mine.shape
    source = pl.BlockSpec((1, height, size), lambda h, b, which, where: (where[b], 0, 0))
    return pl.pallas_call(
        lambda which_ref, where_ref, *refs: join_blocks_kernel(which_ref, *refs),
        grid_spec=pltpu.PrefetchScalarGridSpec(
            num_scalar_prefetch=2,
            grid=(CORES, count),
            in_specs=[source, source],
            out_specs=pl.BlockSpec((height, size), lambda h, b, which, where: (h, b)),
        ),
        out_shape=jax.ShapeDtypeStruct((CORES * height, count * size), F32),
        name="join_blocks",
    )(core[None], jnp.stack(order).astype(jnp.int32), mine, other)


class Line:
    def __init__(self, chips, chip):
        self.chips = chips
        self.inner = (chip == 1) | (chip == 2)
        ends = lambda pairs: [(a * CORES + c, b * CORES + c) for a, b in pairs for c in range(CORES)]
        self.stages = [ends([(0, 1), (3, 2)]), ends([(1, 2), (2, 1)]), ends([(1, 0), (2, 3)])]
        self.groups = [[z * CORES + c for z in range(chips)] for c in range(CORES)]

    def send(self, x, stage):
        if self.chips != 4:
            return (x, lax.psum(x, "seq", axis_index_groups=self.groups) if stage == 0 else x)
        return (x, lax.ppermute(x, "seq", self.stages[stage]))

    def begin(self, x):
        return (0,) + self.send(x, 0)

    def next(self, state):
        stage, x, moved = state
        if self.chips != 4:
            return (stage + 1, moved, moved)
        return (stage + 1,) + self.send(x + moved, stage + 1)

    def end(self, state):
        stage, x, moved = state
        return moved if self.chips != 4 else jnp.where(self.inner, x, moved)

    def run(self, x):
        return self.end(self.next(self.next(self.begin(x))))


def tie(value, work):
    leaves, tree = jax.tree.flatten(work)
    moving = [x for x in leaves if not isinstance(x, int)]
    value, *moving = lax.optimization_barrier((value, *moving))
    moving = iter(moving)
    return value, jax.tree.unflatten(tree, [x if isinstance(x, int) else next(moving) for x in leaves])


def shards(
    layer_input,
    doc_lengths,
    attn_norm,
    q_norm,
    k_norm,
    ffn_norm,
    w_qkv,
    w_gate,
    w_out,
    w_gu,
    w_down,
    cotangent,
):
    rows, tok, width = layer_input.shape
    seq = lax.axis_size("seq")
    dp = lax.axis_size("dp")
    chips = seq // CORES
    place = lax.axis_index("seq")
    core = place % CORES
    chip = place // CORES
    first = core == 0
    chip_tok = tok * CORES
    length = tok * seq
    tokens = rows * chip_tok
    pair = [(s, s ^ 1) for s in range(seq)]
    groups = [[z * CORES + c for z in range(chips)] for c in range(CORES)]
    q_shard = lax.axis_index("dp") * w_qkv.shape[0] < QUERY_HEADS * HEAD

    def swap(x):
        return lax.ppermute(x, "seq", pair)

    def pick(a, b):
        return jnp.where(first, a, b)

    def both(x):
        other = swap(x)
        return jnp.concatenate([pick(x, other), pick(other, x)], axis=1).reshape(tokens, width)

    def exchange(x):
        return lax.all_to_all(x, "seq", 0, 0, axis_index_groups=groups, tiled=True)

    def total_sum(x, names=("seq", "dp")):
        for name in names:
            size = lax.axis_size(name)
            step = 1
            while step < size:
                x = x + lax.ppermute(x, name, [(s, s ^ step) for s in range(size)])
                step *= 2
        return x

    def scatter(x):
        return lax.psum_scatter(x, "dp", scatter_dimension=0, tiled=True)

    def gather(x):
        return lax.all_gather(x, "dp", axis=0, tiled=True)

    def core_rows(w, unit):
        return jnp.concatenate(
            [pick(w[a : a + unit], w[a + unit : a + 2 * unit]) for a in range(0, w.shape[0], 2 * unit)], axis=0
        )

    def core_cols(w, unit):
        return jnp.concatenate(
            [pick(w[:, a : a + unit], w[:, a + unit : a + 2 * unit]) for a in range(0, w.shape[1], 2 * unit)],
            axis=1,
        )

    def trade_blocks(x):
        mine = lax.axis_index("dp")
        found = [(mine, lax.dynamic_index_in_dim(x, mine, 0, keepdims=False))]
        for k in range(1, dp):
            out = lax.dynamic_index_in_dim(x, mine ^ k, 0, keepdims=False)
            found.append((mine ^ k, lax.ppermute(out, "dp", [(d, d ^ k) for d in range(dp)])))
        return found

    half_dp = dp // 2
    me = lax.axis_index("dp")
    upper = me >= half_dp
    trade = [(d, d ^ half_dp) for d in range(dp)]
    units = w_gu.shape[0] // 2
    owned = rows * tok

    qkv_half = jnp.where(q_shard, core_rows(w_qkv, GROUP * HEAD), core_rows(w_qkv, HEAD))
    qkv_full = gather(qkv_half)
    out_full = gather(core_cols(w_out, GROUP * HEAD))
    ctg = cotangent.reshape(owned, width)
    gate_count = w_gate.shape[0]
    gate_full = lax.dynamic_update_slice_in_dim(jnp.zeros((QUERY_HEADS, width), BF), w_gate, me * gate_count, 0)
    gate_full = total_sum(gate_full, ("dp",))
    gate_core = jnp.pad(core_rows(gate_full, GROUP), ((0, HEAD - CORE_Q), (0, 0)))

    gu_keep = jnp.where(upper, w_gu[units:], w_gu[:units])
    quarter = units // 2
    gu_send = jnp.where(
        upper, pick(w_gu[:quarter], w_gu[quarter:units]), pick(w_gu[units : units + quarter], w_gu[units + quarter :])
    )
    out_rows = w_down.shape[0] // 2
    down_core = pick(w_down[:out_rows], w_down[out_rows:])
    unit_block = [(d % half_dp) * 2 + d // half_dp for d in range(dp)]
    down_send = jnp.stack([down_core[:, b * units : (b + 1) * units] for b in unit_block])
    (qkv_full, gu_send, down_send) = lax.optimization_barrier((qkv_full, gu_send, down_send))
    gu_half = lax.ppermute(gu_send, "dp", trade)
    down_half = jnp.zeros_like(down_send)
    for other, moved in trade_blocks(down_send):
        down_half = lax.dynamic_update_index_in_dim(down_half, moved, other, 0)

    start, position = doc_positions(doc_lengths, length)
    low = start.reshape(rows, chips, chip_tok)[:, :, 0] // chip_tok
    local = lax.dynamic_slice_in_dim(position, chip * chip_tok, chip_tok, 1).reshape(tokens)
    freq = jnp.power(theta_base, -(jnp.arange(HEAD // 2, dtype=F32) * 2.0) / HEAD)
    angle = local.astype(F32)[:, None] * freq
    cos = jnp.cos(angle)
    sin = jnp.sin(angle)
    cos = jnp.concatenate([cos, cos], axis=1)
    sin = jnp.concatenate([-sin, sin], axis=1)

    inputs = both(layer_input).astype(F32)
    factor_a = lax.rsqrt(jnp.mean(inputs * inputs, axis=-1, keepdims=True) + epsilon)
    normed_a = (inputs * factor_a * attn_norm).astype(BF)
    logits = dot_nt(normed_a, gate_core)
    proj = dot_nt(normed_a, qkv_full)
    q_gain = q_norm[None, :]
    k_gain = k_norm[None, :]

    packed, results, logs, gated, mid = [], [], [], [], []
    for row in range(rows):
        cos_row = cos
        if row:
            cos_row, logits = tie(cos, logits)
        packed.append(exchange(pack_heads(proj, cos_row, sin, q_gain, k_gain, row, chips, chip_tok)))
    packed[-1], ctg_late = tie(packed[-1], ctg)
    ctg_all = gather(ctg_late)
    for row in range(rows):
        head_out, log = attend(packed[row], start[row : row + 1], low[row])
        results.append(head_out)
        logs.append(log)
    tok_results = [exchange(r) for r in results]
    tok_results[0], (gu_half, down_half) = tie(tok_results[0], (gu_half, down_half))
    gu_other = swap(gu_half)
    down_other = swap(down_half)
    for row in range(rows):
        gated.append(gate_rows(tok_results[row], logits, row))
        part = dot_nt(gated[row], out_full, BF).reshape(CORES, tok, width)
        other = swap(pick(part[1], part[0]))
        mid.append(layer_input[row].astype(F32) + pick(part[0], part[1]).astype(F32) + other.astype(F32))
    mid = jnp.concatenate(mid, axis=0)
    gated = jnp.concatenate(gated, axis=0)

    factor_f = lax.rsqrt(jnp.mean(mid * mid, axis=-1, keepdims=True) + epsilon)
    normed_f = (mid * factor_f * ffn_norm).astype(BF)
    normed_all = gather(normed_f)
    gu_recv = jnp.concatenate([pick(gu_half, gu_other), pick(gu_other, gu_half)], axis=0)
    down_full = jnp.concatenate([pick(down_half, down_other), pick(down_other, down_half)], axis=1)
    down_full = down_full.reshape(width, units)
    d_hidden = dot_nn(ctg_all, down_full, BF)
    normed_all, (d_hidden, gu_recv) = tie(normed_all, (d_hidden, gu_recv))
    keep_part = dot_nt(normed_all, gu_keep, BF)
    recv_part = dot_nt(normed_all, gu_recv, BF)
    gate_part = jnp.where(upper, recv_part, keep_part).astype(F32)
    up_part = jnp.where(upper, keep_part, recv_part).astype(F32)
    d_hid = d_hidden.astype(F32)
    gate_act = jax.nn.sigmoid(gate_part)
    silu = gate_part * gate_act
    hidden = (silu * up_part).astype(BF)
    d_gate = d_hid * up_part * gate_act * (1.0 + gate_part * (1.0 - gate_act))
    d_up = d_hid * silu
    d_keep = jnp.where(upper, d_up, d_gate).astype(BF)
    d_recv = jnp.where(upper, d_gate, d_up).astype(BF)
    d_normed = scatter((dot_nn(d_keep, gu_keep) + dot_nn(d_recv, gu_recv)).astype(BF))

    part_keep = dot_tn(d_keep, normed_all, BF)
    part_recv = dot_tn(d_recv, normed_all, BF)
    part_down = dot_tn(ctg_all, hidden, BF).reshape(dp, CORES, out_rows, units)
    keep_swap = swap(pick(part_keep[quarter:], part_keep[:quarter]))
    recv_swap = swap(pick(part_recv[quarter:], part_recv[:quarter]))
    down_swap = swap(pick(part_down[:, 1], part_down[:, 0]))
    d_normed, (part_keep, part_recv, part_down, keep_swap, recv_swap) = tie(
        d_normed, (part_keep, part_recv, part_down, keep_swap, recv_swap)
    )
    keep_sum = pick(part_keep[:quarter], part_keep[quarter:]) + keep_swap
    recv_sum = pick(part_recv[:quarter], part_recv[quarter:]) + recv_swap
    line = Line(chips, chip)
    keep_line = line.begin(keep_sum)
    sent_sum = lax.ppermute(recv_sum, "dp", trade)

    d_normed = d_normed.astype(F32)
    part_ffn = jnp.sum(d_normed * mid * factor_f, axis=0)
    weighted = d_normed * ffn_norm
    inner = jnp.mean(weighted * mid, axis=-1, keepdims=True)
    d_mid = ctg.astype(F32) + factor_f * weighted - mid * factor_f**3 * inner
    low_mine = d_mid.astype(BF).reshape(rows, tok, width)
    low_other = swap(low_mine)
    low_other, down_swap = tie(low_other, down_swap)
    down_sum = pick(part_down[:, 0], part_down[:, 1]) + down_swap
    down_sum = jnp.stack([moved for _, moved in trade_blocks(down_sum)])

    d_mid_low = jnp.concatenate([pick(low_mine, low_other), pick(low_other, low_mine)], axis=1).reshape(tokens, width)
    part_out = dot_tn(d_mid_low, gated, BF)
    out_part = dot_nt(hidden, down_full, BF)
    d_proj, d_logit, d_heads = [], [], []
    q_sum = 0.0
    k_sum = 0.0
    for row in range(rows):
        low_row = d_mid_low[row * chip_tok : (row + 1) * chip_tok]
        if row == 1:
            low_row, (part_out, out_part) = tie(low_row, (part_out, out_part))
        d_gated = dot_nn(low_row, out_full)
        d_attn, dl = gate_back(d_gated, tok_results[row], logits, row)
        d_logit.append(dl)
        d_heads.append(exchange(d_attn))
    shard_out = scatter(part_out)
    out_sum = scatter(out_part)
    d_heads[0], (keep_line, sent_sum) = tie(d_heads[0], (keep_line, sent_sum))
    keep_line = line.next(keep_line)
    sent_line = line.begin(sent_sum)
    back = []
    for row in range(rows):
        back.append(
            exchange(attend_back(packed[row], d_heads[row], results[row], logs[row], start[row : row + 1], low[row]))
        )
    back[0], (keep_line, sent_line, down_sum) = tie(back[0], (keep_line, sent_line, down_sum))
    keep_line = line.next(keep_line)
    sent_line = line.next(sent_line)
    down_line = line.begin(down_sum)
    back[1], (out_sum, shard_out) = tie(back[1], (out_sum, shard_out))
    output = (mid + out_sum.astype(F32)).astype(BF).reshape(rows, tok, width)
    out_line = line.begin(shard_out)
    for row in range(rows):
        dpr, qs, ks = unpack_heads(back[row], proj, cos, sin, q_gain, k_gain, row, chips, chip_tok)
        d_proj.append(dpr)
        q_sum = q_sum + qs
        k_sum = k_sum + ks
    d_proj = jnp.concatenate(d_proj, axis=0)
    d_logit = jnp.concatenate(d_logit, axis=0)
    half = width // 2
    part_qkv = [dot_tn(d_proj, normed_a[:, a : a + half], BF) for a in (0, half)]
    part_qkv[1], (keep_line, sent_line, down_line, out_line) = tie(
        part_qkv[1], (keep_line, sent_line, down_line, out_line)
    )
    shard_qkv = [scatter(p) for p in part_qkv]
    keep_done = line.end(keep_line)
    keep_other = swap(keep_done)
    sent_line = line.next(sent_line)
    down_line = line.next(down_line)
    out_line = line.next(out_line)
    d_norm_part = (dot_nn(d_proj, qkv_full) + dot_nn(d_logit, gate_core)).astype(BF)
    d_norm_part = d_norm_part.reshape(rows, CORES, tok, width)
    d_norm_other = swap(pick(d_norm_part[:, 1], d_norm_part[:, 0]))
    d_norm_other, (sent_line, down_line, out_line) = tie(d_norm_other, (sent_line, down_line, out_line))
    sent_done = line.end(sent_line)
    sent_other = swap(sent_done)
    down_line = line.next(down_line)
    out_line = line.next(out_line)
    d_normed_a = pick(d_norm_part[:, 0], d_norm_part[:, 1]).astype(F32) + d_norm_other.astype(F32)
    own_in = layer_input.astype(F32)
    own_factor = lax.rsqrt(jnp.mean(own_in * own_in, axis=-1, keepdims=True) + epsilon)
    part_attn = jnp.sum(d_normed_a * own_in * own_factor, axis=(0, 1))
    weighted_a = d_normed_a * attn_norm
    inner_a = jnp.mean(weighted_a * own_in, axis=-1, keepdims=True)
    grad_input = (
        d_mid.reshape(rows, tok, width) + own_factor * weighted_a - own_in * own_factor**3 * inner_a
    ).astype(BF)

    part_gate = dot_tn(d_logit, normed_a)[:CORE_Q]
    zero = jnp.zeros_like(part_gate)
    part_gate = jnp.stack(
        [pick(part_gate, zero).reshape(-1, GROUP, width), pick(zero, part_gate).reshape(-1, GROUP, width)], 1
    )
    part_gate = part_gate.reshape(QUERY_HEADS, width)
    heads = jnp.concatenate([jnp.sum(q_sum, axis=0), jnp.sum(k_sum, axis=0)])
    heads = jnp.pad(heads, (0, width - heads.shape[0]))
    early = total_sum(jnp.concatenate([part_gate, part_ffn[None], jnp.zeros((7, width), F32)], axis=0))
    late = total_sum(jnp.stack([part_attn, heads]))
    grad_w_gate = lax.dynamic_slice_in_dim(early, me * gate_count, gate_count, 0)

    shard_qkv[0], down_line, out_line = lax.optimization_barrier((shard_qkv[0], down_line[1:], out_line[1:]))
    qkv_line = line.begin(shard_qkv[0])
    down_done = line.end((2, *down_line))
    out_done = line.end((2, *out_line))
    grad_gu = join_units([keep_done, sent_done], [keep_other, sent_other], core, upper.astype(jnp.int32))
    grad_down = join_blocks(down_done, swap(down_done), core, [unit_block.index(b) ^ me for b in range(dp)])
    grad_out = join_cols([out_done], [swap(out_done)], core, GROUP * HEAD)
    shard_qkv[1], (grad_gu, grad_down, grad_out) = tie(shard_qkv[1], (grad_gu, grad_down, grad_out))
    qkv_sum = [line.end(line.next(line.next(qkv_line))), line.run(shard_qkv[1])]
    grad_qkv = join_rows(qkv_sum, [swap(p) for p in qkv_sum], core, jnp.where(q_shard, GROUP, 1), HEAD)
    return (
        output,
        grad_input,
        late[0],
        late[1, :HEAD],
        late[1, HEAD : 2 * HEAD],
        early[QUERY_HEADS],
        grad_qkv,
        grad_w_gate,
        grad_out,
        grad_gu,
        grad_down,
    )


def solution(mesh):
    token = P("dp", "seq", None)
    shard = P("dp", None)
    in_specs = (token, shard, P(), P(), P(), P(), shard, shard, shard, shard, shard, token)
    out_specs = (token, token, P(), P(), P(), P(), shard, shard, shard, shard, shard)
    return jax.shard_map(shards, mesh=mesh, in_specs=in_specs, out_specs=out_specs, check_vma=False)
```

```python
import functools
import math

import jax
import jax.numpy as jnp
from jax import lax
from jax.experimental import pallas as pl
from jax.experimental.pallas import tpu as pltpu
from jax.sharding import PartitionSpec as P

QUERY_HEADS = 16
KEY_VALUE_HEADS = 8
HEAD = 128
FF = 6144
CORES = 2

GROUP = QUERY_HEADS // KEY_VALUE_HEADS
CORE_Q = QUERY_HEADS // CORES
CORE_KV = KEY_VALUE_HEADS // CORES
epsilon = 1e-06
theta_base = 1000000.0
SCALE = 1.0 / math.sqrt(HEAD)
SCALE2 = SCALE * math.log2(math.e)
BF = jnp.bfloat16
F32 = jnp.float32


def dot_nt(left, right, out=F32):
    return lax.dot_general(left, right, (((1,), (1,)), ((), ())), preferred_element_type=F32).astype(out)


def dot_nn(left, right, out=F32):
    return lax.dot_general(left, right, (((1,), (0,)), ((), ())), preferred_element_type=F32).astype(out)


def dot_tn(left, right, out=F32):
    return lax.dot_general(left, right, (((0,), (0,)), ((), ())), preferred_element_type=F32).astype(out)


def doc_positions(lengths, total):
    ends = jnp.cumsum(lengths, axis=-1)
    starts = ends - lengths
    places = jnp.arange(total, dtype=jnp.int32)
    segment = jnp.sum((places[:, None] >= ends[..., None, :]).astype(jnp.int32), axis=-1)
    owners = segment[..., None] == jnp.arange(lengths.shape[-1], dtype=jnp.int32)
    first = jnp.sum(jnp.where(owners, starts[..., None, :], 0), axis=-1)
    return first, places - first


def pack_kernel(chips, proj_ref, cos_ref, sin_ref, qg_ref, kg_ref, out_ref):
    per = CORE_Q // chips
    copies = max(1, chips // CORE_KV)
    cos = cos_ref[...]
    sin = sin_ref[...]

    def head(index, gain):
        u = proj_ref[:, index * HEAD : (index + 1) * HEAD]
        factor = lax.rsqrt(jnp.mean(u * u, axis=-1, keepdims=True) + epsilon)
        n = u * factor * gain
        return (n * cos + pltpu.roll(n, HEAD // 2, 1) * sin).astype(BF)

    for z in range(chips):
        for h in range(per):
            out_ref[z, :, h * HEAD : (h + 1) * HEAD] = head(z * per + h, qg_ref[...])
        if z % copies == 0:
            kv = z // copies
            key = head(CORE_Q + kv, kg_ref[...])
            base = (CORE_Q + CORE_KV + kv) * HEAD
            value = proj_ref[:, base : base + HEAD].astype(BF)
        out_ref[z, :, per * HEAD : (per + 1) * HEAD] = key
        out_ref[z, :, (per + 1) * HEAD : (per + 2) * HEAD] = value


def pack_heads(proj, cos, sin, q_gain, k_gain, row, chips, chip_tok):
    per = CORE_Q // chips
    lanes = (per + 2) * HEAD
    block = min(256, chip_tok)
    steps = chip_tok // block
    width = proj.shape[1]
    tok = lambda i: (row * steps + i, 0)
    return pl.pallas_call(
        functools.partial(pack_kernel, chips),
        grid=(steps,),
        in_specs=[
            pl.BlockSpec((block, width), tok),
            pl.BlockSpec((block, HEAD), tok),
            pl.BlockSpec((block, HEAD), tok),
            pl.BlockSpec((1, HEAD), lambda i: (0, 0)),
            pl.BlockSpec((1, HEAD), lambda i: (0, 0)),
        ],
        out_specs=pl.BlockSpec((chips, block, lanes), lambda i: (0, i, 0)),
        out_shape=jax.ShapeDtypeStruct((chips, chip_tok, lanes), BF),
        name="pack_heads",
    )(proj, cos, sin, q_gain, k_gain)


def unpack_kernel(chips, grad_ref, proj_ref, cos_ref, sin_ref, qg_ref, kg_ref, out_ref, qs_ref, ks_ref):
    per = CORE_Q // chips
    copies = max(1, chips // CORE_KV)
    cos = cos_ref[...]
    sin = sin_ref[...]

    @pl.when(pl.program_id(0) == 0)
    def _():
        qs_ref[...] = jnp.zeros_like(qs_ref)
        ks_ref[...] = jnp.zeros_like(ks_ref)

    def head(e, index, gain, sum_ref):
        e = e * cos + pltpu.roll(e * sin, HEAD // 2, 1)
        u = proj_ref[:, index * HEAD : (index + 1) * HEAD]
        factor = lax.rsqrt(jnp.mean(u * u, axis=-1, keepdims=True) + epsilon)
        n = u * factor
        sum_ref[...] += jnp.sum((e * n).reshape(-1, 8, HEAD), axis=0)
        weighted = e * gain
        inner = jnp.mean(weighted * n, axis=-1, keepdims=True)
        out_ref[:, index * HEAD : (index + 1) * HEAD] = (factor * (weighted - n * inner)).astype(BF)

    def part(z, lane):
        return grad_ref[z, :, lane * HEAD : (lane + 1) * HEAD].astype(F32)

    for z in range(chips):
        for h in range(per):
            head(part(z, h), z * per + h, qg_ref[...], qs_ref)
    for kv in range(CORE_KV):
        spread = range(kv * copies, (kv + 1) * copies)
        head(sum(part(z, per) for z in spread), CORE_Q + kv, kg_ref[...], ks_ref)
        base = (CORE_Q + CORE_KV + kv) * HEAD
        out_ref[:, base : base + HEAD] = sum(part(z, per + 1) for z in spread).astype(BF)


def unpack_heads(grads, proj, cos, sin, q_gain, k_gain, row, chips, chip_tok):
    lanes = grads.shape[2]
    block = min(256, chip_tok)
    steps = chip_tok // block
    width = proj.shape[1]
    tok = lambda i: (row * steps + i, 0)
    small = pl.BlockSpec((8, HEAD), lambda i: (0, 0))
    return pl.pallas_call(
        functools.partial(unpack_kernel, chips),
        grid=(steps,),
        in_specs=[
            pl.BlockSpec((chips, block, lanes), lambda i: (0, i, 0)),
            pl.BlockSpec((block, width), tok),
            pl.BlockSpec((block, HEAD), tok),
            pl.BlockSpec((block, HEAD), tok),
            pl.BlockSpec((1, HEAD), lambda i: (0, 0)),
            pl.BlockSpec((1, HEAD), lambda i: (0, 0)),
        ],
        out_specs=[pl.BlockSpec((block, width), lambda i: (i, 0)), small, small],
        out_shape=[
            jax.ShapeDtypeStruct((chip_tok, width), BF),
            jax.ShapeDtypeStruct((8, HEAD), F32),
            jax.ShapeDtypeStruct((8, HEAD), F32),
        ],
        name="unpack_heads",
    )(grads, proj, cos, sin, q_gain, k_gain)


def visible(j, size, start, diagonal):
    inner = lax.broadcasted_iota(jnp.int32, (size, size), 0)
    allowed = inner >= start - j * size
    if diagonal:
        allowed = allowed & (inner <= lax.broadcasted_iota(jnp.int32, (size, size), 1))
    return allowed


def attend_kernel(per, low_ref, q_ref, k_ref, v_ref, start_ref, out_ref, log_ref, acc_ref, sum_ref):
    i = pl.program_id(0)
    size = q_ref.shape[1]
    start = start_ref[...]
    acc_ref[...] = jnp.zeros_like(acc_ref)
    sum_ref[...] = jnp.zeros_like(sum_ref)

    def one(j, diagonal):
        key = k_ref[j]
        value = v_ref[j]
        allowed = visible(j, size, start, diagonal)
        for h in range(per):
            scores = dot_nt(key, q_ref[0, :, h * HEAD : (h + 1) * HEAD])
            p = jnp.where(allowed, jnp.exp2(scores * SCALE2), 0.0)
            sum_ref[h : h + 1, :] += jnp.sum(p, axis=0, keepdims=True)
            acc_ref[h] += dot_tn(value, p.astype(BF))

    def step(j, carry):
        one(j, False)
        return carry

    lax.fori_loop(low_ref[i], i, step, 0)
    one(i, True)
    for h in range(per):
        total = sum_ref[h : h + 1, :]
        out_ref[0, :, h * HEAD : (h + 1) * HEAD] = (acc_ref[h] / total).T.astype(BF)
        log_ref[h : h + 1, :] = jnp.log2(total)


def attend(packed, start, low):
    chips, size, lanes = packed.shape
    per = lanes // HEAD - 2
    return pl.pallas_call(
        functools.partial(attend_kernel, per),
        grid_spec=pltpu.PrefetchScalarGridSpec(
            num_scalar_prefetch=1,
            grid=(chips,),
            in_specs=[
                pl.BlockSpec((1, size, per * HEAD), lambda i, low: (i, 0, 0)),
                pl.BlockSpec((chips, size, HEAD), lambda i, low: (0, 0, per)),
                pl.BlockSpec((chips, size, HEAD), lambda i, low: (0, 0, per + 1)),
                pl.BlockSpec((1, size), lambda i, low: (0, i)),
            ],
            out_specs=[
                pl.BlockSpec((1, size, per * HEAD), lambda i, low: (i, 0, 0)),
                pl.BlockSpec((per, size), lambda i, low: (0, i)),
            ],
            scratch_shapes=[pltpu.VMEM((per, HEAD, size), F32), pltpu.VMEM((per, size), F32)],
        ),
        out_shape=[
            jax.ShapeDtypeStruct((chips, size, per * HEAD), BF),
            jax.ShapeDtypeStruct((per, chips * size), F32),
        ],
        name="attend",
    )(low, packed, packed, packed, start)


def attend_back_kernel(
    per, low_ref, q_ref, k_ref, v_ref, grad_ref, res_ref, log_ref, start_ref, out_ref, dq_ref, dk_ref, dv_ref
):
    i = pl.program_id(0)
    size = q_ref.shape[1]
    start = start_ref[...]

    @pl.when(i == 0)
    def _():
        dk_ref[...] = jnp.zeros_like(dk_ref)
        dv_ref[...] = jnp.zeros_like(dv_ref)

    dq_ref[...] = jnp.zeros_like(dq_ref)
    ones = jnp.ones((8, HEAD), F32)
    inner = []
    for h in range(per):
        cols = slice(h * HEAD, (h + 1) * HEAD)
        both = grad_ref[0, :, cols].astype(F32) * res_ref[0, :, cols].astype(F32)
        sums = lax.dot_general(
            ones, both, (((1,), (1,)), ((), ())), precision=lax.Precision.HIGHEST, preferred_element_type=F32
        )
        inner.append(sums[0:1, :])

    def one(j, diagonal):
        key = k_ref[j]
        value = v_ref[j]
        allowed = visible(j, size, start, diagonal)
        for h in range(per):
            query = q_ref[0, :, h * HEAD : (h + 1) * HEAD]
            grad = grad_ref[0, :, h * HEAD : (h + 1) * HEAD]
            scores = dot_nt(key, query)
            p = jnp.where(allowed, jnp.exp2(scores * SCALE2 - log_ref[h : h + 1, :]), 0.0)
            dp = dot_nt(value, grad)
            ds = (p * (dp - inner[h])).astype(BF)
            dv_ref[j] += dot_nn(p.astype(BF), grad)
            dk_ref[j] += dot_nn(ds, query)
            dq_ref[h] += dot_tn(ds, key)

    def step(j, carry):
        one(j, False)
        return carry

    lax.fori_loop(low_ref[i], i, step, 0)
    one(i, True)
    for h in range(per):
        out_ref[i, :, h * HEAD : (h + 1) * HEAD] = (dq_ref[h] * SCALE).astype(BF)

    @pl.when(i == pl.num_programs(0) - 1)
    def _():
        out_ref[:, :, per * HEAD : (per + 1) * HEAD] = (dk_ref[...] * SCALE).astype(BF)
        out_ref[:, :, (per + 1) * HEAD : (per + 2) * HEAD] = dv_ref[...].astype(BF)


def attend_back(packed, grad, result, logs, start, low):
    chips, size, lanes = packed.shape
    per = lanes // HEAD - 2
    one = pl.BlockSpec((1, size, per * HEAD), lambda i, low: (i, 0, 0))
    return pl.pallas_call(
        functools.partial(attend_back_kernel, per),
        grid_spec=pltpu.PrefetchScalarGridSpec(
            num_scalar_prefetch=1,
            grid=(chips,),
            in_specs=[
                one,
                pl.BlockSpec((chips, size, HEAD), lambda i, low: (0, 0, per)),
                pl.BlockSpec((chips, size, HEAD), lambda i, low: (0, 0, per + 1)),
                one,
                one,
                pl.BlockSpec((per, size), lambda i, low: (0, i)),
                pl.BlockSpec((1, size), lambda i, low: (0, i)),
            ],
            out_specs=pl.BlockSpec((chips, size, lanes), lambda i, low: (0, 0, 0)),
            scratch_shapes=[
                pltpu.VMEM((per, size, HEAD), F32),
                pltpu.VMEM((chips, size, HEAD), F32),
                pltpu.VMEM((chips, size, HEAD), F32),
            ],
        ),
        out_shape=jax.ShapeDtypeStruct((chips, size, lanes), BF),
        name="attend_back",
    )(low, packed, packed, packed, grad, result, logs, start)


def gate_kernel(res_ref, logit_ref, out_ref):
    chips, _, lanes = res_ref.shape
    per = lanes // HEAD
    sig = jax.nn.sigmoid(logit_ref[...])
    for z in range(chips):
        for h in range(per):
            head = z * per + h
            value = res_ref[z, :, h * HEAD : (h + 1) * HEAD].astype(F32)
            out_ref[:, head * HEAD : (head + 1) * HEAD] = (value * sig[:, head : head + 1]).astype(BF)


def gate_rows(result, logits, row):
    chips, size, lanes = result.shape
    block = min(256, size)
    steps = size // block
    return pl.pallas_call(
        gate_kernel,
        grid=(steps,),
        in_specs=[
            pl.BlockSpec((chips, block, lanes), lambda i: (0, i, 0)),
            pl.BlockSpec((block, HEAD), lambda i: (row * steps + i, 0)),
        ],
        out_specs=pl.BlockSpec((block, chips * lanes), lambda i: (i, 0)),
        out_shape=jax.ShapeDtypeStruct((size, chips * lanes), BF),
        name="gate_rows",
    )(result, logits)


def gate_back_kernel(grad_ref, res_ref, logit_ref, out_ref, dlogit_ref):
    chips, size, lanes = res_ref.shape
    per = lanes // HEAD
    sig = jax.nn.sigmoid(logit_ref[...])
    lane = lax.broadcasted_iota(jnp.int32, sig.shape, 1)
    sums = jnp.zeros(sig.shape, F32)
    for z in range(chips):
        for h in range(per):
            head = z * per + h
            e = grad_ref[:, head * HEAD : (head + 1) * HEAD]
            value = res_ref[z, :, h * HEAD : (h + 1) * HEAD].astype(F32)
            out_ref[z, :, h * HEAD : (h + 1) * HEAD] = (e * sig[:, head : head + 1]).astype(BF)
            sums = jnp.where(lane == head, jnp.sum(e * value, axis=-1, keepdims=True), sums)
    dlogit_ref[...] = (sums * sig * (1.0 - sig)).astype(BF)


def gate_back(grad, result, logits, row):
    chips, size, lanes = result.shape
    block = min(256, size)
    steps = size // block
    return pl.pallas_call(
        gate_back_kernel,
        grid=(steps,),
        in_specs=[
            pl.BlockSpec((block, chips * lanes), lambda i: (i, 0)),
            pl.BlockSpec((chips, block, lanes), lambda i: (0, i, 0)),
            pl.BlockSpec((block, HEAD), lambda i: (row * steps + i, 0)),
        ],
        out_specs=[
            pl.BlockSpec((chips, block, lanes), lambda i: (0, i, 0)),
            pl.BlockSpec((block, HEAD), lambda i: (i, 0)),
        ],
        out_shape=[jax.ShapeDtypeStruct((chips, size, lanes), BF), jax.ShapeDtypeStruct((size, HEAD), BF)],
        name="gate_back",
    )(grad, result, logits)


def join_rows_kernel(count, which_ref, *refs):
    out_ref = refs[2 * count]
    size = refs[0].shape[1]
    own_half = pl.program_id(0) == which_ref[0]

    def put(parts):
        for k in range(count):
            out_ref[:, k * size : (k + 1) * size] = parts[k][...].astype(F32)

    pl.when(own_half)(lambda: put(refs[:count]))
    pl.when(jnp.logical_not(own_half))(lambda: put(refs[count : 2 * count]))


def join_rows(mine, other, core, blocks, block):
    count = len(mine)
    height, size = mine[0].shape
    steps = height // block

    def source(side):
        def index(h, i, which):
            active = (h == which[0]) if side == 0 else (h != which[0])
            return (jnp.where(active, i, jnp.where(h == 0, 0, steps - 1)), 0)

        return pl.BlockSpec((block, size), index)

    def target(h, i, which):
        per = which[1]
        return ((i // per) * 2 * per + h * per + i % per, 0)

    return pl.pallas_call(
        functools.partial(join_rows_kernel, count),
        grid_spec=pltpu.PrefetchScalarGridSpec(
            num_scalar_prefetch=1,
            grid=(CORES, steps),
            in_specs=[source(0)] * count + [source(1)] * count,
            out_specs=pl.BlockSpec((block, count * size), target),
        ),
        out_shape=jax.ShapeDtypeStruct((CORES * height, count * size), F32),
        name="join_rows",
    )(jnp.stack([core, blocks.astype(jnp.int32)]), *mine, *other)


def join_cols_kernel(count, per, which_ref, *refs):
    out_ref = refs[2 * count]
    u = pl.program_id(0)
    own_half = pl.program_id(1) == which_ref[0]

    def put(ref):
        out_ref[...] = ref[...].astype(F32)

    for k in range(count):
        here = u // per == k
        pl.when(here & own_half)(functools.partial(put, refs[k]))
        pl.when(here & jnp.logical_not(own_half))(functools.partial(put, refs[count + k]))


def join_cols(mine, other, core, unit):
    count = len(mine)
    height, size = mine[0].shape
    per = size // unit

    def source(k):
        return pl.BlockSpec((height, unit), lambda u, h, which: (0, jnp.clip(u - k * per, 0, per - 1)))

    sources = [source(k) for k in range(count)]
    return pl.pallas_call(
        functools.partial(join_cols_kernel, count, per),
        grid_spec=pltpu.PrefetchScalarGridSpec(
            num_scalar_prefetch=1,
            grid=(count * per, CORES),
            in_specs=sources + sources,
            out_specs=pl.BlockSpec((height, unit), lambda u, h, which: (0, u * CORES + h)),
        ),
        out_shape=jax.ShapeDtypeStruct((height, CORES * count * size), F32),
        name="join_cols",
    )(core[None], *mine, *other)


def join_units_kernel(which_ref, keep_ref, keep_other_ref, sent_ref, sent_other_ref, out_ref):
    kept = pl.program_id(0) == which_ref[1]
    mine = pl.program_id(1) == which_ref[0]
    for side, pair in ((True, (keep_ref, keep_other_ref)), (False, (sent_ref, sent_other_ref))):
        for here, ref in ((True, pair[0]), (False, pair[1])):

            @pl.when((kept == side) & (mine == here))
            def _(ref=ref):
                out_ref[...] = ref[...].astype(F32)


def join_units(mine, other, core, upper):
    height, width = mine[0].shape
    block = 256
    steps = height // block
    sources = []
    for side in (0, 1):
        for half in (0, 1):

            def index(p, h, i, which, side=side, half=half):
                at_side = (p == which[1]) if side == 0 else (p != which[1])
                at_half = (h == which[0]) if half == 0 else (h != which[0])
                side_p = which[1] if side == 0 else 1 - which[1]
                side_h = which[0] if half == 0 else 1 - which[0]
                before = (p * 2 + h) < (side_p * 2 + side_h)
                return (jnp.where(at_side & at_half, i, jnp.where(before, 0, steps - 1)), 0)

            sources.append(pl.BlockSpec((block, width), index))
    return pl.pallas_call(
        join_units_kernel,
        grid_spec=pltpu.PrefetchScalarGridSpec(
            num_scalar_prefetch=1,
            grid=(2, CORES, steps),
            in_specs=sources,
            out_specs=pl.BlockSpec((block, width), lambda p, h, i, which: ((p * CORES + h) * steps + i, 0)),
        ),
        out_shape=jax.ShapeDtypeStruct((2 * CORES * height, width), F32),
        name="join_units",
    )(jnp.stack([core, upper]), mine[0], other[0], mine[1], other[1])


def join_blocks_kernel(which_ref, mine_ref, other_ref, out_ref):
    own_half = pl.program_id(0) == which_ref[0]
    for here, ref in ((True, mine_ref), (False, other_ref)):

        @pl.when(own_half == here)
        def _(ref=ref):
            out_ref[...] = ref[0].astype(F32)


def join_blocks(mine, other, core, order):
    count, height, size = mine.shape
    source = pl.BlockSpec((1, height, size), lambda h, b, which, where: (where[b], 0, 0))
    return pl.pallas_call(
        lambda which_ref, where_ref, *refs: join_blocks_kernel(which_ref, *refs),
        grid_spec=pltpu.PrefetchScalarGridSpec(
            num_scalar_prefetch=2,
            grid=(CORES, count),
            in_specs=[source, source],
            out_specs=pl.BlockSpec((height, size), lambda h, b, which, where: (h, b)),
        ),
        out_shape=jax.ShapeDtypeStruct((CORES * height, count * size), F32),
        name="join_blocks",
    )(core[None], jnp.stack(order).astype(jnp.int32), mine, other)


class Line:
    def __init__(self, chips, chip):
        self.chips = chips
        self.inner = (chip == 1) | (chip == 2)
        ends = lambda pairs: [(a * CORES + c, b * CORES + c) for a, b in pairs for c in range(CORES)]
        self.stages = [ends([(0, 1), (3, 2)]), ends([(1, 2), (2, 1)]), ends([(1, 0), (2, 3)])]
        self.groups = [[z * CORES + c for z in range(chips)] for c in range(CORES)]

    def send(self, x, stage):
        if self.chips != 4:
            return (x, lax.psum(x, "seq", axis_index_groups=self.groups) if stage == 0 else x)
        return (x, lax.ppermute(x, "seq", self.stages[stage]))

    def begin(self, x):
        return (0,) + self.send(x, 0)

    def next(self, state):
        stage, x, moved = state
        if self.chips != 4:
            return (stage + 1, moved, moved)
        return (stage + 1,) + self.send(x + moved, stage + 1)

    def end(self, state):
        stage, x, moved = state
        return moved if self.chips != 4 else jnp.where(self.inner, x, moved)

    def pipeline(self, parts):
        if self.chips != 4:
            return lax.psum(parts, "seq", axis_index_groups=self.groups)
        count = len(parts)
        states = [None] * count
        for step in range(count + 2):
            for k in range(count):
                if k == step:
                    states[k] = self.begin(parts[k])
                elif k < step <= k + 2:
                    states[k] = self.next(states[k])
            live = [k for k in range(count) if states[k] is not None]
            later = [k for k in range(step + 1, min(step + 2, count))]
            moved = lax.optimization_barrier([states[k][1:] for k in live] + [parts[k] for k in later])
            for k, value in zip(live + later, moved):
                if k in later:
                    parts[k] = value
                else:
                    states[k] = (states[k][0], *value)
        return [self.end(state) for state in states]


def tie_all(values, work):
    *values, work = lax.optimization_barrier((*values, work))
    return values, work


def tie(value, work):
    leaves, tree = jax.tree.flatten(work)
    moving = [x for x in leaves if not isinstance(x, int)]
    value, *moving = lax.optimization_barrier((value, *moving))
    moving = iter(moving)
    return value, jax.tree.unflatten(tree, [x if isinstance(x, int) else next(moving) for x in leaves])


def shards(
    layer_input,
    doc_lengths,
    attn_norm,
    q_norm,
    k_norm,
    ffn_norm,
    w_qkv,
    w_gate,
    w_out,
    w_gu,
    w_down,
    cotangent,
):
    rows, tok, width = layer_input.shape
    seq = lax.axis_size("seq")
    dp = lax.axis_size("dp")
    chips = seq // CORES
    place = lax.axis_index("seq")
    core = place % CORES
    chip = place // CORES
    first = core == 0
    chip_tok = tok * CORES
    length = tok * seq
    tokens = rows * chip_tok
    pair = [(s, s ^ 1) for s in range(seq)]
    groups = [[z * CORES + c for z in range(chips)] for c in range(CORES)]
    q_shard = lax.axis_index("dp") * w_qkv.shape[0] < QUERY_HEADS * HEAD

    def swap(x):
        return lax.ppermute(x, "seq", pair)

    def pick(a, b):
        return jnp.where(first, a, b)

    def both(x):
        other = swap(x)
        return jnp.concatenate([pick(x, other), pick(other, x)], axis=1).reshape(tokens, width)

    def exchange(x):
        return lax.all_to_all(x, "seq", 0, 0, axis_index_groups=groups, tiled=True)

    def total_sum(x, names=("seq", "dp")):
        for name in names:
            size = lax.axis_size(name)
            step = 1
            while step < size:
                x = x + lax.ppermute(x, name, [(s, s ^ step) for s in range(size)])
                step *= 2
        return x

    def scatter(x):
        return lax.psum_scatter(x, "dp", scatter_dimension=0, tiled=True)

    def gather(x):
        return lax.all_gather(x, "dp", axis=0, tiled=True)

    def core_rows(w, unit):
        return jnp.concatenate(
            [pick(w[a : a + unit], w[a + unit : a + 2 * unit]) for a in range(0, w.shape[0], 2 * unit)], axis=0
        )

    def core_cols(w, unit):
        return jnp.concatenate(
            [pick(w[:, a : a + unit], w[:, a + unit : a + 2 * unit]) for a in range(0, w.shape[1], 2 * unit)],
            axis=1,
        )

    def trade_blocks(x):
        mine = lax.axis_index("dp")
        found = [(mine, lax.dynamic_index_in_dim(x, mine, 0, keepdims=False))]
        for k in range(1, dp):
            out = lax.dynamic_index_in_dim(x, mine ^ k, 0, keepdims=False)
            found.append((mine ^ k, lax.ppermute(out, "dp", [(d, d ^ k) for d in range(dp)])))
        return found

    def halving(x, flip):
        bits = dp.bit_length() - 1
        mine = lax.axis_index("dp")
        x = x.reshape((2,) * bits + (x.shape[0] // dp, x.shape[1]))
        order = list(range(bits))
        gone = []
        for bit in reversed(order) if flip else order:
            axis = sum(1 for b in order if b > bit and b not in gone)
            low, high = lax.index_in_dim(x, 0, axis, False), lax.index_in_dim(x, 1, axis, False)
            mark = (mine >> bit) % 2 == 1
            sent = lax.ppermute(jnp.where(mark, low, high), "dp", [(d, d ^ (1 << bit)) for d in range(dp)])
            x = jnp.where(mark, high, low) + sent
            gone.append(bit)
        return x

    half_dp = dp // 2
    me = lax.axis_index("dp")
    upper = me >= half_dp
    trade = [(d, d ^ half_dp) for d in range(dp)]
    units = w_gu.shape[0] // 2
    owned = rows * tok

    qkv_half = jnp.where(q_shard, core_rows(w_qkv, GROUP * HEAD), core_rows(w_qkv, HEAD))
    qkv_full = gather(qkv_half)
    out_full = gather(core_cols(w_out, GROUP * HEAD))
    ctg = cotangent.reshape(owned, width)
    gate_count = w_gate.shape[0]
    gate_full = lax.dynamic_update_slice_in_dim(jnp.zeros((QUERY_HEADS, width), BF), w_gate, me * gate_count, 0)
    gate_full = total_sum(gate_full, ("dp",))
    gate_core = jnp.pad(core_rows(gate_full, GROUP), ((0, HEAD - CORE_Q), (0, 0)))

    gu_keep = jnp.where(upper, w_gu[units:], w_gu[:units])
    quarter = units // 2
    gu_send = jnp.where(
        upper, pick(w_gu[:quarter], w_gu[quarter:units]), pick(w_gu[units : units + quarter], w_gu[units + quarter :])
    )
    out_rows = w_down.shape[0] // 2
    down_core = pick(w_down[:out_rows], w_down[out_rows:])
    unit_block = [(d % half_dp) * 2 + d // half_dp for d in range(dp)]
    down_send = jnp.stack([down_core[:, b * units : (b + 1) * units] for b in unit_block])
    (qkv_full, gu_send, down_send) = lax.optimization_barrier((qkv_full, gu_send, down_send))
    gu_pair = lax.all_gather(gu_send, "dp", axis_index_groups=[[d, d + half_dp] for d in range(half_dp)])
    gu_half = jnp.where(upper, gu_pair[0], gu_pair[1])
    down_half = jnp.zeros_like(down_send)
    for other, moved in trade_blocks(down_send):
        down_half = lax.dynamic_update_index_in_dim(down_half, moved, other, 0)

    start, position = doc_positions(doc_lengths, length)
    low = start.reshape(rows, chips, chip_tok)[:, :, 0] // chip_tok
    local = lax.dynamic_slice_in_dim(position, chip * chip_tok, chip_tok, 1).reshape(tokens)
    freq = jnp.power(theta_base, -(jnp.arange(HEAD // 2, dtype=F32) * 2.0) / HEAD)
    angle = local.astype(F32)[:, None] * freq
    cos = jnp.cos(angle)
    sin = jnp.sin(angle)
    cos = jnp.concatenate([cos, cos], axis=1)
    sin = jnp.concatenate([-sin, sin], axis=1)

    inputs = both(layer_input).astype(F32)
    factor_a = lax.rsqrt(jnp.mean(inputs * inputs, axis=-1, keepdims=True) + epsilon)
    normed_a = (inputs * factor_a * attn_norm).astype(BF)
    logits = dot_nt(normed_a, gate_core)
    proj = dot_nt(normed_a, qkv_full)
    q_gain = q_norm[None, :]
    k_gain = k_norm[None, :]

    packed, results, logs, gated, mid = [], [], [], [], []
    for row in range(rows):
        cos_row = cos
        if row:
            cos_row, logits = tie(cos, logits)
        packed.append(exchange(pack_heads(proj, cos_row, sin, q_gain, k_gain, row, chips, chip_tok)))
    packed[0], down_half = tie(packed[0], down_half)
    packed[-1], ctg_late = tie(packed[-1], ctg)
    ctg_all = gather(ctg_late)
    for row in range(rows):
        head_out, log = attend(packed[row], start[row : row + 1], low[row])
        results.append(head_out)
        logs.append(log)
    tok_results = [exchange(r) for r in results]
    gu_other = swap(gu_half)
    down_other = swap(down_half)
    for row in range(rows):
        gated.append(gate_rows(tok_results[row], logits, row))
        part = dot_nt(gated[row], out_full, BF).reshape(CORES, tok, width)
        other = swap(pick(part[1], part[0]))
        mid.append(layer_input[row].astype(F32) + pick(part[0], part[1]).astype(F32) + other.astype(F32))
    mid = jnp.concatenate(mid, axis=0)
    gated = jnp.concatenate(gated, axis=0)

    factor_f = lax.rsqrt(jnp.mean(mid * mid, axis=-1, keepdims=True) + epsilon)
    normed_f = (mid * factor_f * ffn_norm).astype(BF)
    normed_all = gather(normed_f)
    gu_recv = jnp.concatenate([pick(gu_half, gu_other), pick(gu_other, gu_half)], axis=0)
    down_full = jnp.concatenate([pick(down_half, down_other), pick(down_other, down_half)], axis=1)
    down_full = down_full.reshape(width, units)
    d_hidden = dot_nn(ctg_all, down_full, BF)
    normed_all, (d_hidden, gu_recv) = tie(normed_all, (d_hidden, gu_recv))
    keep_part = dot_nt(normed_all, gu_keep, BF)
    recv_part = dot_nt(normed_all, gu_recv, BF)
    gate_part = jnp.where(upper, recv_part, keep_part).astype(F32)
    up_part = jnp.where(upper, keep_part, recv_part).astype(F32)
    d_hid = d_hidden.astype(F32)
    gate_act = jax.nn.sigmoid(gate_part)
    silu = gate_part * gate_act
    hidden = (silu * up_part).astype(BF)
    d_gate = d_hid * up_part * gate_act * (1.0 + gate_part * (1.0 - gate_act))
    d_up = d_hid * silu
    d_keep = jnp.where(upper, d_up, d_gate).astype(BF)
    d_recv = jnp.where(upper, d_gate, d_up).astype(BF)
    d_normed = scatter((dot_nn(d_keep, gu_keep) + dot_nn(d_recv, gu_recv)).astype(BF))

    part_keep = dot_tn(d_keep, normed_all, BF)
    part_recv = dot_tn(d_recv, normed_all, BF)
    part_down = dot_tn(ctg_all, hidden, BF).reshape(dp, CORES, out_rows, units)
    keep_swap = swap(pick(part_keep[quarter:], part_keep[:quarter]))
    recv_swap = swap(pick(part_recv[quarter:], part_recv[:quarter]))
    down_swap = swap(pick(part_down[:, 1], part_down[:, 0]))
    d_normed, (part_keep, part_recv, part_down, keep_swap, recv_swap) = tie(
        d_normed, (part_keep, part_recv, part_down, keep_swap, recv_swap)
    )
    keep_sum = pick(part_keep[:quarter], part_keep[quarter:]) + keep_swap
    recv_sum = pick(part_recv[:quarter], part_recv[quarter:]) + recv_swap
    d_normed, gu_sum = tie(d_normed, jnp.concatenate([keep_sum, recv_sum], axis=0))
    gu_sum = lax.psum(gu_sum, "seq", axis_index_groups=groups)

    d_normed = d_normed.astype(F32)
    part_ffn = jnp.sum(d_normed * mid * factor_f, axis=0)
    weighted = d_normed * ffn_norm
    inner = jnp.mean(weighted * mid, axis=-1, keepdims=True)
    d_mid = ctg.astype(F32) + factor_f * weighted - mid * factor_f**3 * inner
    low_mine = d_mid.astype(BF).reshape(rows, tok, width)
    low_other = swap(low_mine)
    low_other, down_swap = tie(low_other, down_swap)
    down_sum = pick(part_down[:, 0], part_down[:, 1]) + down_swap
    down_sum = jnp.stack([moved for _, moved in trade_blocks(down_sum)])

    d_mid_low = jnp.concatenate([pick(low_mine, low_other), pick(low_other, low_mine)], axis=1).reshape(tokens, width)
    part_out = dot_tn(d_mid_low, gated, BF)
    out_part = dot_nt(hidden, down_full, BF)
    d_proj, d_logit, d_heads = [], [], []
    q_sum = 0.0
    k_sum = 0.0
    for row in range(rows):
        low_row = d_mid_low[row * chip_tok : (row + 1) * chip_tok]
        if row == 1:
            low_row, (part_out, out_part) = tie(low_row, (part_out, out_part))
        d_gated = dot_nn(low_row, out_full)
        d_attn, dl = gate_back(d_gated, tok_results[row], logits, row)
        d_logit.append(dl)
        d_heads.append(exchange(d_attn))
    shard_out = scatter(part_out)
    back = []
    for row in range(rows):
        back.append(
            exchange(attend_back(packed[row], d_heads[row], results[row], logs[row], start[row : row + 1], low[row]))
        )
    back[1], (out_part, down_sum) = tie(back[1], (out_part, down_sum))
    cut = width // 2
    out_sum = jnp.concatenate([halving(out_part[:, :cut], False), halving(out_part[:, cut:], True)], axis=1)
    output = (mid + out_sum.astype(F32)).astype(BF).reshape(rows, tok, width)
    for row in range(rows):
        dpr, qs, ks = unpack_heads(back[row], proj, cos, sin, q_gain, k_gain, row, chips, chip_tok)
        d_proj.append(dpr)
        q_sum = q_sum + qs
        k_sum = k_sum + ks
    d_proj = jnp.concatenate(d_proj, axis=0)
    d_logit = jnp.concatenate(d_logit, axis=0)
    half = width // 2
    part_qkv = [dot_tn(d_proj, normed_a[:, a : a + half], BF) for a in (0, half)]
    part_qkv, gu_sum = tie_all(part_qkv, gu_sum)
    shard_qkv = [scatter(p) for p in part_qkv]
    d_norm_part = (dot_nn(d_proj, qkv_full) + dot_nn(d_logit, gate_core)).astype(BF)
    d_norm_part = d_norm_part.reshape(rows, CORES, tok, width)
    d_norm_other = swap(pick(d_norm_part[:, 1], d_norm_part[:, 0]))
    d_normed_a = pick(d_norm_part[:, 0], d_norm_part[:, 1]).astype(F32) + d_norm_other.astype(F32)
    own_in = layer_input.astype(F32)
    own_factor = lax.rsqrt(jnp.mean(own_in * own_in, axis=-1, keepdims=True) + epsilon)
    part_attn = jnp.sum(d_normed_a * own_in * own_factor, axis=(0, 1))
    weighted_a = d_normed_a * attn_norm
    inner_a = jnp.mean(weighted_a * own_in, axis=-1, keepdims=True)
    grad_input = (
        d_mid.reshape(rows, tok, width) + own_factor * weighted_a - own_in * own_factor**3 * inner_a
    ).astype(BF)

    part_gate = dot_tn(d_logit, normed_a)[:CORE_Q]
    zero = jnp.zeros_like(part_gate)
    part_gate = jnp.stack(
        [pick(part_gate, zero).reshape(-1, GROUP, width), pick(zero, part_gate).reshape(-1, GROUP, width)], 1
    )
    part_gate = part_gate.reshape(QUERY_HEADS, width)
    heads = jnp.concatenate([jnp.sum(q_sum, axis=0), jnp.sum(k_sum, axis=0)])
    heads = jnp.pad(heads, (0, width - heads.shape[0]))
    early = total_sum(jnp.concatenate([part_gate, part_ffn[None], jnp.zeros((7, width), F32)], axis=0))
    late = total_sum(jnp.stack([part_attn, heads]))
    grad_w_gate = lax.dynamic_slice_in_dim(early, me * gate_count, gate_count, 0)

    mid_cut = down_sum.shape[1] // 2
    line = Line(chips, chip)
    down_a, down_b, out_done, qkv_a, qkv_b = line.pipeline(
        [down_sum[:, :mid_cut], down_sum[:, mid_cut:], shard_out, *shard_qkv]
    )
    sent = lax.ppermute(gu_sum[quarter:], "dp", trade)
    keep = gu_sum[:quarter]
    down_done = jnp.concatenate([down_a, down_b], axis=1)
    grad_gu = join_units([keep, sent], [swap(keep), swap(sent)], core, upper.astype(jnp.int32))
    grad_down = join_blocks(down_done, swap(down_done), core, [unit_block.index(b) ^ me for b in range(dp)])
    grad_out = join_cols([out_done], [swap(out_done)], core, GROUP * HEAD)
    grad_qkv = join_rows([qkv_a, qkv_b], [swap(qkv_a), swap(qkv_b)], core, jnp.where(q_shard, GROUP, 1), HEAD)
    return (
        output,
        grad_input,
        late[0],
        late[1, :HEAD],
        late[1, HEAD : 2 * HEAD],
        early[QUERY_HEADS],
        grad_qkv,
        grad_w_gate,
        grad_out,
        grad_gu,
        grad_down,
    )


def solution(mesh):
    token = P("dp", "seq", None)
    shard = P("dp", None)
    in_specs = (token, shard, P(), P(), P(), P(), shard, shard, shard, shard, shard, token)
    out_specs = (token, token, P(), P(), P(), P(), shard, shard, shard, shard, shard)
    return jax.shard_map(shards, mesh=mesh, in_specs=in_specs, out_specs=out_specs, check_vma=False)
```

```python
import functools
import math

import jax
import jax.numpy as jnp
from jax import lax
from jax.experimental import pallas as pl
from jax.experimental.pallas import tpu as pltpu
from jax.sharding import PartitionSpec as P

QUERY_HEADS = 16
KEY_VALUE_HEADS = 8
HEAD = 128
FF = 6144
CORES = 2

GROUP = QUERY_HEADS // KEY_VALUE_HEADS
CORE_Q = QUERY_HEADS // CORES
CORE_KV = KEY_VALUE_HEADS // CORES
epsilon = 1e-06
theta_base = 1000000.0
SCALE = 1.0 / math.sqrt(HEAD)
SCALE2 = SCALE * math.log2(math.e)
BF = jnp.bfloat16
F32 = jnp.float32


def dot_nt(left, right, out=F32):
    return lax.dot_general(left, right, (((1,), (1,)), ((), ())), preferred_element_type=F32).astype(out)


def dot_nn(left, right, out=F32):
    return lax.dot_general(left, right, (((1,), (0,)), ((), ())), preferred_element_type=F32).astype(out)


def dot_tn(left, right, out=F32):
    return lax.dot_general(left, right, (((0,), (0,)), ((), ())), preferred_element_type=F32).astype(out)


def doc_positions(lengths, total):
    ends = jnp.cumsum(lengths, axis=-1)
    starts = ends - lengths
    places = jnp.arange(total, dtype=jnp.int32)
    segment = jnp.sum((places[:, None] >= ends[..., None, :]).astype(jnp.int32), axis=-1)
    owners = segment[..., None] == jnp.arange(lengths.shape[-1], dtype=jnp.int32)
    first = jnp.sum(jnp.where(owners, starts[..., None, :], 0), axis=-1)
    return first, places - first


def pack_kernel(chips, proj_ref, cos_ref, sin_ref, qg_ref, kg_ref, out_ref):
    per = CORE_Q // chips
    copies = max(1, chips // CORE_KV)
    cos = cos_ref[...]
    sin = sin_ref[...]

    def head(index, gain):
        u = proj_ref[:, index * HEAD : (index + 1) * HEAD]
        factor = lax.rsqrt(jnp.mean(u * u, axis=-1, keepdims=True) + epsilon)
        n = u * factor * gain
        return (n * cos + pltpu.roll(n, HEAD // 2, 1) * sin).astype(BF)

    for z in range(chips):
        for h in range(per):
            out_ref[z, :, h * HEAD : (h + 1) * HEAD] = head(z * per + h, qg_ref[...])
        if z % copies == 0:
            kv = z // copies
            key = head(CORE_Q + kv, kg_ref[...])
            base = (CORE_Q + CORE_KV + kv) * HEAD
            value = proj_ref[:, base : base + HEAD].astype(BF)
        out_ref[z, :, per * HEAD : (per + 1) * HEAD] = key
        out_ref[z, :, (per + 1) * HEAD : (per + 2) * HEAD] = value


def pack_heads(proj, cos, sin, q_gain, k_gain, row, chips, chip_tok):
    per = CORE_Q // chips
    lanes = (per + 2) * HEAD
    block = min(256, chip_tok)
    steps = chip_tok // block
    width = proj.shape[1]
    tok = lambda i: (row * steps + i, 0)
    return pl.pallas_call(
        functools.partial(pack_kernel, chips),
        grid=(steps,),
        in_specs=[
            pl.BlockSpec((block, width), tok),
            pl.BlockSpec((block, HEAD), tok),
            pl.BlockSpec((block, HEAD), tok),
            pl.BlockSpec((1, HEAD), lambda i: (0, 0)),
            pl.BlockSpec((1, HEAD), lambda i: (0, 0)),
        ],
        out_specs=pl.BlockSpec((chips, block, lanes), lambda i: (0, i, 0)),
        out_shape=jax.ShapeDtypeStruct((chips, chip_tok, lanes), BF),
        name="pack_heads",
    )(proj, cos, sin, q_gain, k_gain)


def unpack_kernel(chips, grad_ref, proj_ref, cos_ref, sin_ref, qg_ref, kg_ref, out_ref, qs_ref, ks_ref):
    per = CORE_Q // chips
    copies = max(1, chips // CORE_KV)
    cos = cos_ref[...]
    sin = sin_ref[...]

    @pl.when(pl.program_id(0) == 0)
    def _():
        qs_ref[...] = jnp.zeros_like(qs_ref)
        ks_ref[...] = jnp.zeros_like(ks_ref)

    def head(e, index, gain, sum_ref):
        e = e * cos + pltpu.roll(e * sin, HEAD // 2, 1)
        u = proj_ref[:, index * HEAD : (index + 1) * HEAD]
        factor = lax.rsqrt(jnp.mean(u * u, axis=-1, keepdims=True) + epsilon)
        n = u * factor
        sum_ref[...] += jnp.sum((e * n).reshape(-1, 8, HEAD), axis=0)
        weighted = e * gain
        inner = jnp.mean(weighted * n, axis=-1, keepdims=True)
        out_ref[:, index * HEAD : (index + 1) * HEAD] = (factor * (weighted - n * inner)).astype(BF)

    def part(z, lane):
        return grad_ref[z, :, lane * HEAD : (lane + 1) * HEAD].astype(F32)

    for z in range(chips):
        for h in range(per):
            head(part(z, h), z * per + h, qg_ref[...], qs_ref)
    for kv in range(CORE_KV):
        spread = range(kv * copies, (kv + 1) * copies)
        head(sum(part(z, per) for z in spread), CORE_Q + kv, kg_ref[...], ks_ref)
        base = (CORE_Q + CORE_KV + kv) * HEAD
        out_ref[:, base : base + HEAD] = sum(part(z, per + 1) for z in spread).astype(BF)


def unpack_heads(grads, proj, cos, sin, q_gain, k_gain, row, chips, chip_tok):
    lanes = grads.shape[2]
    block = min(256, chip_tok)
    steps = chip_tok // block
    width = proj.shape[1]
    tok = lambda i: (row * steps + i, 0)
    small = pl.BlockSpec((8, HEAD), lambda i: (0, 0))
    return pl.pallas_call(
        functools.partial(unpack_kernel, chips),
        grid=(steps,),
        in_specs=[
            pl.BlockSpec((chips, block, lanes), lambda i: (0, i, 0)),
            pl.BlockSpec((block, width), tok),
            pl.BlockSpec((block, HEAD), tok),
            pl.BlockSpec((block, HEAD), tok),
            pl.BlockSpec((1, HEAD), lambda i: (0, 0)),
            pl.BlockSpec((1, HEAD), lambda i: (0, 0)),
        ],
        out_specs=[pl.BlockSpec((block, width), lambda i: (i, 0)), small, small],
        out_shape=[
            jax.ShapeDtypeStruct((chip_tok, width), BF),
            jax.ShapeDtypeStruct((8, HEAD), F32),
            jax.ShapeDtypeStruct((8, HEAD), F32),
        ],
        name="unpack_heads",
    )(grads, proj, cos, sin, q_gain, k_gain)


def visible(j, size, start, diagonal):
    inner = lax.broadcasted_iota(jnp.int32, (size, size), 0)
    allowed = inner >= start - j * size
    if diagonal:
        allowed = allowed & (inner <= lax.broadcasted_iota(jnp.int32, (size, size), 1))
    return allowed


def attend_kernel(per, low_ref, q_ref, k_ref, v_ref, start_ref, out_ref, log_ref, acc_ref, sum_ref):
    i = pl.program_id(0)
    size = q_ref.shape[1]
    start = start_ref[...]
    acc_ref[...] = jnp.zeros_like(acc_ref)
    sum_ref[...] = jnp.zeros_like(sum_ref)

    def one(j, diagonal):
        key = k_ref[j]
        value = v_ref[j]
        allowed = visible(j, size, start, diagonal)
        for h in range(per):
            scores = dot_nt(key, q_ref[0, :, h * HEAD : (h + 1) * HEAD])
            p = jnp.where(allowed, jnp.exp2(scores * SCALE2), 0.0)
            sum_ref[h : h + 1, :] += jnp.sum(p, axis=0, keepdims=True)
            acc_ref[h] += dot_tn(value, p.astype(BF))

    def step(j, carry):
        one(j, False)
        return carry

    lax.fori_loop(low_ref[i], i, step, 0)
    one(i, True)
    for h in range(per):
        total = sum_ref[h : h + 1, :]
        out_ref[0, :, h * HEAD : (h + 1) * HEAD] = (acc_ref[h] / total).T.astype(BF)
        log_ref[h : h + 1, :] = jnp.log2(total)


def attend(packed, start, low):
    chips, size, lanes = packed.shape
    per = lanes // HEAD - 2
    return pl.pallas_call(
        functools.partial(attend_kernel, per),
        grid_spec=pltpu.PrefetchScalarGridSpec(
            num_scalar_prefetch=1,
            grid=(chips,),
            in_specs=[
                pl.BlockSpec((1, size, per * HEAD), lambda i, low: (i, 0, 0)),
                pl.BlockSpec((chips, size, HEAD), lambda i, low: (0, 0, per)),
                pl.BlockSpec((chips, size, HEAD), lambda i, low: (0, 0, per + 1)),
                pl.BlockSpec((1, size), lambda i, low: (0, i)),
            ],
            out_specs=[
                pl.BlockSpec((1, size, per * HEAD), lambda i, low: (i, 0, 0)),
                pl.BlockSpec((per, size), lambda i, low: (0, i)),
            ],
            scratch_shapes=[pltpu.VMEM((per, HEAD, size), F32), pltpu.VMEM((per, size), F32)],
        ),
        out_shape=[
            jax.ShapeDtypeStruct((chips, size, per * HEAD), BF),
            jax.ShapeDtypeStruct((per, chips * size), F32),
        ],
        name="attend",
    )(low, packed, packed, packed, start)


def attend_back_kernel(
    per, low_ref, q_ref, k_ref, v_ref, grad_ref, res_ref, log_ref, start_ref, out_ref, dq_ref, dk_ref, dv_ref
):
    i = pl.program_id(0)
    size = q_ref.shape[1]
    start = start_ref[...]

    @pl.when(i == 0)
    def _():
        dk_ref[...] = jnp.zeros_like(dk_ref)
        dv_ref[...] = jnp.zeros_like(dv_ref)

    dq_ref[...] = jnp.zeros_like(dq_ref)
    ones = jnp.ones((8, HEAD), F32)
    inner = []
    for h in range(per):
        cols = slice(h * HEAD, (h + 1) * HEAD)
        both = grad_ref[0, :, cols].astype(F32) * res_ref[0, :, cols].astype(F32)
        sums = lax.dot_general(
            ones, both, (((1,), (1,)), ((), ())), precision=lax.Precision.HIGHEST, preferred_element_type=F32
        )
        inner.append(sums[0:1, :])

    def one(j, diagonal):
        key = k_ref[j]
        value = v_ref[j]
        allowed = visible(j, size, start, diagonal)
        for h in range(per):
            query = q_ref[0, :, h * HEAD : (h + 1) * HEAD]
            grad = grad_ref[0, :, h * HEAD : (h + 1) * HEAD]
            scores = dot_nt(key, query)
            p = jnp.where(allowed, jnp.exp2(scores * SCALE2 - log_ref[h : h + 1, :]), 0.0)
            dp = dot_nt(value, grad)
            ds = (p * (dp - inner[h])).astype(BF)
            dv_ref[j] += dot_nn(p.astype(BF), grad)
            dk_ref[j] += dot_nn(ds, query)
            dq_ref[h] += dot_tn(ds, key)

    def step(j, carry):
        one(j, False)
        return carry

    lax.fori_loop(low_ref[i], i, step, 0)
    one(i, True)
    for h in range(per):
        out_ref[i, :, h * HEAD : (h + 1) * HEAD] = (dq_ref[h] * SCALE).astype(BF)

    @pl.when(i == pl.num_programs(0) - 1)
    def _():
        out_ref[:, :, per * HEAD : (per + 1) * HEAD] = (dk_ref[...] * SCALE).astype(BF)
        out_ref[:, :, (per + 1) * HEAD : (per + 2) * HEAD] = dv_ref[...].astype(BF)


def attend_back(packed, grad, result, logs, start, low):
    chips, size, lanes = packed.shape
    per = lanes // HEAD - 2
    one = pl.BlockSpec((1, size, per * HEAD), lambda i, low: (i, 0, 0))
    return pl.pallas_call(
        functools.partial(attend_back_kernel, per),
        grid_spec=pltpu.PrefetchScalarGridSpec(
            num_scalar_prefetch=1,
            grid=(chips,),
            in_specs=[
                one,
                pl.BlockSpec((chips, size, HEAD), lambda i, low: (0, 0, per)),
                pl.BlockSpec((chips, size, HEAD), lambda i, low: (0, 0, per + 1)),
                one,
                one,
                pl.BlockSpec((per, size), lambda i, low: (0, i)),
                pl.BlockSpec((1, size), lambda i, low: (0, i)),
            ],
            out_specs=pl.BlockSpec((chips, size, lanes), lambda i, low: (0, 0, 0)),
            scratch_shapes=[
                pltpu.VMEM((per, size, HEAD), F32),
                pltpu.VMEM((chips, size, HEAD), F32),
                pltpu.VMEM((chips, size, HEAD), F32),
            ],
        ),
        out_shape=jax.ShapeDtypeStruct((chips, size, lanes), BF),
        name="attend_back",
    )(low, packed, packed, packed, grad, result, logs, start)


def gate_kernel(res_ref, logit_ref, out_ref):
    chips, _, lanes = res_ref.shape
    per = lanes // HEAD
    sig = jax.nn.sigmoid(logit_ref[...])
    for z in range(chips):
        for h in range(per):
            head = z * per + h
            value = res_ref[z, :, h * HEAD : (h + 1) * HEAD].astype(F32)
            out_ref[:, head * HEAD : (head + 1) * HEAD] = (value * sig[:, head : head + 1]).astype(BF)


def gate_rows(result, logits, row):
    chips, size, lanes = result.shape
    block = min(256, size)
    steps = size // block
    return pl.pallas_call(
        gate_kernel,
        grid=(steps,),
        in_specs=[
            pl.BlockSpec((chips, block, lanes), lambda i: (0, i, 0)),
            pl.BlockSpec((block, HEAD), lambda i: (row * steps + i, 0)),
        ],
        out_specs=pl.BlockSpec((block, chips * lanes), lambda i: (i, 0)),
        out_shape=jax.ShapeDtypeStruct((size, chips * lanes), BF),
        name="gate_rows",
    )(result, logits)


def gate_back_kernel(grad_ref, res_ref, logit_ref, out_ref, dlogit_ref):
    chips, size, lanes = res_ref.shape
    per = lanes // HEAD
    sig = jax.nn.sigmoid(logit_ref[...])
    lane = lax.broadcasted_iota(jnp.int32, sig.shape, 1)
    sums = jnp.zeros(sig.shape, F32)
    for z in range(chips):
        for h in range(per):
            head = z * per + h
            e = grad_ref[:, head * HEAD : (head + 1) * HEAD]
            value = res_ref[z, :, h * HEAD : (h + 1) * HEAD].astype(F32)
            out_ref[z, :, h * HEAD : (h + 1) * HEAD] = (e * sig[:, head : head + 1]).astype(BF)
            sums = jnp.where(lane == head, jnp.sum(e * value, axis=-1, keepdims=True), sums)
    dlogit_ref[...] = (sums * sig * (1.0 - sig)).astype(BF)


def gate_back(grad, result, logits, row):
    chips, size, lanes = result.shape
    block = min(256, size)
    steps = size // block
    return pl.pallas_call(
        gate_back_kernel,
        grid=(steps,),
        in_specs=[
            pl.BlockSpec((block, chips * lanes), lambda i: (i, 0)),
            pl.BlockSpec((chips, block, lanes), lambda i: (0, i, 0)),
            pl.BlockSpec((block, HEAD), lambda i: (row * steps + i, 0)),
        ],
        out_specs=[
            pl.BlockSpec((chips, block, lanes), lambda i: (0, i, 0)),
            pl.BlockSpec((block, HEAD), lambda i: (i, 0)),
        ],
        out_shape=[jax.ShapeDtypeStruct((chips, size, lanes), BF), jax.ShapeDtypeStruct((size, HEAD), BF)],
        name="gate_back",
    )(grad, result, logits)


def join_rows_kernel(count, which_ref, *refs):
    out_ref = refs[2 * count]
    size = refs[0].shape[1]
    own_half = pl.program_id(0) == which_ref[0]

    def put(parts):
        for k in range(count):
            out_ref[:, k * size : (k + 1) * size] = parts[k][...].astype(F32)

    pl.when(own_half)(lambda: put(refs[:count]))
    pl.when(jnp.logical_not(own_half))(lambda: put(refs[count : 2 * count]))


def join_rows(mine, other, core, blocks, block):
    count = len(mine)
    height, size = mine[0].shape
    steps = height // block

    def source(side):
        def index(h, i, which):
            active = (h == which[0]) if side == 0 else (h != which[0])
            return (jnp.where(active, i, jnp.where(h == 0, 0, steps - 1)), 0)

        return pl.BlockSpec((block, size), index)

    def target(h, i, which):
        per = which[1]
        return ((i // per) * 2 * per + h * per + i % per, 0)

    return pl.pallas_call(
        functools.partial(join_rows_kernel, count),
        grid_spec=pltpu.PrefetchScalarGridSpec(
            num_scalar_prefetch=1,
            grid=(CORES, steps),
            in_specs=[source(0)] * count + [source(1)] * count,
            out_specs=pl.BlockSpec((block, count * size), target),
        ),
        out_shape=jax.ShapeDtypeStruct((CORES * height, count * size), F32),
        name="join_rows",
    )(jnp.stack([core, blocks.astype(jnp.int32)]), *mine, *other)


def join_cols_kernel(count, per, which_ref, *refs):
    out_ref = refs[2 * count]
    u = pl.program_id(0)
    own_half = pl.program_id(1) == which_ref[0]

    def put(ref):
        out_ref[...] = ref[...].astype(F32)

    for k in range(count):
        here = u // per == k
        pl.when(here & own_half)(functools.partial(put, refs[k]))
        pl.when(here & jnp.logical_not(own_half))(functools.partial(put, refs[count + k]))


def join_cols(mine, other, core, unit):
    count = len(mine)
    height, size = mine[0].shape
    per = size // unit

    def source(k):
        return pl.BlockSpec((height, unit), lambda u, h, which: (0, jnp.clip(u - k * per, 0, per - 1)))

    sources = [source(k) for k in range(count)]
    return pl.pallas_call(
        functools.partial(join_cols_kernel, count, per),
        grid_spec=pltpu.PrefetchScalarGridSpec(
            num_scalar_prefetch=1,
            grid=(count * per, CORES),
            in_specs=sources + sources,
            out_specs=pl.BlockSpec((height, unit), lambda u, h, which: (0, u * CORES + h)),
        ),
        out_shape=jax.ShapeDtypeStruct((height, CORES * count * size), F32),
        name="join_cols",
    )(core[None], *mine, *other)


def join_units_kernel(which_ref, keep_ref, keep_other_ref, sent_ref, sent_other_ref, out_ref):
    kept = pl.program_id(0) == which_ref[1]
    mine = pl.program_id(1) == which_ref[0]
    for side, pair in ((True, (keep_ref, keep_other_ref)), (False, (sent_ref, sent_other_ref))):
        for here, ref in ((True, pair[0]), (False, pair[1])):

            @pl.when((kept == side) & (mine == here))
            def _(ref=ref):
                out_ref[...] = ref[...].astype(F32)


def join_units(mine, other, core, upper):
    height, width = mine[0].shape
    block = 256
    steps = height // block
    sources = []
    for side in (0, 1):
        for half in (0, 1):

            def index(p, h, i, which, side=side, half=half):
                at_side = (p == which[1]) if side == 0 else (p != which[1])
                at_half = (h == which[0]) if half == 0 else (h != which[0])
                side_p = which[1] if side == 0 else 1 - which[1]
                side_h = which[0] if half == 0 else 1 - which[0]
                before = (p * 2 + h) < (side_p * 2 + side_h)
                return (jnp.where(at_side & at_half, i, jnp.where(before, 0, steps - 1)), 0)

            sources.append(pl.BlockSpec((block, width), index))
    return pl.pallas_call(
        join_units_kernel,
        grid_spec=pltpu.PrefetchScalarGridSpec(
            num_scalar_prefetch=1,
            grid=(2, CORES, steps),
            in_specs=sources,
            out_specs=pl.BlockSpec((block, width), lambda p, h, i, which: ((p * CORES + h) * steps + i, 0)),
        ),
        out_shape=jax.ShapeDtypeStruct((2 * CORES * height, width), F32),
        name="join_units",
    )(jnp.stack([core, upper]), mine[0], other[0], mine[1], other[1])


def join_blocks_kernel(which_ref, mine_ref, other_ref, out_ref):
    own_half = pl.program_id(0) == which_ref[0]
    for here, ref in ((True, mine_ref), (False, other_ref)):

        @pl.when(own_half == here)
        def _(ref=ref):
            out_ref[...] = ref[0].astype(F32)


def join_blocks(mine, other, core, order):
    count, height, size = mine.shape
    source = pl.BlockSpec((1, height, size), lambda h, b, which, where: (where[b], 0, 0))
    return pl.pallas_call(
        lambda which_ref, where_ref, *refs: join_blocks_kernel(which_ref, *refs),
        grid_spec=pltpu.PrefetchScalarGridSpec(
            num_scalar_prefetch=2,
            grid=(CORES, count),
            in_specs=[source, source],
            out_specs=pl.BlockSpec((height, size), lambda h, b, which, where: (h, b)),
        ),
        out_shape=jax.ShapeDtypeStruct((CORES * height, count * size), F32),
        name="join_blocks",
    )(core[None], jnp.stack(order).astype(jnp.int32), mine, other)


class Halving:
    def __init__(self, x, dp, flip):
        self.dp = dp
        self.mine = lax.axis_index("dp")
        bits = dp.bit_length() - 1
        self.left = list(range(bits))
        self.order = self.left[::-1] if flip else self.left[:]
        self.x = x.reshape((2,) * bits + (x.shape[0] // dp, x.shape[1]))

    def send(self):
        bit = self.order.pop(0)
        axis = sum(1 for b in self.left if b > bit)
        self.left.remove(bit)
        low, high = lax.index_in_dim(self.x, 0, axis, False), lax.index_in_dim(self.x, 1, axis, False)
        mark = (self.mine >> bit) % 2 == 1
        pairs = [(d, d ^ (1 << bit)) for d in range(self.dp)]
        self.keep = jnp.where(mark, high, low)
        return lax.ppermute(jnp.where(mark, low, high), "dp", pairs)

    def add(self, moved):
        self.x = self.keep + moved


class Line:
    def __init__(self, chips, chip):
        self.chips = chips
        self.inner = (chip == 1) | (chip == 2)
        ends = lambda pairs: [(a * CORES + c, b * CORES + c) for a, b in pairs for c in range(CORES)]
        self.stages = [ends([(0, 1), (3, 2)]), ends([(1, 2), (2, 1)]), ends([(1, 0), (2, 3)])]
        self.groups = [[z * CORES + c for z in range(chips)] for c in range(CORES)]

    def send(self, x, stage):
        if self.chips != 4:
            return (x, lax.psum(x, "seq", axis_index_groups=self.groups) if stage == 0 else x)
        return (x, lax.ppermute(x, "seq", self.stages[stage]))

    def begin(self, x):
        return (0,) + self.send(x, 0)

    def next(self, state):
        stage, x, moved = state
        if self.chips != 4:
            return (stage + 1, moved, moved)
        return (stage + 1,) + self.send(x + moved, stage + 1)

    def end(self, state):
        stage, x, moved = state
        return moved if self.chips != 4 else jnp.where(self.inner, x, moved)

    def pipeline(self, parts, fillers):
        if self.chips != 4:
            done = lax.psum(parts, "seq", axis_index_groups=self.groups)
            return done, [filler(done) for filler in fillers.values()]
        count = len(parts)
        states = [None] * count
        made = []
        for step in range(count + 2):
            for k in range(count):
                if k == step:
                    states[k] = self.begin(parts[k])
                elif k < step <= k + 2:
                    states[k] = self.next(states[k])
            done = [self.end(states[k]) if k + 3 <= step else None for k in range(count)]
            extra = fillers[step](done) if step in fillers else []
            live = [k for k in range(count) if states[k] is not None]
            later = [k for k in range(step + 1, min(step + 2, count))]
            moved, extra = lax.optimization_barrier(
                ([states[k][1:] for k in live] + [parts[k] for k in later], extra)
            )
            if step in fillers:
                made.append(extra)
            for k, value in zip(live + later, moved):
                if k in later:
                    parts[k] = value
                else:
                    states[k] = (states[k][0], *value)
        return [self.end(state) for state in states], made


def tie_all(values, work):
    *values, work = lax.optimization_barrier((*values, work))
    return values, work


def tie(value, work):
    leaves, tree = jax.tree.flatten(work)
    moving = [x for x in leaves if not isinstance(x, int)]
    value, *moving = lax.optimization_barrier((value, *moving))
    moving = iter(moving)
    return value, jax.tree.unflatten(tree, [x if isinstance(x, int) else next(moving) for x in leaves])


def shards(
    layer_input,
    doc_lengths,
    attn_norm,
    q_norm,
    k_norm,
    ffn_norm,
    w_qkv,
    w_gate,
    w_out,
    w_gu,
    w_down,
    cotangent,
):
    rows, tok, width = layer_input.shape
    seq = lax.axis_size("seq")
    dp = lax.axis_size("dp")
    chips = seq // CORES
    place = lax.axis_index("seq")
    core = place % CORES
    chip = place // CORES
    first = core == 0
    chip_tok = tok * CORES
    length = tok * seq
    tokens = rows * chip_tok
    pair = [(s, s ^ 1) for s in range(seq)]
    groups = [[z * CORES + c for z in range(chips)] for c in range(CORES)]
    q_shard = lax.axis_index("dp") * w_qkv.shape[0] < QUERY_HEADS * HEAD

    def swap(x):
        return lax.ppermute(x, "seq", pair)

    def pick(a, b):
        return jnp.where(first, a, b)

    def both(x):
        other = swap(x)
        return jnp.concatenate([pick(x, other), pick(other, x)], axis=1).reshape(tokens, width)

    def exchange(x):
        return lax.all_to_all(x, "seq", 0, 0, axis_index_groups=groups, tiled=True)

    def total_sum(x, names=("seq", "dp")):
        for name in names:
            size = lax.axis_size(name)
            step = 1
            while step < size:
                x = x + lax.ppermute(x, name, [(s, s ^ step) for s in range(size)])
                step *= 2
        return x

    def scatter(x):
        return lax.psum_scatter(x, "dp", scatter_dimension=0, tiled=True)

    def gather(x):
        return lax.all_gather(x, "dp", axis=0, tiled=True)

    def core_rows(w, unit):
        return jnp.concatenate(
            [pick(w[a : a + unit], w[a + unit : a + 2 * unit]) for a in range(0, w.shape[0], 2 * unit)], axis=0
        )

    def core_cols(w, unit):
        return jnp.concatenate(
            [pick(w[:, a : a + unit], w[:, a + unit : a + 2 * unit]) for a in range(0, w.shape[1], 2 * unit)],
            axis=1,
        )

    def trade_blocks(x):
        mine = lax.axis_index("dp")
        found = [(mine, lax.dynamic_index_in_dim(x, mine, 0, keepdims=False))]
        for k in range(1, dp):
            out = lax.dynamic_index_in_dim(x, mine ^ k, 0, keepdims=False)
            found.append((mine ^ k, lax.ppermute(out, "dp", [(d, d ^ k) for d in range(dp)])))
        return found

    half_dp = dp // 2
    me = lax.axis_index("dp")
    upper = me >= half_dp
    trade = [(d, d ^ half_dp) for d in range(dp)]
    units = w_gu.shape[0] // 2
    owned = rows * tok

    qkv_half = jnp.where(q_shard, core_rows(w_qkv, GROUP * HEAD), core_rows(w_qkv, HEAD))
    qkv_full = gather(qkv_half)
    out_full = gather(core_cols(w_out, GROUP * HEAD))
    ctg = cotangent.reshape(owned, width)
    gate_count = w_gate.shape[0]
    gate_full = lax.dynamic_update_slice_in_dim(jnp.zeros((QUERY_HEADS, width), BF), w_gate, me * gate_count, 0)
    gate_full = total_sum(gate_full, ("dp",))
    gate_core = jnp.pad(core_rows(gate_full, GROUP), ((0, HEAD - CORE_Q), (0, 0)))

    gu_keep = jnp.where(upper, w_gu[units:], w_gu[:units])
    quarter = units // 2
    gu_send = jnp.where(
        upper, pick(w_gu[:quarter], w_gu[quarter:units]), pick(w_gu[units : units + quarter], w_gu[units + quarter :])
    )
    out_rows = w_down.shape[0] // 2
    down_core = pick(w_down[:out_rows], w_down[out_rows:])
    unit_block = [(d % half_dp) * 2 + d // half_dp for d in range(dp)]
    down_send = jnp.stack([down_core[:, b * units : (b + 1) * units] for b in unit_block])
    (qkv_full, gu_send, down_send) = lax.optimization_barrier((qkv_full, gu_send, down_send))
    gu_pair = lax.all_gather(gu_send, "dp", axis_index_groups=[[d, d + half_dp] for d in range(half_dp)])
    gu_half = jnp.where(upper, gu_pair[0], gu_pair[1])
    down_half = jnp.zeros_like(down_send)
    for other, moved in trade_blocks(down_send):
        down_half = lax.dynamic_update_index_in_dim(down_half, moved, other, 0)

    start, position = doc_positions(doc_lengths, length)
    low = start.reshape(rows, chips, chip_tok)[:, :, 0] // chip_tok
    local = lax.dynamic_slice_in_dim(position, chip * chip_tok, chip_tok, 1).reshape(tokens)
    freq = jnp.power(theta_base, -(jnp.arange(HEAD // 2, dtype=F32) * 2.0) / HEAD)
    angle = local.astype(F32)[:, None] * freq
    cos = jnp.cos(angle)
    sin = jnp.sin(angle)
    cos = jnp.concatenate([cos, cos], axis=1)
    sin = jnp.concatenate([-sin, sin], axis=1)

    inputs = both(layer_input).astype(F32)
    factor_a = lax.rsqrt(jnp.mean(inputs * inputs, axis=-1, keepdims=True) + epsilon)
    normed_a = (inputs * factor_a * attn_norm).astype(BF)
    logits = dot_nt(normed_a, gate_core)
    proj = dot_nt(normed_a, qkv_full)
    q_gain = q_norm[None, :]
    k_gain = k_norm[None, :]

    packed, results, logs, gated, mid = [], [], [], [], []
    for row in range(rows):
        cos_row = cos
        if row:
            cos_row, logits = tie(cos, logits)
        packed.append(exchange(pack_heads(proj, cos_row, sin, q_gain, k_gain, row, chips, chip_tok)))
    packed[0], down_half = tie(packed[0], down_half)
    packed[-1], ctg_late = tie(packed[-1], ctg)
    ctg_all = gather(ctg_late)
    for row in range(rows):
        head_out, log = attend(packed[row], start[row : row + 1], low[row])
        results.append(head_out)
        logs.append(log)
    tok_results = [exchange(r) for r in results]
    gu_other = swap(gu_half)
    down_other = swap(down_half)
    for row in range(rows):
        gated.append(gate_rows(tok_results[row], logits, row))
        part = dot_nt(gated[row], out_full, BF).reshape(CORES, tok, width)
        other = swap(pick(part[1], part[0]))
        mid.append(layer_input[row].astype(F32) + pick(part[0], part[1]).astype(F32) + other.astype(F32))
    mid = jnp.concatenate(mid, axis=0)
    gated = jnp.concatenate(gated, axis=0)

    factor_f = lax.rsqrt(jnp.mean(mid * mid, axis=-1, keepdims=True) + epsilon)
    normed_f = (mid * factor_f * ffn_norm).astype(BF)
    normed_all = gather(normed_f)
    gu_recv = jnp.concatenate([pick(gu_half, gu_other), pick(gu_other, gu_half)], axis=0)
    down_full = jnp.concatenate([pick(down_half, down_other), pick(down_other, down_half)], axis=1)
    down_full = down_full.reshape(width, units)
    d_hidden = dot_nn(ctg_all, down_full, BF)
    normed_all, (d_hidden, gu_recv) = tie(normed_all, (d_hidden, gu_recv))
    keep_part = dot_nt(normed_all, gu_keep, BF)
    recv_part = dot_nt(normed_all, gu_recv, BF)
    gate_part = jnp.where(upper, recv_part, keep_part).astype(F32)
    up_part = jnp.where(upper, keep_part, recv_part).astype(F32)
    d_hid = d_hidden.astype(F32)
    gate_act = jax.nn.sigmoid(gate_part)
    silu = gate_part * gate_act
    hidden = (silu * up_part).astype(BF)
    d_gate = d_hid * up_part * gate_act * (1.0 + gate_part * (1.0 - gate_act))
    d_up = d_hid * silu
    d_keep = jnp.where(upper, d_up, d_gate).astype(BF)
    d_recv = jnp.where(upper, d_gate, d_up).astype(BF)
    d_normed = scatter((dot_nn(d_keep, gu_keep) + dot_nn(d_recv, gu_recv)).astype(BF))

    part_keep = dot_tn(d_keep, normed_all, BF)
    part_recv = dot_tn(d_recv, normed_all, BF)
    part_down = dot_tn(ctg_all, hidden, BF).reshape(dp, CORES, out_rows, units)
    keep_swap = swap(pick(part_keep[quarter:], part_keep[:quarter]))
    recv_swap = swap(pick(part_recv[quarter:], part_recv[:quarter]))
    down_swap = swap(pick(part_down[:, 1], part_down[:, 0]))
    d_normed, (part_keep, part_recv, part_down, keep_swap, recv_swap) = tie(
        d_normed, (part_keep, part_recv, part_down, keep_swap, recv_swap)
    )
    keep_sum = pick(part_keep[:quarter], part_keep[quarter:]) + keep_swap
    recv_sum = pick(part_recv[:quarter], part_recv[quarter:]) + recv_swap
    d_normed, (keep_sum, recv_sum) = tie(d_normed, (keep_sum, recv_sum))
    keep = lax.psum(keep_sum, "seq", axis_index_groups=groups)

    d_normed = d_normed.astype(F32)
    part_ffn = jnp.sum(d_normed * mid * factor_f, axis=0)
    weighted = d_normed * ffn_norm
    inner = jnp.mean(weighted * mid, axis=-1, keepdims=True)
    d_mid = ctg.astype(F32) + factor_f * weighted - mid * factor_f**3 * inner
    low_mine = d_mid.astype(BF).reshape(rows, tok, width)
    low_other = swap(low_mine)
    low_other, down_swap = tie(low_other, down_swap)
    down_sum = pick(part_down[:, 0], part_down[:, 1]) + down_swap
    down_sum = jnp.stack([moved for _, moved in trade_blocks(down_sum)])

    d_mid_low = jnp.concatenate([pick(low_mine, low_other), pick(low_other, low_mine)], axis=1).reshape(tokens, width)
    def early_sum(d_logit):
        part_gate = dot_tn(d_logit, normed_a)[:CORE_Q]
        zero = jnp.zeros_like(part_gate)
        part_gate = jnp.stack(
            [pick(part_gate, zero).reshape(-1, GROUP, width), pick(zero, part_gate).reshape(-1, GROUP, width)], 1
        )
        part_gate = part_gate.reshape(QUERY_HEADS, width)
        return total_sum(jnp.concatenate([part_gate, part_ffn[None], jnp.zeros((7, width), F32)], axis=0))

    part_out = dot_tn(d_mid_low, gated, BF)
    out_part = dot_nt(hidden, down_full, BF)
    d_proj, d_logit, d_heads = [], [], []
    q_sum = 0.0
    k_sum = 0.0
    for row in range(rows):
        low_row = d_mid_low[row * chip_tok : (row + 1) * chip_tok]
        if row == 1:
            low_row, (part_out, out_part) = tie(low_row, (part_out, out_part))
        d_gated = dot_nn(low_row, out_full)
        d_attn, dl = gate_back(d_gated, tok_results[row], logits, row)
        d_logit.append(dl)
        d_heads.append(exchange(d_attn))
    back = []
    for row in range(rows):
        grads = attend_back(packed[row], d_heads[row], results[row], logs[row], start[row : row + 1], low[row])
        if row == 0:
            grads, keep = tie(grads, keep)
        back.append(exchange(grads))
    cut = width // 2
    half_out = part_out.shape[1] // 2
    trading = [
        Halving(out_part[:, :cut], dp, False),
        Halving(out_part[:, cut:], dp, True),
        Halving(part_out[:, :half_out], dp, False),
        Halving(part_out[:, half_out:], dp, True),
    ]
    moved = [t.send() for t in trading]
    back[0], (moved, recv_sum) = tie(back[0], (moved, recv_sum))
    recv = lax.psum(recv_sum, "seq", axis_index_groups=groups)
    while trading[0].order:
        for t, m in zip(trading, moved):
            t.add(m)
        moved = [t.send() for t in trading]
    early = early_sum(jnp.concatenate(d_logit, axis=0))
    back[1], (moved, down_sum, early) = tie(back[1], (moved, down_sum, early))
    for t, m in zip(trading, moved):
        t.add(m)
    out_sum = jnp.concatenate([trading[0].x, trading[1].x], axis=1)
    shard_out = jnp.concatenate([trading[2].x, trading[3].x], axis=1)
    output = (mid + out_sum.astype(F32)).astype(BF).reshape(rows, tok, width)
    for row in range(rows):
        dpr, qs, ks = unpack_heads(back[row], proj, cos, sin, q_gain, k_gain, row, chips, chip_tok)
        d_proj.append(dpr)
        q_sum = q_sum + qs
        k_sum = k_sum + ks
    d_proj = jnp.concatenate(d_proj, axis=0)
    d_logit = jnp.concatenate(d_logit, axis=0)
    half = width // 2
    part_qkv = [dot_tn(d_proj, normed_a[:, a : a + half], BF) for a in (0, half)]
    trading = [Halving(p, dp, flip) for p, flip in zip(part_qkv, (False, True))]
    moved = [t.send() for t in trading]
    moved, recv = tie_all(moved, recv)
    while trading[0].order:
        for t, m in zip(trading, moved):
            t.add(m)
        moved = [t.send() for t in trading]
    for t, m in zip(trading, moved):
        t.add(m)
    shard_qkv = [t.x for t in trading]
    d_norm_part = (dot_nn(d_proj, qkv_full) + dot_nn(d_logit, gate_core)).astype(BF)
    d_norm_part = d_norm_part.reshape(rows, CORES, tok, width)
    d_norm_other = swap(pick(d_norm_part[:, 1], d_norm_part[:, 0]))
    d_normed_a = pick(d_norm_part[:, 0], d_norm_part[:, 1]).astype(F32) + d_norm_other.astype(F32)
    own_in = layer_input.astype(F32)
    own_factor = lax.rsqrt(jnp.mean(own_in * own_in, axis=-1, keepdims=True) + epsilon)
    part_attn = jnp.sum(d_normed_a * own_in * own_factor, axis=(0, 1))
    weighted_a = d_normed_a * attn_norm
    inner_a = jnp.mean(weighted_a * own_in, axis=-1, keepdims=True)
    grad_input = (
        d_mid.reshape(rows, tok, width) + own_factor * weighted_a - own_in * own_factor**3 * inner_a
    ).astype(BF)

    heads = jnp.concatenate([jnp.sum(q_sum, axis=0), jnp.sum(k_sum, axis=0)])
    heads = jnp.pad(heads, (0, width - heads.shape[0]))
    late = total_sum(jnp.stack([part_attn, heads]))
    grad_w_gate = lax.dynamic_slice_in_dim(early, me * gate_count, gate_count, 0)

    mid_cut = down_sum.shape[1] // 2
    line = Line(chips, chip)
    sent = lax.ppermute(recv, "dp", trade)

    def join_early(done):
        down_done = jnp.concatenate(done[:2], axis=1)
        places = [unit_block.index(b) ^ me for b in range(dp)]
        return [
            join_units([keep, sent], [swap(keep), swap(sent)], core, upper.astype(jnp.int32)),
            join_blocks(down_done, swap(down_done), core, places),
        ]

    def join_late(done):
        return [join_cols([done[2]], [swap(done[2])], core, GROUP * HEAD)]

    sums, ((grad_gu, grad_down), (grad_out,)) = line.pipeline(
        [down_sum[:, :mid_cut], down_sum[:, mid_cut:], shard_out, *shard_qkv], {5: join_early, 6: join_late}
    )
    qkv_sum = sums[3:]
    grad_qkv = join_rows(qkv_sum, [swap(p) for p in qkv_sum], core, jnp.where(q_shard, GROUP, 1), HEAD)
    return (
        output,
        grad_input,
        late[0],
        late[1, :HEAD],
        late[1, HEAD : 2 * HEAD],
        early[QUERY_HEADS],
        grad_qkv,
        grad_w_gate,
        grad_out,
        grad_gu,
        grad_down,
    )


def solution(mesh):
    token = P("dp", "seq", None)
    shard = P("dp", None)
    in_specs = (token, shard, P(), P(), P(), P(), shard, shard, shard, shard, shard, token)
    out_specs = (token, token, P(), P(), P(), P(), shard, shard, shard, shard, shard)
    return jax.shard_map(shards, mesh=mesh, in_specs=in_specs, out_specs=out_specs, check_vma=False)
```

```python
import functools
import math

import jax
import jax.numpy as jnp
from jax import lax
from jax.experimental import pallas as pl
from jax.experimental.pallas import tpu as pltpu
from jax.sharding import PartitionSpec as P

QUERY_HEADS = 16
KEY_VALUE_HEADS = 8
HEAD = 128
FF = 6144
CORES = 2

GROUP = QUERY_HEADS // KEY_VALUE_HEADS
CORE_Q = QUERY_HEADS // CORES
CORE_KV = KEY_VALUE_HEADS // CORES
epsilon = 1e-06
theta_base = 1000000.0
SCALE = 1.0 / math.sqrt(HEAD)
SCALE2 = SCALE * math.log2(math.e)
BF = jnp.bfloat16
F32 = jnp.float32


def dot_nt(left, right, out=F32):
    return lax.dot_general(left, right, (((1,), (1,)), ((), ())), preferred_element_type=F32).astype(out)


def dot_nn(left, right, out=F32):
    return lax.dot_general(left, right, (((1,), (0,)), ((), ())), preferred_element_type=F32).astype(out)


def dot_tn(left, right, out=F32):
    return lax.dot_general(left, right, (((0,), (0,)), ((), ())), preferred_element_type=F32).astype(out)


def doc_positions(lengths, total):
    ends = jnp.cumsum(lengths, axis=-1)
    starts = ends - lengths
    places = jnp.arange(total, dtype=jnp.int32)
    segment = jnp.sum((places[:, None] >= ends[..., None, :]).astype(jnp.int32), axis=-1)
    owners = segment[..., None] == jnp.arange(lengths.shape[-1], dtype=jnp.int32)
    first = jnp.sum(jnp.where(owners, starts[..., None, :], 0), axis=-1)
    return first, places - first


def pack_kernel(chips, proj_ref, cos_ref, sin_ref, qg_ref, kg_ref, out_ref):
    per = CORE_Q // chips
    copies = max(1, chips // CORE_KV)
    cos = cos_ref[...]
    sin = sin_ref[...]

    def head(index, gain):
        u = proj_ref[:, index * HEAD : (index + 1) * HEAD]
        factor = lax.rsqrt(jnp.mean(u * u, axis=-1, keepdims=True) + epsilon)
        n = u * factor * gain
        return (n * cos + pltpu.roll(n, HEAD // 2, 1) * sin).astype(BF)

    for z in range(chips):
        for h in range(per):
            out_ref[z, :, h * HEAD : (h + 1) * HEAD] = head(z * per + h, qg_ref[...])
        if z % copies == 0:
            kv = z // copies
            key = head(CORE_Q + kv, kg_ref[...])
            base = (CORE_Q + CORE_KV + kv) * HEAD
            value = proj_ref[:, base : base + HEAD].astype(BF)
        out_ref[z, :, per * HEAD : (per + 1) * HEAD] = key
        out_ref[z, :, (per + 1) * HEAD : (per + 2) * HEAD] = value


def pack_heads(proj, cos, sin, q_gain, k_gain, row, chips, chip_tok):
    per = CORE_Q // chips
    lanes = (per + 2) * HEAD
    block = min(256, chip_tok)
    steps = chip_tok // block
    width = proj.shape[1]
    tok = lambda i: (row * steps + i, 0)
    return pl.pallas_call(
        functools.partial(pack_kernel, chips),
        grid=(steps,),
        in_specs=[
            pl.BlockSpec((block, width), tok),
            pl.BlockSpec((block, HEAD), tok),
            pl.BlockSpec((block, HEAD), tok),
            pl.BlockSpec((1, HEAD), lambda i: (0, 0)),
            pl.BlockSpec((1, HEAD), lambda i: (0, 0)),
        ],
        out_specs=pl.BlockSpec((chips, block, lanes), lambda i: (0, i, 0)),
        out_shape=jax.ShapeDtypeStruct((chips, chip_tok, lanes), BF),
        name="pack_heads",
    )(proj, cos, sin, q_gain, k_gain)


def unpack_kernel(chips, grad_ref, proj_ref, cos_ref, sin_ref, qg_ref, kg_ref, out_ref, qs_ref, ks_ref):
    per = CORE_Q // chips
    copies = max(1, chips // CORE_KV)
    cos = cos_ref[...]
    sin = sin_ref[...]

    @pl.when(pl.program_id(0) == 0)
    def _():
        qs_ref[...] = jnp.zeros_like(qs_ref)
        ks_ref[...] = jnp.zeros_like(ks_ref)

    def head(e, index, gain, sum_ref):
        e = e * cos + pltpu.roll(e * sin, HEAD // 2, 1)
        u = proj_ref[:, index * HEAD : (index + 1) * HEAD]
        factor = lax.rsqrt(jnp.mean(u * u, axis=-1, keepdims=True) + epsilon)
        n = u * factor
        sum_ref[...] += jnp.sum((e * n).reshape(-1, 8, HEAD), axis=0)
        weighted = e * gain
        inner = jnp.mean(weighted * n, axis=-1, keepdims=True)
        out_ref[:, index * HEAD : (index + 1) * HEAD] = (factor * (weighted - n * inner)).astype(BF)

    def part(z, lane):
        return grad_ref[z, :, lane * HEAD : (lane + 1) * HEAD].astype(F32)

    for z in range(chips):
        for h in range(per):
            head(part(z, h), z * per + h, qg_ref[...], qs_ref)
    for kv in range(CORE_KV):
        spread = range(kv * copies, (kv + 1) * copies)
        head(sum(part(z, per) for z in spread), CORE_Q + kv, kg_ref[...], ks_ref)
        base = (CORE_Q + CORE_KV + kv) * HEAD
        out_ref[:, base : base + HEAD] = sum(part(z, per + 1) for z in spread).astype(BF)


def unpack_heads(grads, proj, cos, sin, q_gain, k_gain, row, chips, chip_tok):
    lanes = grads.shape[2]
    block = min(256, chip_tok)
    steps = chip_tok // block
    width = proj.shape[1]
    tok = lambda i: (row * steps + i, 0)
    small = pl.BlockSpec((8, HEAD), lambda i: (0, 0))
    return pl.pallas_call(
        functools.partial(unpack_kernel, chips),
        grid=(steps,),
        in_specs=[
            pl.BlockSpec((chips, block, lanes), lambda i: (0, i, 0)),
            pl.BlockSpec((block, width), tok),
            pl.BlockSpec((block, HEAD), tok),
            pl.BlockSpec((block, HEAD), tok),
            pl.BlockSpec((1, HEAD), lambda i: (0, 0)),
            pl.BlockSpec((1, HEAD), lambda i: (0, 0)),
        ],
        out_specs=[pl.BlockSpec((block, width), lambda i: (i, 0)), small, small],
        out_shape=[
            jax.ShapeDtypeStruct((chip_tok, width), BF),
            jax.ShapeDtypeStruct((8, HEAD), F32),
            jax.ShapeDtypeStruct((8, HEAD), F32),
        ],
        name="unpack_heads",
    )(grads, proj, cos, sin, q_gain, k_gain)


def visible(j, size, start, diagonal):
    inner = lax.broadcasted_iota(jnp.int32, (size, size), 0)
    allowed = inner >= start - j * size
    if diagonal:
        allowed = allowed & (inner <= lax.broadcasted_iota(jnp.int32, (size, size), 1))
    return allowed


def attend_kernel(per, low_ref, q_ref, k_ref, v_ref, start_ref, out_ref, log_ref, acc_ref, sum_ref):
    i = pl.program_id(0)
    size = q_ref.shape[1]
    start = start_ref[...]
    acc_ref[...] = jnp.zeros_like(acc_ref)
    sum_ref[...] = jnp.zeros_like(sum_ref)

    def one(j, diagonal):
        key = k_ref[j]
        value = v_ref[j]
        allowed = visible(j, size, start, diagonal)
        for h in range(per):
            scores = dot_nt(key, q_ref[0, :, h * HEAD : (h + 1) * HEAD])
            p = jnp.where(allowed, jnp.exp2(scores * SCALE2), 0.0)
            sum_ref[h : h + 1, :] += jnp.sum(p, axis=0, keepdims=True)
            acc_ref[h] += dot_tn(value, p.astype(BF))

    def step(j, carry):
        one(j, False)
        return carry

    lax.fori_loop(low_ref[i], i, step, 0)
    one(i, True)
    for h in range(per):
        total = sum_ref[h : h + 1, :]
        out_ref[0, :, h * HEAD : (h + 1) * HEAD] = (acc_ref[h] / total).T.astype(BF)
        log_ref[h : h + 1, :] = jnp.log2(total)


def attend(packed, start, low):
    chips, size, lanes = packed.shape
    per = lanes // HEAD - 2
    return pl.pallas_call(
        functools.partial(attend_kernel, per),
        grid_spec=pltpu.PrefetchScalarGridSpec(
            num_scalar_prefetch=1,
            grid=(chips,),
            in_specs=[
                pl.BlockSpec((1, size, per * HEAD), lambda i, low: (i, 0, 0)),
                pl.BlockSpec((chips, size, HEAD), lambda i, low: (0, 0, per)),
                pl.BlockSpec((chips, size, HEAD), lambda i, low: (0, 0, per + 1)),
                pl.BlockSpec((1, size), lambda i, low: (0, i)),
            ],
            out_specs=[
                pl.BlockSpec((1, size, per * HEAD), lambda i, low: (i, 0, 0)),
                pl.BlockSpec((per, size), lambda i, low: (0, i)),
            ],
            scratch_shapes=[pltpu.VMEM((per, HEAD, size), F32), pltpu.VMEM((per, size), F32)],
        ),
        out_shape=[
            jax.ShapeDtypeStruct((chips, size, per * HEAD), BF),
            jax.ShapeDtypeStruct((per, chips * size), F32),
        ],
        name="attend",
    )(low, packed, packed, packed, start)


def attend_back_kernel(
    per, low_ref, q_ref, k_ref, v_ref, grad_ref, res_ref, log_ref, start_ref, out_ref, dq_ref, dk_ref, dv_ref
):
    i = pl.program_id(0)
    size = q_ref.shape[1]
    start = start_ref[...]

    @pl.when(i == 0)
    def _():
        dk_ref[...] = jnp.zeros_like(dk_ref)
        dv_ref[...] = jnp.zeros_like(dv_ref)

    dq_ref[...] = jnp.zeros_like(dq_ref)
    ones = jnp.ones((8, HEAD), F32)
    inner = []
    for h in range(per):
        cols = slice(h * HEAD, (h + 1) * HEAD)
        both = grad_ref[0, :, cols].astype(F32) * res_ref[0, :, cols].astype(F32)
        sums = lax.dot_general(
            ones, both, (((1,), (1,)), ((), ())), precision=lax.Precision.HIGHEST, preferred_element_type=F32
        )
        inner.append(sums[0:1, :])

    def one(j, diagonal):
        key = k_ref[j]
        value = v_ref[j]
        allowed = visible(j, size, start, diagonal)
        for h in range(per):
            query = q_ref[0, :, h * HEAD : (h + 1) * HEAD]
            grad = grad_ref[0, :, h * HEAD : (h + 1) * HEAD]
            scores = dot_nt(key, query)
            p = jnp.where(allowed, jnp.exp2(scores * SCALE2 - log_ref[h : h + 1, :]), 0.0)
            dp = dot_nt(value, grad)
            ds = (p * (dp - inner[h])).astype(BF)
            dv_ref[j] += dot_nn(p.astype(BF), grad)
            dk_ref[j] += dot_nn(ds, query)
            dq_ref[h] += dot_tn(ds, key)

    def step(j, carry):
        one(j, False)
        return carry

    lax.fori_loop(low_ref[i], i, step, 0)
    one(i, True)
    for h in range(per):
        out_ref[i, :, h * HEAD : (h + 1) * HEAD] = (dq_ref[h] * SCALE).astype(BF)

    @pl.when(i == pl.num_programs(0) - 1)
    def _():
        out_ref[:, :, per * HEAD : (per + 1) * HEAD] = (dk_ref[...] * SCALE).astype(BF)
        out_ref[:, :, (per + 1) * HEAD : (per + 2) * HEAD] = dv_ref[...].astype(BF)


def attend_back(packed, grad, result, logs, start, low):
    chips, size, lanes = packed.shape
    per = lanes // HEAD - 2
    one = pl.BlockSpec((1, size, per * HEAD), lambda i, low: (i, 0, 0))
    return pl.pallas_call(
        functools.partial(attend_back_kernel, per),
        grid_spec=pltpu.PrefetchScalarGridSpec(
            num_scalar_prefetch=1,
            grid=(chips,),
            in_specs=[
                one,
                pl.BlockSpec((chips, size, HEAD), lambda i, low: (0, 0, per)),
                pl.BlockSpec((chips, size, HEAD), lambda i, low: (0, 0, per + 1)),
                one,
                one,
                pl.BlockSpec((per, size), lambda i, low: (0, i)),
                pl.BlockSpec((1, size), lambda i, low: (0, i)),
            ],
            out_specs=pl.BlockSpec((chips, size, lanes), lambda i, low: (0, 0, 0)),
            scratch_shapes=[
                pltpu.VMEM((per, size, HEAD), F32),
                pltpu.VMEM((chips, size, HEAD), F32),
                pltpu.VMEM((chips, size, HEAD), F32),
            ],
        ),
        out_shape=jax.ShapeDtypeStruct((chips, size, lanes), BF),
        name="attend_back",
    )(low, packed, packed, packed, grad, result, logs, start)


def gate_kernel(res_ref, logit_ref, out_ref):
    chips, _, lanes = res_ref.shape
    per = lanes // HEAD
    sig = jax.nn.sigmoid(logit_ref[...])
    for z in range(chips):
        for h in range(per):
            head = z * per + h
            value = res_ref[z, :, h * HEAD : (h + 1) * HEAD].astype(F32)
            out_ref[:, head * HEAD : (head + 1) * HEAD] = (value * sig[:, head : head + 1]).astype(BF)


def gate_rows(result, logits, row):
    chips, size, lanes = result.shape
    block = min(256, size)
    steps = size // block
    return pl.pallas_call(
        gate_kernel,
        grid=(steps,),
        in_specs=[
            pl.BlockSpec((chips, block, lanes), lambda i: (0, i, 0)),
            pl.BlockSpec((block, HEAD), lambda i: (row * steps + i, 0)),
        ],
        out_specs=pl.BlockSpec((block, chips * lanes), lambda i: (i, 0)),
        out_shape=jax.ShapeDtypeStruct((size, chips * lanes), BF),
        name="gate_rows",
    )(result, logits)


def gate_back_kernel(grad_ref, res_ref, logit_ref, out_ref, dlogit_ref):
    chips, size, lanes = res_ref.shape
    per = lanes // HEAD
    sig = jax.nn.sigmoid(logit_ref[...])
    lane = lax.broadcasted_iota(jnp.int32, sig.shape, 1)
    sums = jnp.zeros(sig.shape, F32)
    for z in range(chips):
        for h in range(per):
            head = z * per + h
            e = grad_ref[:, head * HEAD : (head + 1) * HEAD]
            value = res_ref[z, :, h * HEAD : (h + 1) * HEAD].astype(F32)
            out_ref[z, :, h * HEAD : (h + 1) * HEAD] = (e * sig[:, head : head + 1]).astype(BF)
            sums = jnp.where(lane == head, jnp.sum(e * value, axis=-1, keepdims=True), sums)
    dlogit_ref[...] = (sums * sig * (1.0 - sig)).astype(BF)


def gate_back(grad, result, logits, row):
    chips, size, lanes = result.shape
    block = min(256, size)
    steps = size // block
    return pl.pallas_call(
        gate_back_kernel,
        grid=(steps,),
        in_specs=[
            pl.BlockSpec((block, chips * lanes), lambda i: (i, 0)),
            pl.BlockSpec((chips, block, lanes), lambda i: (0, i, 0)),
            pl.BlockSpec((block, HEAD), lambda i: (row * steps + i, 0)),
        ],
        out_specs=[
            pl.BlockSpec((chips, block, lanes), lambda i: (0, i, 0)),
            pl.BlockSpec((block, HEAD), lambda i: (i, 0)),
        ],
        out_shape=[jax.ShapeDtypeStruct((chips, size, lanes), BF), jax.ShapeDtypeStruct((size, HEAD), BF)],
        name="gate_back",
    )(grad, result, logits)


def join_rows_kernel(count, which_ref, *refs):
    out_ref = refs[2 * count]
    size = refs[0].shape[1]
    own_half = pl.program_id(0) == which_ref[0]

    def put(parts):
        for k in range(count):
            out_ref[:, k * size : (k + 1) * size] = parts[k][...].astype(F32)

    pl.when(own_half)(lambda: put(refs[:count]))
    pl.when(jnp.logical_not(own_half))(lambda: put(refs[count : 2 * count]))


def join_rows(mine, other, core, blocks, block):
    count = len(mine)
    height, size = mine[0].shape
    steps = height // block

    def source(side):
        def index(h, i, which):
            active = (h == which[0]) if side == 0 else (h != which[0])
            return (jnp.where(active, i, jnp.where(h == 0, 0, steps - 1)), 0)

        return pl.BlockSpec((block, size), index)

    def target(h, i, which):
        per = which[1]
        return ((i // per) * 2 * per + h * per + i % per, 0)

    return pl.pallas_call(
        functools.partial(join_rows_kernel, count),
        grid_spec=pltpu.PrefetchScalarGridSpec(
            num_scalar_prefetch=1,
            grid=(CORES, steps),
            in_specs=[source(0)] * count + [source(1)] * count,
            out_specs=pl.BlockSpec((block, count * size), target),
        ),
        out_shape=jax.ShapeDtypeStruct((CORES * height, count * size), F32),
        name="join_rows",
    )(jnp.stack([core, blocks.astype(jnp.int32)]), *mine, *other)


def join_cols_kernel(count, per, which_ref, *refs):
    out_ref = refs[2 * count]
    u = pl.program_id(0)
    own_half = pl.program_id(1) == which_ref[0]

    def put(ref):
        out_ref[...] = ref[...].astype(F32)

    for k in range(count):
        here = u // per == k
        pl.when(here & own_half)(functools.partial(put, refs[k]))
        pl.when(here & jnp.logical_not(own_half))(functools.partial(put, refs[count + k]))


def join_cols(mine, other, core, unit):
    count = len(mine)
    height, size = mine[0].shape
    per = size // unit

    def source(k):
        return pl.BlockSpec((height, unit), lambda u, h, which: (0, jnp.clip(u - k * per, 0, per - 1)))

    sources = [source(k) for k in range(count)]
    return pl.pallas_call(
        functools.partial(join_cols_kernel, count, per),
        grid_spec=pltpu.PrefetchScalarGridSpec(
            num_scalar_prefetch=1,
            grid=(count * per, CORES),
            in_specs=sources + sources,
            out_specs=pl.BlockSpec((height, unit), lambda u, h, which: (0, u * CORES + h)),
        ),
        out_shape=jax.ShapeDtypeStruct((height, CORES * count * size), F32),
        name="join_cols",
    )(core[None], *mine, *other)


def join_units_kernel(which_ref, keep_ref, keep_other_ref, sent_ref, sent_other_ref, out_ref):
    kept = pl.program_id(0) == which_ref[1]
    mine = pl.program_id(1) == which_ref[0]
    for side, pair in ((True, (keep_ref, keep_other_ref)), (False, (sent_ref, sent_other_ref))):
        for here, ref in ((True, pair[0]), (False, pair[1])):

            @pl.when((kept == side) & (mine == here))
            def _(ref=ref):
                out_ref[...] = ref[...].astype(F32)


def join_units(mine, other, core, upper):
    height, width = mine[0].shape
    block = 256
    steps = height // block
    sources = []
    for side in (0, 1):
        for half in (0, 1):

            def index(p, h, i, which, side=side, half=half):
                at_side = (p == which[1]) if side == 0 else (p != which[1])
                at_half = (h == which[0]) if half == 0 else (h != which[0])
                side_p = which[1] if side == 0 else 1 - which[1]
                side_h = which[0] if half == 0 else 1 - which[0]
                before = (p * 2 + h) < (side_p * 2 + side_h)
                return (jnp.where(at_side & at_half, i, jnp.where(before, 0, steps - 1)), 0)

            sources.append(pl.BlockSpec((block, width), index))
    return pl.pallas_call(
        join_units_kernel,
        grid_spec=pltpu.PrefetchScalarGridSpec(
            num_scalar_prefetch=1,
            grid=(2, CORES, steps),
            in_specs=sources,
            out_specs=pl.BlockSpec((block, width), lambda p, h, i, which: ((p * CORES + h) * steps + i, 0)),
        ),
        out_shape=jax.ShapeDtypeStruct((2 * CORES * height, width), F32),
        name="join_units",
    )(jnp.stack([core, upper]), mine[0], other[0], mine[1], other[1])


def join_blocks_kernel(which_ref, mine_ref, other_ref, out_ref):
    own_half = pl.program_id(0) == which_ref[0]
    for here, ref in ((True, mine_ref), (False, other_ref)):

        @pl.when(own_half == here)
        def _(ref=ref):
            out_ref[...] = ref[0].astype(F32)


def join_blocks(mine, other, core, order):
    count, height, size = mine.shape
    source = pl.BlockSpec((1, height, size), lambda h, b, which, where: (where[b], 0, 0))
    return pl.pallas_call(
        lambda which_ref, where_ref, *refs: join_blocks_kernel(which_ref, *refs),
        grid_spec=pltpu.PrefetchScalarGridSpec(
            num_scalar_prefetch=2,
            grid=(CORES, count),
            in_specs=[source, source],
            out_specs=pl.BlockSpec((height, size), lambda h, b, which, where: (h, b)),
        ),
        out_shape=jax.ShapeDtypeStruct((CORES * height, count * size), F32),
        name="join_blocks",
    )(core[None], jnp.stack(order).astype(jnp.int32), mine, other)


class Halving:
    def __init__(self, x, dp, flip):
        self.dp = dp
        self.mine = lax.axis_index("dp")
        bits = dp.bit_length() - 1
        self.left = list(range(bits))
        self.order = self.left[::-1] if flip else self.left[:]
        self.x = x.reshape((2,) * bits + (x.shape[0] // dp, x.shape[1]))

    def send(self):
        bit = self.order.pop(0)
        axis = sum(1 for b in self.left if b > bit)
        self.left.remove(bit)
        low, high = lax.index_in_dim(self.x, 0, axis, False), lax.index_in_dim(self.x, 1, axis, False)
        mark = (self.mine >> bit) % 2 == 1
        pairs = [(d, d ^ (1 << bit)) for d in range(self.dp)]
        self.keep = jnp.where(mark, high, low)
        return lax.ppermute(jnp.where(mark, low, high), "dp", pairs)

    def add(self, moved):
        self.x = self.keep + moved


class Line:
    def __init__(self, chips, chip):
        self.chips = chips
        self.inner = (chip == 1) | (chip == 2)
        ends = lambda pairs: [(a * CORES + c, b * CORES + c) for a, b in pairs for c in range(CORES)]
        self.stages = [ends([(0, 1), (3, 2)]), ends([(1, 2), (2, 1)]), ends([(1, 0), (2, 3)])]
        self.groups = [[z * CORES + c for z in range(chips)] for c in range(CORES)]

    def send(self, x, stage):
        if self.chips != 4:
            return (x, lax.psum(x, "seq", axis_index_groups=self.groups) if stage == 0 else x)
        return (x, lax.ppermute(x, "seq", self.stages[stage]))

    def begin(self, x):
        return (0,) + self.send(x, 0)

    def next(self, state):
        stage, x, moved = state
        if self.chips != 4:
            return (stage + 1, moved, moved)
        return (stage + 1,) + self.send(x + moved, stage + 1)

    def end(self, state):
        stage, x, moved = state
        return moved if self.chips != 4 else jnp.where(self.inner, x, moved)

    def pipeline(self, parts, fillers):
        if self.chips != 4:
            done = lax.psum(parts, "seq", axis_index_groups=self.groups)
            return done, [filler(done) for filler in fillers.values()]
        count = len(parts)
        states = [None] * count
        made = []
        for step in range(count + 2):
            for k in range(count):
                if k == step:
                    states[k] = self.begin(parts[k])
                elif k < step <= k + 2:
                    states[k] = self.next(states[k])
            done = [self.end(states[k]) if k + 3 <= step else None for k in range(count)]
            extra = fillers[step](done) if step in fillers else []
            live = [k for k in range(count) if states[k] is not None]
            later = [k for k in range(step + 1, min(step + 2, count))]
            moved, extra = lax.optimization_barrier(
                ([states[k][1:] for k in live] + [parts[k] for k in later], extra)
            )
            if step in fillers:
                made.append(extra)
            for k, value in zip(live + later, moved):
                if k in later:
                    parts[k] = value
                else:
                    states[k] = (states[k][0], *value)
        return [self.end(state) for state in states], made


def tie_all(values, work):
    *values, work = lax.optimization_barrier((*values, work))
    return values, work


def tie(value, work):
    leaves, tree = jax.tree.flatten(work)
    moving = [x for x in leaves if not isinstance(x, int)]
    value, *moving = lax.optimization_barrier((value, *moving))
    moving = iter(moving)
    return value, jax.tree.unflatten(tree, [x if isinstance(x, int) else next(moving) for x in leaves])


def shards(
    layer_input,
    doc_lengths,
    attn_norm,
    q_norm,
    k_norm,
    ffn_norm,
    w_qkv,
    w_gate,
    w_out,
    w_gu,
    w_down,
    cotangent,
):
    rows, tok, width = layer_input.shape
    seq = lax.axis_size("seq")
    dp = lax.axis_size("dp")
    chips = seq // CORES
    place = lax.axis_index("seq")
    core = place % CORES
    chip = place // CORES
    first = core == 0
    chip_tok = tok * CORES
    length = tok * seq
    tokens = rows * chip_tok
    pair = [(s, s ^ 1) for s in range(seq)]
    groups = [[z * CORES + c for z in range(chips)] for c in range(CORES)]
    q_shard = lax.axis_index("dp") * w_qkv.shape[0] < QUERY_HEADS * HEAD

    def swap(x):
        return lax.ppermute(x, "seq", pair)

    def pick(a, b):
        return jnp.where(first, a, b)

    def both(x):
        other = swap(x)
        return jnp.concatenate([pick(x, other), pick(other, x)], axis=1).reshape(tokens, width)

    def exchange(x):
        return lax.all_to_all(x, "seq", 0, 0, axis_index_groups=groups, tiled=True)

    def total_sum(x, names=("seq", "dp")):
        for name in names:
            size = lax.axis_size(name)
            step = 1
            while step < size:
                x = x + lax.ppermute(x, name, [(s, s ^ step) for s in range(size)])
                step *= 2
        return x

    def scatter(x):
        return lax.psum_scatter(x, "dp", scatter_dimension=0, tiled=True)

    def gather(x):
        return lax.all_gather(x, "dp", axis=0, tiled=True)

    def core_rows(w, unit):
        return jnp.concatenate(
            [pick(w[a : a + unit], w[a + unit : a + 2 * unit]) for a in range(0, w.shape[0], 2 * unit)], axis=0
        )

    def core_cols(w, unit):
        return jnp.concatenate(
            [pick(w[:, a : a + unit], w[:, a + unit : a + 2 * unit]) for a in range(0, w.shape[1], 2 * unit)],
            axis=1,
        )

    def trade_blocks(x):
        mine = lax.axis_index("dp")
        found = [(mine, lax.dynamic_index_in_dim(x, mine, 0, keepdims=False))]
        for k in range(1, dp):
            out = lax.dynamic_index_in_dim(x, mine ^ k, 0, keepdims=False)
            found.append((mine ^ k, lax.ppermute(out, "dp", [(d, d ^ k) for d in range(dp)])))
        return found

    half_dp = dp // 2
    me = lax.axis_index("dp")
    upper = me >= half_dp
    trade = [(d, d ^ half_dp) for d in range(dp)]
    units = w_gu.shape[0] // 2
    owned = rows * tok

    qkv_half = jnp.where(q_shard, core_rows(w_qkv, GROUP * HEAD), core_rows(w_qkv, HEAD))
    qkv_full = gather(qkv_half)
    out_full = gather(core_cols(w_out, GROUP * HEAD))
    ctg = cotangent.reshape(owned, width)
    gate_count = w_gate.shape[0]
    gate_full = lax.dynamic_update_slice_in_dim(jnp.zeros((QUERY_HEADS, width), BF), w_gate, me * gate_count, 0)
    gate_full = total_sum(gate_full, ("dp",))
    gate_core = jnp.pad(core_rows(gate_full, GROUP), ((0, HEAD - CORE_Q), (0, 0)))

    gu_keep = jnp.where(upper, w_gu[units:], w_gu[:units])
    quarter = units // 2
    gu_send = jnp.where(
        upper, pick(w_gu[:quarter], w_gu[quarter:units]), pick(w_gu[units : units + quarter], w_gu[units + quarter :])
    )
    out_rows = w_down.shape[0] // 2
    down_core = pick(w_down[:out_rows], w_down[out_rows:])
    unit_block = [(d % half_dp) * 2 + d // half_dp for d in range(dp)]
    down_send = jnp.stack([down_core[:, b * units : (b + 1) * units] for b in unit_block])
    (qkv_full, gu_send, down_send) = lax.optimization_barrier((qkv_full, gu_send, down_send))
    gu_pair = lax.all_gather(gu_send, "dp", axis_index_groups=[[d, d + half_dp] for d in range(half_dp)])
    gu_half = jnp.where(upper, gu_pair[0], gu_pair[1])
    down_half = jnp.zeros_like(down_send)
    for other, moved in trade_blocks(down_send):
        down_half = lax.dynamic_update_index_in_dim(down_half, moved, other, 0)

    start, position = doc_positions(doc_lengths, length)
    low = start.reshape(rows, chips, chip_tok)[:, :, 0] // chip_tok
    local = lax.dynamic_slice_in_dim(position, chip * chip_tok, chip_tok, 1).reshape(tokens)
    freq = jnp.power(theta_base, -(jnp.arange(HEAD // 2, dtype=F32) * 2.0) / HEAD)
    angle = local.astype(F32)[:, None] * freq
    cos = jnp.cos(angle)
    sin = jnp.sin(angle)
    cos = jnp.concatenate([cos, cos], axis=1)
    sin = jnp.concatenate([-sin, sin], axis=1)

    inputs = both(layer_input).astype(F32)
    factor_a = lax.rsqrt(jnp.mean(inputs * inputs, axis=-1, keepdims=True) + epsilon)
    normed_a = (inputs * factor_a * attn_norm).astype(BF)
    logits = dot_nt(normed_a, gate_core)
    proj = dot_nt(normed_a, qkv_full)
    q_gain = q_norm[None, :]
    k_gain = k_norm[None, :]

    packed, results, logs, gated, mid = [], [], [], [], []
    for row in range(rows):
        cos_row = cos
        if row:
            cos_row, logits = tie(cos, logits)
        packed.append(exchange(pack_heads(proj, cos_row, sin, q_gain, k_gain, row, chips, chip_tok)))
    packed[0], down_half = tie(packed[0], down_half)
    packed[-1], ctg_late = tie(packed[-1], ctg)
    ctg_all = gather(ctg_late)
    for row in range(rows):
        head_out, log = attend(packed[row], start[row : row + 1], low[row])
        results.append(head_out)
        logs.append(log)
    tok_results = [exchange(r) for r in results]
    gu_other = swap(gu_half)
    down_other = swap(down_half)
    for row in range(rows):
        gated.append(gate_rows(tok_results[row], logits, row))
        part = dot_nt(gated[row], out_full, BF).reshape(CORES, tok, width)
        other = swap(pick(part[1], part[0]))
        mid.append(layer_input[row].astype(F32) + pick(part[0], part[1]).astype(F32) + other.astype(F32))
    mid = jnp.concatenate(mid, axis=0)
    gated = jnp.concatenate(gated, axis=0)

    factor_f = lax.rsqrt(jnp.mean(mid * mid, axis=-1, keepdims=True) + epsilon)
    normed_f = (mid * factor_f * ffn_norm).astype(BF)
    normed_all = gather(normed_f)
    gu_recv = jnp.concatenate([pick(gu_half, gu_other), pick(gu_other, gu_half)], axis=0)
    down_full = jnp.concatenate([pick(down_half, down_other), pick(down_other, down_half)], axis=1)
    down_full = down_full.reshape(width, units)
    d_hidden = dot_nn(ctg_all, down_full, BF)
    normed_all, (d_hidden, gu_recv) = tie(normed_all, (d_hidden, gu_recv))
    keep_part = dot_nt(normed_all, gu_keep, BF)
    recv_part = dot_nt(normed_all, gu_recv, BF)
    gate_part = jnp.where(upper, recv_part, keep_part).astype(F32)
    up_part = jnp.where(upper, keep_part, recv_part).astype(F32)
    d_hid = d_hidden.astype(F32)
    gate_act = jax.nn.sigmoid(gate_part)
    silu = gate_part * gate_act
    hidden = (silu * up_part).astype(BF)
    d_gate = d_hid * up_part * gate_act * (1.0 + gate_part * (1.0 - gate_act))
    d_up = d_hid * silu
    d_keep = jnp.where(upper, d_up, d_gate).astype(BF)
    d_recv = jnp.where(upper, d_gate, d_up).astype(BF)
    d_normed = scatter((dot_nn(d_keep, gu_keep) + dot_nn(d_recv, gu_recv)).astype(BF))

    part_keep = dot_tn(d_keep, normed_all, BF)
    part_recv = dot_tn(d_recv, normed_all, BF)
    part_down = dot_tn(ctg_all, hidden, BF).reshape(dp, CORES, out_rows, units)
    keep_swap = swap(pick(part_keep[quarter:], part_keep[:quarter]))
    recv_swap = swap(pick(part_recv[quarter:], part_recv[:quarter]))
    down_swap = swap(pick(part_down[:, 1], part_down[:, 0]))
    d_normed, (part_keep, part_recv, part_down, keep_swap, recv_swap) = tie(
        d_normed, (part_keep, part_recv, part_down, keep_swap, recv_swap)
    )
    keep_sum = pick(part_keep[:quarter], part_keep[quarter:]) + keep_swap
    recv_sum = pick(part_recv[:quarter], part_recv[quarter:]) + recv_swap
    d_normed, (keep_sum, recv_sum) = tie(d_normed, (keep_sum, recv_sum))
    keep = lax.psum(keep_sum, "seq", axis_index_groups=groups)

    d_normed = d_normed.astype(F32)
    part_ffn = jnp.sum(d_normed * mid * factor_f, axis=0)
    weighted = d_normed * ffn_norm
    inner = jnp.mean(weighted * mid, axis=-1, keepdims=True)
    d_mid = ctg.astype(F32) + factor_f * weighted - mid * factor_f**3 * inner
    low_mine = d_mid.astype(BF).reshape(rows, tok, width)
    low_other = swap(low_mine)
    low_other, down_swap = tie(low_other, down_swap)
    down_sum = pick(part_down[:, 0], part_down[:, 1]) + down_swap
    down_sum = jnp.stack([moved for _, moved in trade_blocks(down_sum)])

    d_mid_low = jnp.concatenate([pick(low_mine, low_other), pick(low_other, low_mine)], axis=1).reshape(tokens, width)
    def early_sum(d_logit):
        part_gate = dot_tn(d_logit, normed_a)[:CORE_Q]
        zero = jnp.zeros_like(part_gate)
        part_gate = jnp.stack(
            [pick(part_gate, zero).reshape(-1, GROUP, width), pick(zero, part_gate).reshape(-1, GROUP, width)], 1
        )
        part_gate = part_gate.reshape(QUERY_HEADS, width)
        return total_sum(jnp.concatenate([part_gate, part_ffn[None], jnp.zeros((7, width), F32)], axis=0))

    part_out = dot_tn(d_mid_low, gated, BF)
    d_proj, d_logit, d_heads = [], [], []
    q_sum = 0.0
    k_sum = 0.0
    for row in range(rows):
        low_row = d_mid_low[row * chip_tok : (row + 1) * chip_tok]
        if row == 1:
            out_part = dot_nt(hidden, down_full, BF)
            low_row, (part_out, out_part) = tie(low_row, (part_out, out_part))
        d_gated = dot_nn(low_row, out_full)
        d_attn, dl = gate_back(d_gated, tok_results[row], logits, row)
        if row == 0:
            d_attn, hidden = tie(d_attn, hidden)
        d_logit.append(dl)
        d_heads.append(exchange(d_attn))
    back = []
    for row in range(rows):
        grads = attend_back(packed[row], d_heads[row], results[row], logs[row], start[row : row + 1], low[row])
        if row == 0:
            grads, (keep, recv_sum) = tie(grads, (keep, recv_sum))
            recv = lax.psum(recv_sum, "seq", axis_index_groups=groups)
        back.append(exchange(grads))
    cut = width // 2
    half_out = part_out.shape[1] // 2
    trading = [
        Halving(out_part[:, :cut], dp, False),
        Halving(out_part[:, cut:], dp, True),
        Halving(part_out[:, :half_out], dp, False),
        Halving(part_out[:, half_out:], dp, True),
    ]
    moved = [t.send() for t in trading]
    back[0], moved = tie(back[0], moved)
    while trading[0].order:
        for t, m in zip(trading, moved):
            t.add(m)
        moved = [t.send() for t in trading]
    early = early_sum(jnp.concatenate(d_logit, axis=0))
    back[1], (moved, down_sum, early) = tie(back[1], (moved, down_sum, early))
    for t, m in zip(trading, moved):
        t.add(m)
    out_sum = jnp.concatenate([trading[0].x, trading[1].x], axis=1)
    shard_out = jnp.concatenate([trading[2].x, trading[3].x], axis=1)
    output = (mid + out_sum.astype(F32)).astype(BF).reshape(rows, tok, width)
    for row in range(rows):
        dpr, qs, ks = unpack_heads(back[row], proj, cos, sin, q_gain, k_gain, row, chips, chip_tok)
        d_proj.append(dpr)
        q_sum = q_sum + qs
        k_sum = k_sum + ks
    d_proj = jnp.concatenate(d_proj, axis=0)
    d_proj, recv = tie(d_proj, recv)
    d_logit = jnp.concatenate(d_logit, axis=0)
    half = width // 2
    part_qkv = [dot_tn(d_proj, normed_a[:, a : a + half], BF) for a in (0, half)]
    trading = [Halving(p, dp, flip) for p, flip in zip(part_qkv, (False, True))]
    moved = [t.send() for t in trading]
    while trading[0].order:
        for t, m in zip(trading, moved):
            t.add(m)
        moved = [t.send() for t in trading]
    for t, m in zip(trading, moved):
        t.add(m)
    shard_qkv = [t.x for t in trading]
    d_norm_part = (dot_nn(d_proj, qkv_full) + dot_nn(d_logit, gate_core)).astype(BF)
    d_norm_part = d_norm_part.reshape(rows, CORES, tok, width)
    d_norm_other = swap(pick(d_norm_part[:, 1], d_norm_part[:, 0]))
    d_normed_a = pick(d_norm_part[:, 0], d_norm_part[:, 1]).astype(F32) + d_norm_other.astype(F32)
    own_in = layer_input.astype(F32)
    own_factor = lax.rsqrt(jnp.mean(own_in * own_in, axis=-1, keepdims=True) + epsilon)
    part_attn = jnp.sum(d_normed_a * own_in * own_factor, axis=(0, 1))
    weighted_a = d_normed_a * attn_norm
    inner_a = jnp.mean(weighted_a * own_in, axis=-1, keepdims=True)
    grad_input = (
        d_mid.reshape(rows, tok, width) + own_factor * weighted_a - own_in * own_factor**3 * inner_a
    ).astype(BF)

    heads = jnp.concatenate([jnp.sum(q_sum, axis=0), jnp.sum(k_sum, axis=0)])
    heads = jnp.pad(heads, (0, width - heads.shape[0]))

    def norm_done(done):
        return [part_attn, grad_input]

    def late_sum(done):
        return [total_sum(jnp.stack([part_attn, heads]))]

    grad_w_gate = lax.dynamic_slice_in_dim(early, me * gate_count, gate_count, 0)

    mid_cut = down_sum.shape[1] // 2
    line = Line(chips, chip)
    sent = lax.ppermute(recv, "dp", trade)

    def join_early(done):
        down_done = jnp.concatenate(done[:2], axis=1)
        places = [unit_block.index(b) ^ me for b in range(dp)]
        return [
            join_units([keep, sent], [swap(keep), swap(sent)], core, upper.astype(jnp.int32)),
            join_blocks(down_done, swap(down_done), core, places),
        ]

    def join_late(done):
        return [join_cols([done[2]], [swap(done[2])], core, GROUP * HEAD)]

    sums, ((_, grad_input), (late,), (grad_gu, grad_down), (grad_out,)) = line.pipeline(
        [down_sum[:, :mid_cut], down_sum[:, mid_cut:], shard_out, *shard_qkv],
        {1: norm_done, 3: late_sum, 5: join_early, 6: join_late},
    )
    qkv_sum = sums[3:]
    grad_qkv = join_rows(qkv_sum, [swap(p) for p in qkv_sum], core, jnp.where(q_shard, GROUP, 1), HEAD)
    return (
        output,
        grad_input,
        late[0],
        late[1, :HEAD],
        late[1, HEAD : 2 * HEAD],
        early[QUERY_HEADS],
        grad_qkv,
        grad_w_gate,
        grad_out,
        grad_gu,
        grad_down,
    )


def solution(mesh):
    token = P("dp", "seq", None)
    shard = P("dp", None)
    in_specs = (token, shard, P(), P(), P(), P(), shard, shard, shard, shard, shard, token)
    out_specs = (token, token, P(), P(), P(), P(), shard, shard, shard, shard, shard)
    return jax.shard_map(shards, mesh=mesh, in_specs=in_specs, out_specs=out_specs, check_vma=False)
```

```python
import functools
import math

import jax
import jax.numpy as jnp
from jax import lax
from jax.experimental import pallas as pl
from jax.experimental.pallas import tpu as pltpu
from jax.sharding import PartitionSpec as P

QUERY_HEADS = 16
KEY_VALUE_HEADS = 8
HEAD = 128
FF = 6144
CORES = 2

GROUP = QUERY_HEADS // KEY_VALUE_HEADS
CORE_Q = QUERY_HEADS // CORES
CORE_KV = KEY_VALUE_HEADS // CORES
epsilon = 1e-06
theta_base = 1000000.0
SCALE = 1.0 / math.sqrt(HEAD)
SCALE2 = SCALE * math.log2(math.e)
BF = jnp.bfloat16
F32 = jnp.float32


def dot_nt(left, right, out=F32):
    return lax.dot_general(left, right, (((1,), (1,)), ((), ())), preferred_element_type=F32).astype(out)


def dot_nn(left, right, out=F32):
    return lax.dot_general(left, right, (((1,), (0,)), ((), ())), preferred_element_type=F32).astype(out)


def dot_tn(left, right, out=F32):
    return lax.dot_general(left, right, (((0,), (0,)), ((), ())), preferred_element_type=F32).astype(out)


def doc_positions(lengths, total):
    ends = jnp.cumsum(lengths, axis=-1)
    starts = ends - lengths
    places = jnp.arange(total, dtype=jnp.int32)
    segment = jnp.sum((places[:, None] >= ends[..., None, :]).astype(jnp.int32), axis=-1)
    owners = segment[..., None] == jnp.arange(lengths.shape[-1], dtype=jnp.int32)
    first = jnp.sum(jnp.where(owners, starts[..., None, :], 0), axis=-1)
    return first, places - first


def pack_kernel(chips, proj_ref, cos_ref, sin_ref, qg_ref, kg_ref, out_ref):
    per = CORE_Q // chips
    copies = max(1, chips // CORE_KV)
    cos = cos_ref[...]
    sin = sin_ref[...]

    def head(index, gain):
        u = proj_ref[:, index * HEAD : (index + 1) * HEAD]
        factor = lax.rsqrt(jnp.mean(u * u, axis=-1, keepdims=True) + epsilon)
        n = u * factor * gain
        return (n * cos + pltpu.roll(n, HEAD // 2, 1) * sin).astype(BF)

    for z in range(chips):
        for h in range(per):
            out_ref[z, :, h * HEAD : (h + 1) * HEAD] = head(z * per + h, qg_ref[...])
        if z % copies == 0:
            kv = z // copies
            key = head(CORE_Q + kv, kg_ref[...])
            base = (CORE_Q + CORE_KV + kv) * HEAD
            value = proj_ref[:, base : base + HEAD].astype(BF)
        out_ref[z, :, per * HEAD : (per + 1) * HEAD] = key
        out_ref[z, :, (per + 1) * HEAD : (per + 2) * HEAD] = value


def pack_heads(proj, cos, sin, q_gain, k_gain, row, chips, chip_tok):
    per = CORE_Q // chips
    lanes = (per + 2) * HEAD
    block = min(256, chip_tok)
    steps = chip_tok // block
    width = proj.shape[1]
    tok = lambda i: (row * steps + i, 0)
    return pl.pallas_call(
        functools.partial(pack_kernel, chips),
        grid=(steps,),
        in_specs=[
            pl.BlockSpec((block, width), tok),
            pl.BlockSpec((block, HEAD), tok),
            pl.BlockSpec((block, HEAD), tok),
            pl.BlockSpec((1, HEAD), lambda i: (0, 0)),
            pl.BlockSpec((1, HEAD), lambda i: (0, 0)),
        ],
        out_specs=pl.BlockSpec((chips, block, lanes), lambda i: (0, i, 0)),
        out_shape=jax.ShapeDtypeStruct((chips, chip_tok, lanes), BF),
        name="pack_heads",
    )(proj, cos, sin, q_gain, k_gain)


def unpack_kernel(chips, grad_ref, proj_ref, cos_ref, sin_ref, qg_ref, kg_ref, out_ref, qs_ref, ks_ref):
    per = CORE_Q // chips
    copies = max(1, chips // CORE_KV)
    cos = cos_ref[...]
    sin = sin_ref[...]

    @pl.when(pl.program_id(0) == 0)
    def _():
        qs_ref[...] = jnp.zeros_like(qs_ref)
        ks_ref[...] = jnp.zeros_like(ks_ref)

    def head(e, index, gain, sum_ref):
        e = e * cos + pltpu.roll(e * sin, HEAD // 2, 1)
        u = proj_ref[:, index * HEAD : (index + 1) * HEAD]
        factor = lax.rsqrt(jnp.mean(u * u, axis=-1, keepdims=True) + epsilon)
        n = u * factor
        sum_ref[...] += jnp.sum((e * n).reshape(-1, 8, HEAD), axis=0)
        weighted = e * gain
        inner = jnp.mean(weighted * n, axis=-1, keepdims=True)
        out_ref[:, index * HEAD : (index + 1) * HEAD] = (factor * (weighted - n * inner)).astype(BF)

    def part(z, lane):
        return grad_ref[z, :, lane * HEAD : (lane + 1) * HEAD].astype(F32)

    for z in range(chips):
        for h in range(per):
            head(part(z, h), z * per + h, qg_ref[...], qs_ref)
    for kv in range(CORE_KV):
        spread = range(kv * copies, (kv + 1) * copies)
        head(sum(part(z, per) for z in spread), CORE_Q + kv, kg_ref[...], ks_ref)
        base = (CORE_Q + CORE_KV + kv) * HEAD
        out_ref[:, base : base + HEAD] = sum(part(z, per + 1) for z in spread).astype(BF)


def unpack_heads(grads, proj, cos, sin, q_gain, k_gain, row, chips, chip_tok):
    lanes = grads.shape[2]
    block = min(256, chip_tok)
    steps = chip_tok // block
    width = proj.shape[1]
    tok = lambda i: (row * steps + i, 0)
    small = pl.BlockSpec((8, HEAD), lambda i: (0, 0))
    return pl.pallas_call(
        functools.partial(unpack_kernel, chips),
        grid=(steps,),
        in_specs=[
            pl.BlockSpec((chips, block, lanes), lambda i: (0, i, 0)),
            pl.BlockSpec((block, width), tok),
            pl.BlockSpec((block, HEAD), tok),
            pl.BlockSpec((block, HEAD), tok),
            pl.BlockSpec((1, HEAD), lambda i: (0, 0)),
            pl.BlockSpec((1, HEAD), lambda i: (0, 0)),
        ],
        out_specs=[pl.BlockSpec((block, width), lambda i: (i, 0)), small, small],
        out_shape=[
            jax.ShapeDtypeStruct((chip_tok, width), BF),
            jax.ShapeDtypeStruct((8, HEAD), F32),
            jax.ShapeDtypeStruct((8, HEAD), F32),
        ],
        name="unpack_heads",
    )(grads, proj, cos, sin, q_gain, k_gain)


def visible(j, size, start, diagonal):
    inner = lax.broadcasted_iota(jnp.int32, (size, size), 0)
    allowed = inner >= start - j * size
    if diagonal:
        allowed = allowed & (inner <= lax.broadcasted_iota(jnp.int32, (size, size), 1))
    return allowed


def attend_kernel(per, low_ref, q_ref, k_ref, v_ref, start_ref, out_ref, log_ref, acc_ref, sum_ref):
    i = pl.program_id(0)
    size = q_ref.shape[1]
    start = start_ref[...]
    acc_ref[...] = jnp.zeros_like(acc_ref)
    sum_ref[...] = jnp.zeros_like(sum_ref)

    def one(j, diagonal):
        key = k_ref[j]
        value = v_ref[j]
        allowed = visible(j, size, start, diagonal)
        for h in range(per):
            scores = dot_nt(key, q_ref[0, :, h * HEAD : (h + 1) * HEAD])
            p = jnp.where(allowed, jnp.exp2(scores * SCALE2), 0.0)
            sum_ref[h : h + 1, :] += jnp.sum(p, axis=0, keepdims=True)
            acc_ref[h] += dot_tn(value, p.astype(BF))

    def step(j, carry):
        one(j, False)
        return carry

    lax.fori_loop(low_ref[i], i, step, 0)
    one(i, True)
    for h in range(per):
        total = sum_ref[h : h + 1, :]
        out_ref[0, :, h * HEAD : (h + 1) * HEAD] = (acc_ref[h] / total).T.astype(BF)
        log_ref[h : h + 1, :] = jnp.log2(total)


def attend(packed, start, low):
    chips, size, lanes = packed.shape
    per = lanes // HEAD - 2
    return pl.pallas_call(
        functools.partial(attend_kernel, per),
        grid_spec=pltpu.PrefetchScalarGridSpec(
            num_scalar_prefetch=1,
            grid=(chips,),
            in_specs=[
                pl.BlockSpec((1, size, per * HEAD), lambda i, low: (i, 0, 0)),
                pl.BlockSpec((chips, size, HEAD), lambda i, low: (0, 0, per)),
                pl.BlockSpec((chips, size, HEAD), lambda i, low: (0, 0, per + 1)),
                pl.BlockSpec((1, size), lambda i, low: (0, i)),
            ],
            out_specs=[
                pl.BlockSpec((1, size, per * HEAD), lambda i, low: (i, 0, 0)),
                pl.BlockSpec((per, size), lambda i, low: (0, i)),
            ],
            scratch_shapes=[pltpu.VMEM((per, HEAD, size), F32), pltpu.VMEM((per, size), F32)],
        ),
        out_shape=[
            jax.ShapeDtypeStruct((chips, size, per * HEAD), BF),
            jax.ShapeDtypeStruct((per, chips * size), F32),
        ],
        name="attend",
    )(low, packed, packed, packed, start)


def attend_back_kernel(
    per, low_ref, q_ref, k_ref, v_ref, grad_ref, res_ref, log_ref, start_ref, out_ref, dq_ref, dk_ref, dv_ref
):
    i = pl.program_id(0)
    size = q_ref.shape[1]
    start = start_ref[...]

    @pl.when(i == 0)
    def _():
        dk_ref[...] = jnp.zeros_like(dk_ref)
        dv_ref[...] = jnp.zeros_like(dv_ref)

    dq_ref[...] = jnp.zeros_like(dq_ref)
    ones = jnp.ones((8, HEAD), F32)
    inner = []
    for h in range(per):
        cols = slice(h * HEAD, (h + 1) * HEAD)
        both = grad_ref[0, :, cols].astype(F32) * res_ref[0, :, cols].astype(F32)
        sums = lax.dot_general(
            ones, both, (((1,), (1,)), ((), ())), precision=lax.Precision.HIGHEST, preferred_element_type=F32
        )
        inner.append(sums[0:1, :])

    def one(j, diagonal):
        key = k_ref[j]
        value = v_ref[j]
        allowed = visible(j, size, start, diagonal)
        for h in range(per):
            query = q_ref[0, :, h * HEAD : (h + 1) * HEAD]
            grad = grad_ref[0, :, h * HEAD : (h + 1) * HEAD]
            scores = dot_nt(key, query)
            p = jnp.where(allowed, jnp.exp2(scores * SCALE2 - log_ref[h : h + 1, :]), 0.0)
            dp = dot_nt(value, grad)
            ds = (p * (dp - inner[h])).astype(BF)
            dv_ref[j] += dot_nn(p.astype(BF), grad)
            dk_ref[j] += dot_nn(ds, query)
            dq_ref[h] += dot_tn(ds, key)

    def step(j, carry):
        one(j, False)
        return carry

    lax.fori_loop(low_ref[i], i, step, 0)
    one(i, True)
    for h in range(per):
        out_ref[i, :, h * HEAD : (h + 1) * HEAD] = (dq_ref[h] * SCALE).astype(BF)

    @pl.when(i == pl.num_programs(0) - 1)
    def _():
        out_ref[:, :, per * HEAD : (per + 1) * HEAD] = (dk_ref[...] * SCALE).astype(BF)
        out_ref[:, :, (per + 1) * HEAD : (per + 2) * HEAD] = dv_ref[...].astype(BF)


def attend_back(packed, grad, result, logs, start, low):
    chips, size, lanes = packed.shape
    per = lanes // HEAD - 2
    one = pl.BlockSpec((1, size, per * HEAD), lambda i, low: (i, 0, 0))
    return pl.pallas_call(
        functools.partial(attend_back_kernel, per),
        grid_spec=pltpu.PrefetchScalarGridSpec(
            num_scalar_prefetch=1,
            grid=(chips,),
            in_specs=[
                one,
                pl.BlockSpec((chips, size, HEAD), lambda i, low: (0, 0, per)),
                pl.BlockSpec((chips, size, HEAD), lambda i, low: (0, 0, per + 1)),
                one,
                one,
                pl.BlockSpec((per, size), lambda i, low: (0, i)),
                pl.BlockSpec((1, size), lambda i, low: (0, i)),
            ],
            out_specs=pl.BlockSpec((chips, size, lanes), lambda i, low: (0, 0, 0)),
            scratch_shapes=[
                pltpu.VMEM((per, size, HEAD), F32),
                pltpu.VMEM((chips, size, HEAD), F32),
                pltpu.VMEM((chips, size, HEAD), F32),
            ],
        ),
        out_shape=jax.ShapeDtypeStruct((chips, size, lanes), BF),
        name="attend_back",
    )(low, packed, packed, packed, grad, result, logs, start)


def gate_kernel(res_ref, logit_ref, out_ref):
    chips, _, lanes = res_ref.shape
    per = lanes // HEAD
    sig = jax.nn.sigmoid(logit_ref[...])
    for z in range(chips):
        for h in range(per):
            head = z * per + h
            value = res_ref[z, :, h * HEAD : (h + 1) * HEAD].astype(F32)
            out_ref[:, head * HEAD : (head + 1) * HEAD] = (value * sig[:, head : head + 1]).astype(BF)


def gate_rows(result, logits, row):
    chips, size, lanes = result.shape
    block = min(256, size)
    steps = size // block
    return pl.pallas_call(
        gate_kernel,
        grid=(steps,),
        in_specs=[
            pl.BlockSpec((chips, block, lanes), lambda i: (0, i, 0)),
            pl.BlockSpec((block, HEAD), lambda i: (row * steps + i, 0)),
        ],
        out_specs=pl.BlockSpec((block, chips * lanes), lambda i: (i, 0)),
        out_shape=jax.ShapeDtypeStruct((size, chips * lanes), BF),
        name="gate_rows",
    )(result, logits)


def gate_back_kernel(grad_ref, res_ref, logit_ref, out_ref, dlogit_ref):
    chips, size, lanes = res_ref.shape
    per = lanes // HEAD
    sig = jax.nn.sigmoid(logit_ref[...])
    lane = lax.broadcasted_iota(jnp.int32, sig.shape, 1)
    sums = jnp.zeros(sig.shape, F32)
    for z in range(chips):
        for h in range(per):
            head = z * per + h
            e = grad_ref[:, head * HEAD : (head + 1) * HEAD]
            value = res_ref[z, :, h * HEAD : (h + 1) * HEAD].astype(F32)
            out_ref[z, :, h * HEAD : (h + 1) * HEAD] = (e * sig[:, head : head + 1]).astype(BF)
            sums = jnp.where(lane == head, jnp.sum(e * value, axis=-1, keepdims=True), sums)
    dlogit_ref[...] = (sums * sig * (1.0 - sig)).astype(BF)


def gate_back(grad, result, logits, row):
    chips, size, lanes = result.shape
    block = min(256, size)
    steps = size // block
    return pl.pallas_call(
        gate_back_kernel,
        grid=(steps,),
        in_specs=[
            pl.BlockSpec((block, chips * lanes), lambda i: (i, 0)),
            pl.BlockSpec((chips, block, lanes), lambda i: (0, i, 0)),
            pl.BlockSpec((block, HEAD), lambda i: (row * steps + i, 0)),
        ],
        out_specs=[
            pl.BlockSpec((chips, block, lanes), lambda i: (0, i, 0)),
            pl.BlockSpec((block, HEAD), lambda i: (i, 0)),
        ],
        out_shape=[jax.ShapeDtypeStruct((chips, size, lanes), BF), jax.ShapeDtypeStruct((size, HEAD), BF)],
        name="gate_back",
    )(grad, result, logits)


def join_rows_kernel(count, which_ref, *refs):
    out_ref = refs[2 * count]
    size = refs[0].shape[1]
    own_half = pl.program_id(0) == which_ref[0]

    def put(parts):
        for k in range(count):
            out_ref[:, k * size : (k + 1) * size] = parts[k][...].astype(F32)

    pl.when(own_half)(lambda: put(refs[:count]))
    pl.when(jnp.logical_not(own_half))(lambda: put(refs[count : 2 * count]))


def join_rows(mine, other, core, blocks, block):
    count = len(mine)
    height, size = mine[0].shape
    steps = height // block

    def source(side):
        def index(h, i, which):
            active = (h == which[0]) if side == 0 else (h != which[0])
            return (jnp.where(active, i, jnp.where(h == 0, 0, steps - 1)), 0)

        return pl.BlockSpec((block, size), index)

    def target(h, i, which):
        per = which[1]
        return ((i // per) * 2 * per + h * per + i % per, 0)

    return pl.pallas_call(
        functools.partial(join_rows_kernel, count),
        grid_spec=pltpu.PrefetchScalarGridSpec(
            num_scalar_prefetch=1,
            grid=(CORES, steps),
            in_specs=[source(0)] * count + [source(1)] * count,
            out_specs=pl.BlockSpec((block, count * size), target),
        ),
        out_shape=jax.ShapeDtypeStruct((CORES * height, count * size), F32),
        name="join_rows",
    )(jnp.stack([core, blocks.astype(jnp.int32)]), *mine, *other)


def join_cols_kernel(count, per, which_ref, *refs):
    out_ref = refs[2 * count]
    u = pl.program_id(0)
    own_half = pl.program_id(1) == which_ref[0]

    def put(ref):
        out_ref[...] = ref[...].astype(F32)

    for k in range(count):
        here = u // per == k
        pl.when(here & own_half)(functools.partial(put, refs[k]))
        pl.when(here & jnp.logical_not(own_half))(functools.partial(put, refs[count + k]))


def join_cols(mine, other, core, unit):
    count = len(mine)
    height, size = mine[0].shape
    per = size // unit

    def source(k):
        return pl.BlockSpec((height, unit), lambda u, h, which: (0, jnp.clip(u - k * per, 0, per - 1)))

    sources = [source(k) for k in range(count)]
    return pl.pallas_call(
        functools.partial(join_cols_kernel, count, per),
        grid_spec=pltpu.PrefetchScalarGridSpec(
            num_scalar_prefetch=1,
            grid=(count * per, CORES),
            in_specs=sources + sources,
            out_specs=pl.BlockSpec((height, unit), lambda u, h, which: (0, u * CORES + h)),
        ),
        out_shape=jax.ShapeDtypeStruct((height, CORES * count * size), F32),
        name="join_cols",
    )(core[None], *mine, *other)


def join_units_kernel(which_ref, keep_ref, keep_other_ref, sent_ref, sent_other_ref, out_ref):
    kept = pl.program_id(0) == which_ref[1]
    mine = pl.program_id(1) == which_ref[0]
    for side, pair in ((True, (keep_ref, keep_other_ref)), (False, (sent_ref, sent_other_ref))):
        for here, ref in ((True, pair[0]), (False, pair[1])):

            @pl.when((kept == side) & (mine == here))
            def _(ref=ref):
                out_ref[...] = ref[...].astype(F32)


def join_units(mine, other, core, upper):
    height, width = mine[0].shape
    block = 256
    steps = height // block
    sources = []
    for side in (0, 1):
        for half in (0, 1):

            def index(p, h, i, which, side=side, half=half):
                at_side = (p == which[1]) if side == 0 else (p != which[1])
                at_half = (h == which[0]) if half == 0 else (h != which[0])
                side_p = which[1] if side == 0 else 1 - which[1]
                side_h = which[0] if half == 0 else 1 - which[0]
                before = (p * 2 + h) < (side_p * 2 + side_h)
                return (jnp.where(at_side & at_half, i, jnp.where(before, 0, steps - 1)), 0)

            sources.append(pl.BlockSpec((block, width), index))
    return pl.pallas_call(
        join_units_kernel,
        grid_spec=pltpu.PrefetchScalarGridSpec(
            num_scalar_prefetch=1,
            grid=(2, CORES, steps),
            in_specs=sources,
            out_specs=pl.BlockSpec((block, width), lambda p, h, i, which: ((p * CORES + h) * steps + i, 0)),
        ),
        out_shape=jax.ShapeDtypeStruct((2 * CORES * height, width), F32),
        name="join_units",
    )(jnp.stack([core, upper]), mine[0], other[0], mine[1], other[1])


def join_blocks_kernel(which_ref, mine_ref, other_ref, out_ref):
    own_half = pl.program_id(0) == which_ref[0]
    for here, ref in ((True, mine_ref), (False, other_ref)):

        @pl.when(own_half == here)
        def _(ref=ref):
            out_ref[...] = ref[0].astype(F32)


def join_blocks(mine, other, core, order):
    count, height, size = mine.shape
    source = pl.BlockSpec((1, height, size), lambda h, b, which, where: (where[b], 0, 0))
    return pl.pallas_call(
        lambda which_ref, where_ref, *refs: join_blocks_kernel(which_ref, *refs),
        grid_spec=pltpu.PrefetchScalarGridSpec(
            num_scalar_prefetch=2,
            grid=(CORES, count),
            in_specs=[source, source],
            out_specs=pl.BlockSpec((height, size), lambda h, b, which, where: (h, b)),
        ),
        out_shape=jax.ShapeDtypeStruct((CORES * height, count * size), F32),
        name="join_blocks",
    )(core[None], jnp.stack(order).astype(jnp.int32), mine, other)


class Halving:
    def __init__(self, x, dp, flip):
        self.dp = dp
        self.mine = lax.axis_index("dp")
        bits = dp.bit_length() - 1
        self.left = list(range(bits))
        self.order = self.left[::-1] if flip else self.left[:]
        self.x = x.reshape((2,) * bits + (x.shape[0] // dp, x.shape[1]))

    def send(self):
        bit = self.order.pop(0)
        axis = sum(1 for b in self.left if b > bit)
        self.left.remove(bit)
        low, high = lax.index_in_dim(self.x, 0, axis, False), lax.index_in_dim(self.x, 1, axis, False)
        mark = (self.mine >> bit) % 2 == 1
        pairs = [(d, d ^ (1 << bit)) for d in range(self.dp)]
        self.keep = jnp.where(mark, high, low)
        return lax.ppermute(jnp.where(mark, low, high), "dp", pairs)

    def add(self, moved):
        self.x = self.keep + moved


class Line:
    def __init__(self, chips, chip):
        self.chips = chips
        self.inner = (chip == 1) | (chip == 2)
        ends = lambda pairs: [(a * CORES + c, b * CORES + c) for a, b in pairs for c in range(CORES)]
        self.stages = [ends([(0, 1), (3, 2)]), ends([(1, 2), (2, 1)]), ends([(1, 0), (2, 3)])]
        self.groups = [[z * CORES + c for z in range(chips)] for c in range(CORES)]

    def send(self, x, stage):
        if self.chips != 4:
            return (x, lax.psum(x, "seq", axis_index_groups=self.groups) if stage == 0 else x)
        return (x, lax.ppermute(x, "seq", self.stages[stage]))

    def begin(self, x):
        return (0,) + self.send(x, 0)

    def next(self, state):
        stage, x, moved = state
        if self.chips != 4:
            return (stage + 1, moved, moved)
        return (stage + 1,) + self.send(x + moved, stage + 1)

    def end(self, state):
        stage, x, moved = state
        return moved if self.chips != 4 else jnp.where(self.inner, x, moved)

    def pipeline(self, parts, fillers):
        if self.chips != 4:
            done = lax.psum(parts, "seq", axis_index_groups=self.groups)
            return done, [filler(done) for filler in fillers.values()]
        count = len(parts)
        states = [None] * count
        made = []
        for step in range(count + 2):
            for k in range(count):
                if k == step:
                    states[k] = self.begin(parts[k])
                elif k < step <= k + 2:
                    states[k] = self.next(states[k])
            done = [self.end(states[k]) if k + 3 <= step else None for k in range(count)]
            extra = fillers[step](done) if step in fillers else []
            live = [k for k in range(count) if states[k] is not None]
            later = [k for k in range(step + 1, min(step + 2, count))]
            moved, extra = lax.optimization_barrier(
                ([states[k][1:] for k in live] + [parts[k] for k in later], extra)
            )
            if step in fillers:
                made.append(extra)
            for k, value in zip(live + later, moved):
                if k in later:
                    parts[k] = value
                else:
                    states[k] = (states[k][0], *value)
        return [self.end(state) for state in states], made


def tie_all(values, work):
    return lax.optimization_barrier((values, work))


def tie(value, work):
    leaves, tree = jax.tree.flatten(work)
    moving = [x for x in leaves if not isinstance(x, int)]
    value, *moving = lax.optimization_barrier((value, *moving))
    moving = iter(moving)
    return value, jax.tree.unflatten(tree, [x if isinstance(x, int) else next(moving) for x in leaves])


def shards(
    layer_input,
    doc_lengths,
    attn_norm,
    q_norm,
    k_norm,
    ffn_norm,
    w_qkv,
    w_gate,
    w_out,
    w_gu,
    w_down,
    cotangent,
):
    rows, tok, width = layer_input.shape
    seq = lax.axis_size("seq")
    dp = lax.axis_size("dp")
    chips = seq // CORES
    place = lax.axis_index("seq")
    core = place % CORES
    chip = place // CORES
    first = core == 0
    chip_tok = tok * CORES
    length = tok * seq
    tokens = rows * chip_tok
    pair = [(s, s ^ 1) for s in range(seq)]
    groups = [[z * CORES + c for z in range(chips)] for c in range(CORES)]
    q_shard = lax.axis_index("dp") * w_qkv.shape[0] < QUERY_HEADS * HEAD

    def swap(x):
        return lax.ppermute(x, "seq", pair)

    def pick(a, b):
        return jnp.where(first, a, b)

    def both(x):
        other = swap(x)
        return jnp.concatenate([pick(x, other), pick(other, x)], axis=1).reshape(tokens, width)

    def exchange(x):
        return lax.all_to_all(x, "seq", 0, 0, axis_index_groups=groups, tiled=True)

    def total_sum(x, names=("seq", "dp")):
        for name in names:
            size = lax.axis_size(name)
            step = 1
            while step < size:
                x = x + lax.ppermute(x, name, [(s, s ^ step) for s in range(size)])
                step *= 2
        return x

    def scatter(x):
        return lax.psum_scatter(x, "dp", scatter_dimension=0, tiled=True)

    def gather(x):
        return lax.all_gather(x, "dp", axis=0, tiled=True)

    def core_rows(w, unit):
        return jnp.concatenate(
            [pick(w[a : a + unit], w[a + unit : a + 2 * unit]) for a in range(0, w.shape[0], 2 * unit)], axis=0
        )

    def core_cols(w, unit):
        return jnp.concatenate(
            [pick(w[:, a : a + unit], w[:, a + unit : a + 2 * unit]) for a in range(0, w.shape[1], 2 * unit)],
            axis=1,
        )

    def trade_blocks(x):
        mine = lax.axis_index("dp")
        found = [(mine, lax.dynamic_index_in_dim(x, mine, 0, keepdims=False))]
        for k in range(1, dp):
            out = lax.dynamic_index_in_dim(x, mine ^ k, 0, keepdims=False)
            found.append((mine ^ k, lax.ppermute(out, "dp", [(d, d ^ k) for d in range(dp)])))
        return found

    half_dp = dp // 2
    me = lax.axis_index("dp")
    upper = me >= half_dp
    trade = [(d, d ^ half_dp) for d in range(dp)]
    units = w_gu.shape[0] // 2
    owned = rows * tok

    qkv_half = jnp.where(q_shard, core_rows(w_qkv, GROUP * HEAD), core_rows(w_qkv, HEAD))
    qkv_full = gather(qkv_half)
    out_full = gather(core_cols(w_out, GROUP * HEAD))
    ctg = cotangent.reshape(owned, width)
    gate_count = w_gate.shape[0]
    gate_full = lax.dynamic_update_slice_in_dim(jnp.zeros((QUERY_HEADS, width), BF), w_gate, me * gate_count, 0)
    gate_full = total_sum(gate_full, ("dp",))
    gate_core = jnp.pad(core_rows(gate_full, GROUP), ((0, HEAD - CORE_Q), (0, 0)))

    gu_keep = jnp.where(upper, w_gu[units:], w_gu[:units])
    quarter = units // 2
    gu_send = jnp.where(
        upper, pick(w_gu[:quarter], w_gu[quarter:units]), pick(w_gu[units : units + quarter], w_gu[units + quarter :])
    )
    out_rows = w_down.shape[0] // 2
    down_core = pick(w_down[:out_rows], w_down[out_rows:])
    unit_block = [(d % half_dp) * 2 + d // half_dp for d in range(dp)]
    down_send = jnp.stack([down_core[:, b * units : (b + 1) * units] for b in unit_block])
    (qkv_full, gu_send, down_send) = lax.optimization_barrier((qkv_full, gu_send, down_send))
    gu_pair = lax.all_gather(gu_send, "dp", axis_index_groups=[[d, d + half_dp] for d in range(half_dp)])
    gu_half = jnp.where(upper, gu_pair[0], gu_pair[1])
    down_half = jnp.zeros_like(down_send)
    for other, moved in trade_blocks(down_send):
        down_half = lax.dynamic_update_index_in_dim(down_half, moved, other, 0)

    start, position = doc_positions(doc_lengths, length)
    low = start.reshape(rows, chips, chip_tok)[:, :, 0] // chip_tok
    local = lax.dynamic_slice_in_dim(position, chip * chip_tok, chip_tok, 1).reshape(tokens)
    freq = jnp.power(theta_base, -(jnp.arange(HEAD // 2, dtype=F32) * 2.0) / HEAD)
    angle = local.astype(F32)[:, None] * freq
    cos = jnp.cos(angle)
    sin = jnp.sin(angle)
    cos = jnp.concatenate([cos, cos], axis=1)
    sin = jnp.concatenate([-sin, sin], axis=1)

    inputs = both(layer_input).astype(F32)
    factor_a = lax.rsqrt(jnp.mean(inputs * inputs, axis=-1, keepdims=True) + epsilon)
    normed_a = (inputs * factor_a * attn_norm).astype(BF)
    logits = dot_nt(normed_a, gate_core)
    proj = dot_nt(normed_a, qkv_full)
    q_gain = q_norm[None, :]
    k_gain = k_norm[None, :]

    packed, results, logs, gated, mid = [], [], [], [], []
    for row in range(rows):
        cos_row = cos
        if row:
            cos_row, logits = tie(cos, logits)
        packed.append(exchange(pack_heads(proj, cos_row, sin, q_gain, k_gain, row, chips, chip_tok)))
    packed[0], down_half = tie(packed[0], down_half)
    packed[-1], ctg_late = tie(packed[-1], ctg)
    ctg_all = gather(ctg_late)
    for row in range(rows):
        head_out, log = attend(packed[row], start[row : row + 1], low[row])
        results.append(head_out)
        logs.append(log)
    tok_results = [exchange(r) for r in results]
    gu_other = swap(gu_half)
    down_other = swap(down_half)
    for row in range(rows):
        gated.append(gate_rows(tok_results[row], logits, row))
        part = dot_nt(gated[row], out_full, BF).reshape(CORES, tok, width)
        other = swap(pick(part[1], part[0]))
        mid.append(layer_input[row].astype(F32) + pick(part[0], part[1]).astype(F32) + other.astype(F32))
    mid = jnp.concatenate(mid, axis=0)
    gated = jnp.concatenate(gated, axis=0)

    factor_f = lax.rsqrt(jnp.mean(mid * mid, axis=-1, keepdims=True) + epsilon)
    normed_f = (mid * factor_f * ffn_norm).astype(BF)
    normed_all = gather(normed_f)
    gu_recv = jnp.concatenate([pick(gu_half, gu_other), pick(gu_other, gu_half)], axis=0)
    down_full = jnp.concatenate([pick(down_half, down_other), pick(down_other, down_half)], axis=1)
    down_full = down_full.reshape(width, units)
    d_hidden = dot_nn(ctg_all, down_full, BF)
    normed_all, (d_hidden, gu_recv) = tie(normed_all, (d_hidden, gu_recv))
    keep_part = dot_nt(normed_all, gu_keep, BF)
    recv_part = dot_nt(normed_all, gu_recv, BF)
    gate_part = jnp.where(upper, recv_part, keep_part).astype(F32)
    up_part = jnp.where(upper, keep_part, recv_part).astype(F32)
    d_hid = d_hidden.astype(F32)
    gate_act = jax.nn.sigmoid(gate_part)
    silu = gate_part * gate_act
    hidden = (silu * up_part).astype(BF)
    d_gate = d_hid * up_part * gate_act * (1.0 + gate_part * (1.0 - gate_act))
    d_up = d_hid * silu
    d_keep = jnp.where(upper, d_up, d_gate).astype(BF)
    d_recv = jnp.where(upper, d_gate, d_up).astype(BF)
    d_normed = scatter((dot_nn(d_keep, gu_keep) + dot_nn(d_recv, gu_recv)).astype(BF))

    part_keep = dot_tn(d_keep, normed_all, BF)
    part_recv = dot_tn(d_recv, normed_all, BF)
    part_down = dot_tn(ctg_all, hidden, BF).reshape(dp, CORES, out_rows, units)
    keep_swap = swap(pick(part_keep[quarter:], part_keep[:quarter]))
    recv_swap = swap(pick(part_recv[quarter:], part_recv[:quarter]))
    down_swap = swap(pick(part_down[:, 1], part_down[:, 0]))
    d_normed, (part_keep, part_recv, part_down, keep_swap, recv_swap) = tie(
        d_normed, (part_keep, part_recv, part_down, keep_swap, recv_swap)
    )
    keep_sum = pick(part_keep[:quarter], part_keep[quarter:]) + keep_swap
    recv_sum = pick(part_recv[:quarter], part_recv[quarter:]) + recv_swap
    d_normed, gu_sum = tie(d_normed, jnp.concatenate([keep_sum, recv_sum], axis=0))
    gu_sum = lax.psum(gu_sum, "seq", axis_index_groups=groups)

    d_normed = d_normed.astype(F32)
    part_ffn = jnp.sum(d_normed * mid * factor_f, axis=0)
    weighted = d_normed * ffn_norm
    inner = jnp.mean(weighted * mid, axis=-1, keepdims=True)
    d_mid = ctg.astype(F32) + factor_f * weighted - mid * factor_f**3 * inner
    low_mine = d_mid.astype(BF).reshape(rows, tok, width)
    low_other = swap(low_mine)
    low_other, down_swap = tie(low_other, down_swap)
    down_sum = pick(part_down[:, 0], part_down[:, 1]) + down_swap
    down_sum = jnp.stack([moved for _, moved in trade_blocks(down_sum)])

    d_mid_low = jnp.concatenate([pick(low_mine, low_other), pick(low_other, low_mine)], axis=1).reshape(tokens, width)
    part_out = dot_tn(d_mid_low, gated, BF)
    d_proj, d_logit, d_heads = [], [], []
    q_sum = 0.0
    k_sum = 0.0
    for row in range(rows):
        low_row = d_mid_low[row * chip_tok : (row + 1) * chip_tok]
        if row == 1:
            out_part = dot_nt(hidden, down_full, BF)
            low_row, (part_out, out_part) = tie(low_row, (part_out, out_part))
        d_gated = dot_nn(low_row, out_full)
        d_attn, dl = gate_back(d_gated, tok_results[row], logits, row)
        if row == 0:
            d_attn, hidden = tie(d_attn, hidden)
        d_logit.append(dl)
        d_heads.append(exchange(d_attn))
    back = []
    for row in range(rows):
        grads = attend_back(packed[row], d_heads[row], results[row], logs[row], start[row : row + 1], low[row])
        back.append(exchange(grads))
    shard_out = scatter(part_out)
    back[1], down_sum = tie(back[1], down_sum)
    for row in range(rows):
        dpr, qs, ks = unpack_heads(back[row], proj, cos, sin, q_gain, k_gain, row, chips, chip_tok)
        d_proj.append(dpr)
        q_sum = q_sum + qs
        k_sum = k_sum + ks
    d_proj = jnp.concatenate(d_proj, axis=0)
    d_logit = jnp.concatenate(d_logit, axis=0)
    half = width // 2
    part_qkv = [dot_tn(d_proj, normed_a[:, a : a + half], BF) for a in (0, half)]
    part_qkv, (gu_sum, out_part, d_proj) = tie_all(part_qkv, (gu_sum, out_part, d_proj))
    trading = [Halving(p, dp, flip) for p, flip in zip(part_qkv, (False, True))]
    moved = [t.send() for t in trading]
    while trading[0].order:
        for t, m in zip(trading, moved):
            t.add(m)
        moved = [t.send() for t in trading]
    for t, m in zip(trading, moved):
        t.add(m)
    shard_qkv = [t.x for t in trading]
    output = (mid + scatter(out_part).astype(F32)).astype(BF).reshape(rows, tok, width)
    d_norm_part = (dot_nn(d_proj, qkv_full) + dot_nn(d_logit, gate_core)).astype(BF)
    d_norm_part = d_norm_part.reshape(rows, CORES, tok, width)
    d_norm_other = swap(pick(d_norm_part[:, 1], d_norm_part[:, 0]))
    d_normed_a = pick(d_norm_part[:, 0], d_norm_part[:, 1]).astype(F32) + d_norm_other.astype(F32)
    own_in = layer_input.astype(F32)
    own_factor = lax.rsqrt(jnp.mean(own_in * own_in, axis=-1, keepdims=True) + epsilon)
    part_attn = jnp.sum(d_normed_a * own_in * own_factor, axis=(0, 1))
    weighted_a = d_normed_a * attn_norm
    inner_a = jnp.mean(weighted_a * own_in, axis=-1, keepdims=True)
    grad_input = (
        d_mid.reshape(rows, tok, width) + own_factor * weighted_a - own_in * own_factor**3 * inner_a
    ).astype(BF)

    heads = jnp.concatenate([jnp.sum(q_sum, axis=0), jnp.sum(k_sum, axis=0)])
    heads = jnp.pad(heads, (0, width - heads.shape[0]))

    def norm_done(done):
        return [part_attn, grad_input]

    part_gate = dot_tn(d_logit, normed_a)[:CORE_Q]
    zero = jnp.zeros_like(part_gate)
    part_gate = jnp.stack(
        [pick(part_gate, zero).reshape(-1, GROUP, width), pick(zero, part_gate).reshape(-1, GROUP, width)], 1
    )
    part_gate = part_gate.reshape(QUERY_HEADS, width)
    small = jnp.concatenate([part_gate, part_ffn[None], part_attn[None], heads[None], jnp.zeros((5, width), F32)], axis=0)
    hops = [("dp", 1 << k) for k in range(dp.bit_length() - 1)] + [("seq", 1 << k) for k in range(seq.bit_length() - 1)]
    near = dp.bit_length()
    sums_at = [small]

    def hop(some):
        def work(done):
            x = sums_at[-1]
            for name, bit in some:
                x = x + lax.ppermute(x, name, [(p, p ^ bit) for p in range(lax.axis_size(name))])
            sums_at.append(x)
            return [x]

        return work


    mid_cut = down_sum.shape[1] // 2
    line = Line(chips, chip)
    keep = gu_sum[:quarter]
    sent = lax.ppermute(gu_sum[quarter:], "dp", trade)

    def join_early(done):
        down_done = jnp.concatenate(done[:2], axis=1)
        places = [unit_block.index(b) ^ me for b in range(dp)]
        return [
            join_units([keep, sent], [swap(keep), swap(sent)], core, upper.astype(jnp.int32)),
            join_blocks(down_done, swap(down_done), core, places),
        ]

    def join_late(done):
        return [join_cols([done[2]], [swap(done[2])], core, GROUP * HEAD), output]

    sums, ((_, grad_input), _, _, (small,), (grad_gu, grad_down), (grad_out, output)) = line.pipeline(
        [down_sum[:, :mid_cut], down_sum[:, mid_cut:], shard_out, *shard_qkv],
        {
            1: norm_done,
            2: hop(hops[:near]),
            3: hop(hops[near : near + 1]),
            4: hop(hops[near + 1 :]),
            5: join_early,
            6: join_late,
        },
    )
    grad_w_gate = lax.dynamic_slice_in_dim(small, me * gate_count, gate_count, 0)
    qkv_sum = sums[3:]
    grad_qkv = join_rows(qkv_sum, [swap(p) for p in qkv_sum], core, jnp.where(q_shard, GROUP, 1), HEAD)
    return (
        output,
        grad_input,
        small[QUERY_HEADS + 1],
        small[QUERY_HEADS + 2, :HEAD],
        small[QUERY_HEADS + 2, HEAD : 2 * HEAD],
        small[QUERY_HEADS],
        grad_qkv,
        grad_w_gate,
        grad_out,
        grad_gu,
        grad_down,
    )


def solution(mesh):
    token = P("dp", "seq", None)
    shard = P("dp", None)
    in_specs = (token, shard, P(), P(), P(), P(), shard, shard, shard, shard, shard, token)
    out_specs = (token, token, P(), P(), P(), P(), shard, shard, shard, shard, shard)
    return jax.shard_map(shards, mesh=mesh, in_specs=in_specs, out_specs=out_specs, check_vma=False)
```

```python
import functools
import math

import jax
import jax.numpy as jnp
from jax import lax
from jax.experimental import pallas as pl
from jax.experimental.pallas import tpu as pltpu
from jax.sharding import PartitionSpec as P

QUERY_HEADS = 16
KEY_VALUE_HEADS = 8
HEAD = 128
FF = 6144
CORES = 2

GROUP = QUERY_HEADS // KEY_VALUE_HEADS
CORE_Q = QUERY_HEADS // CORES
CORE_KV = KEY_VALUE_HEADS // CORES
epsilon = 1e-06
theta_base = 1000000.0
SCALE = 1.0 / math.sqrt(HEAD)
SCALE2 = SCALE * math.log2(math.e)
BF = jnp.bfloat16
F32 = jnp.float32


def dot_nt(left, right, out=F32):
    return lax.dot_general(left, right, (((1,), (1,)), ((), ())), preferred_element_type=F32).astype(out)


def dot_nn(left, right, out=F32):
    return lax.dot_general(left, right, (((1,), (0,)), ((), ())), preferred_element_type=F32).astype(out)


def dot_tn(left, right, out=F32):
    return lax.dot_general(left, right, (((0,), (0,)), ((), ())), preferred_element_type=F32).astype(out)


def doc_positions(lengths, total):
    ends = jnp.cumsum(lengths, axis=-1)
    starts = ends - lengths
    places = jnp.arange(total, dtype=jnp.int32)
    segment = jnp.sum((places[:, None] >= ends[..., None, :]).astype(jnp.int32), axis=-1)
    owners = segment[..., None] == jnp.arange(lengths.shape[-1], dtype=jnp.int32)
    first = jnp.sum(jnp.where(owners, starts[..., None, :], 0), axis=-1)
    return first, places - first


def pack_kernel(chips, proj_ref, cos_ref, sin_ref, qg_ref, kg_ref, out_ref):
    per = CORE_Q // chips
    copies = max(1, chips // CORE_KV)
    cos = cos_ref[...]
    sin = sin_ref[...]

    def head(index, gain):
        u = proj_ref[:, index * HEAD : (index + 1) * HEAD]
        factor = lax.rsqrt(jnp.mean(u * u, axis=-1, keepdims=True) + epsilon)
        n = u * factor * gain
        return (n * cos + pltpu.roll(n, HEAD // 2, 1) * sin).astype(BF)

    for z in range(chips):
        for h in range(per):
            out_ref[z, :, h * HEAD : (h + 1) * HEAD] = head(z * per + h, qg_ref[...])
        if z % copies == 0:
            kv = z // copies
            key = head(CORE_Q + kv, kg_ref[...])
            base = (CORE_Q + CORE_KV + kv) * HEAD
            value = proj_ref[:, base : base + HEAD].astype(BF)
        out_ref[z, :, per * HEAD : (per + 1) * HEAD] = key
        out_ref[z, :, (per + 1) * HEAD : (per + 2) * HEAD] = value


def pack_heads(proj, cos, sin, q_gain, k_gain, row, chips, chip_tok):
    per = CORE_Q // chips
    lanes = (per + 2) * HEAD
    block = min(256, chip_tok)
    steps = chip_tok // block
    width = proj.shape[1]
    tok = lambda i: (row * steps + i, 0)
    return pl.pallas_call(
        functools.partial(pack_kernel, chips),
        grid=(steps,),
        in_specs=[
            pl.BlockSpec((block, width), tok),
            pl.BlockSpec((block, HEAD), tok),
            pl.BlockSpec((block, HEAD), tok),
            pl.BlockSpec((1, HEAD), lambda i: (0, 0)),
            pl.BlockSpec((1, HEAD), lambda i: (0, 0)),
        ],
        out_specs=pl.BlockSpec((chips, block, lanes), lambda i: (0, i, 0)),
        out_shape=jax.ShapeDtypeStruct((chips, chip_tok, lanes), BF),
        name="pack_heads",
    )(proj, cos, sin, q_gain, k_gain)


def unpack_kernel(chips, grad_ref, proj_ref, cos_ref, sin_ref, qg_ref, kg_ref, out_ref, qs_ref, ks_ref):
    per = CORE_Q // chips
    copies = max(1, chips // CORE_KV)
    cos = cos_ref[...]
    sin = sin_ref[...]

    @pl.when(pl.program_id(0) == 0)
    def _():
        qs_ref[...] = jnp.zeros_like(qs_ref)
        ks_ref[...] = jnp.zeros_like(ks_ref)

    def head(e, index, gain, sum_ref):
        e = e * cos + pltpu.roll(e * sin, HEAD // 2, 1)
        u = proj_ref[:, index * HEAD : (index + 1) * HEAD]
        factor = lax.rsqrt(jnp.mean(u * u, axis=-1, keepdims=True) + epsilon)
        n = u * factor
        sum_ref[...] += jnp.sum((e * n).reshape(-1, 8, HEAD), axis=0)
        weighted = e * gain
        inner = jnp.mean(weighted * n, axis=-1, keepdims=True)
        out_ref[:, index * HEAD : (index + 1) * HEAD] = (factor * (weighted - n * inner)).astype(BF)

    def part(z, lane):
        return grad_ref[z, :, lane * HEAD : (lane + 1) * HEAD].astype(F32)

    for z in range(chips):
        for h in range(per):
            head(part(z, h), z * per + h, qg_ref[...], qs_ref)
    for kv in range(CORE_KV):
        spread = range(kv * copies, (kv + 1) * copies)
        head(sum(part(z, per) for z in spread), CORE_Q + kv, kg_ref[...], ks_ref)
        base = (CORE_Q + CORE_KV + kv) * HEAD
        out_ref[:, base : base + HEAD] = sum(part(z, per + 1) for z in spread).astype(BF)


def unpack_heads(grads, proj, cos, sin, q_gain, k_gain, row, chips, chip_tok):
    lanes = grads.shape[2]
    block = min(256, chip_tok)
    steps = chip_tok // block
    width = proj.shape[1]
    tok = lambda i: (row * steps + i, 0)
    small = pl.BlockSpec((8, HEAD), lambda i: (0, 0))
    return pl.pallas_call(
        functools.partial(unpack_kernel, chips),
        grid=(steps,),
        in_specs=[
            pl.BlockSpec((chips, block, lanes), lambda i: (0, i, 0)),
            pl.BlockSpec((block, width), tok),
            pl.BlockSpec((block, HEAD), tok),
            pl.BlockSpec((block, HEAD), tok),
            pl.BlockSpec((1, HEAD), lambda i: (0, 0)),
            pl.BlockSpec((1, HEAD), lambda i: (0, 0)),
        ],
        out_specs=[pl.BlockSpec((block, width), lambda i: (i, 0)), small, small],
        out_shape=[
            jax.ShapeDtypeStruct((chip_tok, width), BF),
            jax.ShapeDtypeStruct((8, HEAD), F32),
            jax.ShapeDtypeStruct((8, HEAD), F32),
        ],
        name="unpack_heads",
    )(grads, proj, cos, sin, q_gain, k_gain)


def visible(j, size, start, diagonal):
    inner = lax.broadcasted_iota(jnp.int32, (size, size), 0)
    allowed = inner >= start - j * size
    if diagonal:
        allowed = allowed & (inner <= lax.broadcasted_iota(jnp.int32, (size, size), 1))
    return allowed


def attend_kernel(per, low_ref, q_ref, k_ref, v_ref, start_ref, out_ref, log_ref, acc_ref, sum_ref):
    i = pl.program_id(0)
    size = q_ref.shape[1]
    start = start_ref[...]
    acc_ref[...] = jnp.zeros_like(acc_ref)
    sum_ref[...] = jnp.zeros_like(sum_ref)

    def one(j, diagonal):
        key = k_ref[j]
        value = v_ref[j]
        allowed = visible(j, size, start, diagonal)
        for h in range(per):
            scores = dot_nt(key, q_ref[0, :, h * HEAD : (h + 1) * HEAD])
            p = jnp.where(allowed, jnp.exp2(scores * SCALE2), 0.0)
            sum_ref[h : h + 1, :] += jnp.sum(p, axis=0, keepdims=True)
            acc_ref[h] += dot_tn(value, p.astype(BF))

    def step(j, carry):
        one(j, False)
        return carry

    lax.fori_loop(low_ref[i], i, step, 0)
    one(i, True)
    for h in range(per):
        total = sum_ref[h : h + 1, :]
        out_ref[0, :, h * HEAD : (h + 1) * HEAD] = (acc_ref[h] / total).T.astype(BF)
        log_ref[h : h + 1, :] = jnp.log2(total)


def attend(packed, start, low):
    chips, size, lanes = packed.shape
    per = lanes // HEAD - 2
    return pl.pallas_call(
        functools.partial(attend_kernel, per),
        grid_spec=pltpu.PrefetchScalarGridSpec(
            num_scalar_prefetch=1,
            grid=(chips,),
            in_specs=[
                pl.BlockSpec((1, size, per * HEAD), lambda i, low: (i, 0, 0)),
                pl.BlockSpec((chips, size, HEAD), lambda i, low: (0, 0, per)),
                pl.BlockSpec((chips, size, HEAD), lambda i, low: (0, 0, per + 1)),
                pl.BlockSpec((1, size), lambda i, low: (0, i)),
            ],
            out_specs=[
                pl.BlockSpec((1, size, per * HEAD), lambda i, low: (i, 0, 0)),
                pl.BlockSpec((per, size), lambda i, low: (0, i)),
            ],
            scratch_shapes=[pltpu.VMEM((per, HEAD, size), F32), pltpu.VMEM((per, size), F32)],
        ),
        out_shape=[
            jax.ShapeDtypeStruct((chips, size, per * HEAD), BF),
            jax.ShapeDtypeStruct((per, chips * size), F32),
        ],
        name="attend",
    )(low, packed, packed, packed, start)


def attend_back_kernel(
    per, low_ref, q_ref, k_ref, v_ref, grad_ref, res_ref, log_ref, start_ref, out_ref, dq_ref, dk_ref, dv_ref
):
    i = pl.program_id(0)
    size = q_ref.shape[1]
    start = start_ref[...]

    @pl.when(i == 0)
    def _():
        dk_ref[...] = jnp.zeros_like(dk_ref)
        dv_ref[...] = jnp.zeros_like(dv_ref)

    dq_ref[...] = jnp.zeros_like(dq_ref)
    ones = jnp.ones((8, HEAD), F32)
    inner = []
    for h in range(per):
        cols = slice(h * HEAD, (h + 1) * HEAD)
        both = grad_ref[0, :, cols].astype(F32) * res_ref[0, :, cols].astype(F32)
        sums = lax.dot_general(
            ones, both, (((1,), (1,)), ((), ())), precision=lax.Precision.HIGHEST, preferred_element_type=F32
        )
        inner.append(sums[0:1, :])

    def one(j, diagonal):
        key = k_ref[j]
        value = v_ref[j]
        allowed = visible(j, size, start, diagonal)
        for h in range(per):
            query = q_ref[0, :, h * HEAD : (h + 1) * HEAD]
            grad = grad_ref[0, :, h * HEAD : (h + 1) * HEAD]
            scores = dot_nt(key, query)
            p = jnp.where(allowed, jnp.exp2(scores * SCALE2 - log_ref[h : h + 1, :]), 0.0)
            dp = dot_nt(value, grad)
            ds = (p * (dp - inner[h])).astype(BF)
            dv_ref[j] += dot_nn(p.astype(BF), grad)
            dk_ref[j] += dot_nn(ds, query)
            dq_ref[h] += dot_tn(ds, key)

    def step(j, carry):
        one(j, False)
        return carry

    lax.fori_loop(low_ref[i], i, step, 0)
    one(i, True)
    for h in range(per):
        out_ref[i, :, h * HEAD : (h + 1) * HEAD] = (dq_ref[h] * SCALE).astype(BF)

    @pl.when(i == pl.num_programs(0) - 1)
    def _():
        out_ref[:, :, per * HEAD : (per + 1) * HEAD] = (dk_ref[...] * SCALE).astype(BF)
        out_ref[:, :, (per + 1) * HEAD : (per + 2) * HEAD] = dv_ref[...].astype(BF)


def attend_back(packed, grad, result, logs, start, low):
    chips, size, lanes = packed.shape
    per = lanes // HEAD - 2
    one = pl.BlockSpec((1, size, per * HEAD), lambda i, low: (i, 0, 0))
    return pl.pallas_call(
        functools.partial(attend_back_kernel, per),
        grid_spec=pltpu.PrefetchScalarGridSpec(
            num_scalar_prefetch=1,
            grid=(chips,),
            in_specs=[
                one,
                pl.BlockSpec((chips, size, HEAD), lambda i, low: (0, 0, per)),
                pl.BlockSpec((chips, size, HEAD), lambda i, low: (0, 0, per + 1)),
                one,
                one,
                pl.BlockSpec((per, size), lambda i, low: (0, i)),
                pl.BlockSpec((1, size), lambda i, low: (0, i)),
            ],
            out_specs=pl.BlockSpec((chips, size, lanes), lambda i, low: (0, 0, 0)),
            scratch_shapes=[
                pltpu.VMEM((per, size, HEAD), F32),
                pltpu.VMEM((chips, size, HEAD), F32),
                pltpu.VMEM((chips, size, HEAD), F32),
            ],
        ),
        out_shape=jax.ShapeDtypeStruct((chips, size, lanes), BF),
        name="attend_back",
    )(low, packed, packed, packed, grad, result, logs, start)


def gate_kernel(res_ref, logit_ref, out_ref):
    chips, _, lanes = res_ref.shape
    per = lanes // HEAD
    sig = jax.nn.sigmoid(logit_ref[...])
    for z in range(chips):
        for h in range(per):
            head = z * per + h
            value = res_ref[z, :, h * HEAD : (h + 1) * HEAD].astype(F32)
            out_ref[:, head * HEAD : (head + 1) * HEAD] = (value * sig[:, head : head + 1]).astype(BF)


def gate_rows(result, logits, row):
    chips, size, lanes = result.shape
    block = min(256, size)
    steps = size // block
    return pl.pallas_call(
        gate_kernel,
        grid=(steps,),
        in_specs=[
            pl.BlockSpec((chips, block, lanes), lambda i: (0, i, 0)),
            pl.BlockSpec((block, HEAD), lambda i: (row * steps + i, 0)),
        ],
        out_specs=pl.BlockSpec((block, chips * lanes), lambda i: (i, 0)),
        out_shape=jax.ShapeDtypeStruct((size, chips * lanes), BF),
        name="gate_rows",
    )(result, logits)


def gate_back_kernel(grad_ref, res_ref, logit_ref, out_ref, dlogit_ref):
    chips, size, lanes = res_ref.shape
    per = lanes // HEAD
    sig = jax.nn.sigmoid(logit_ref[...])
    lane = lax.broadcasted_iota(jnp.int32, sig.shape, 1)
    sums = jnp.zeros(sig.shape, F32)
    for z in range(chips):
        for h in range(per):
            head = z * per + h
            e = grad_ref[:, head * HEAD : (head + 1) * HEAD]
            value = res_ref[z, :, h * HEAD : (h + 1) * HEAD].astype(F32)
            out_ref[z, :, h * HEAD : (h + 1) * HEAD] = (e * sig[:, head : head + 1]).astype(BF)
            sums = jnp.where(lane == head, jnp.sum(e * value, axis=-1, keepdims=True), sums)
    dlogit_ref[...] = (sums * sig * (1.0 - sig)).astype(BF)


def gate_back(grad, result, logits, row):
    chips, size, lanes = result.shape
    block = min(256, size)
    steps = size // block
    return pl.pallas_call(
        gate_back_kernel,
        grid=(steps,),
        in_specs=[
            pl.BlockSpec((block, chips * lanes), lambda i: (i, 0)),
            pl.BlockSpec((chips, block, lanes), lambda i: (0, i, 0)),
            pl.BlockSpec((block, HEAD), lambda i: (row * steps + i, 0)),
        ],
        out_specs=[
            pl.BlockSpec((chips, block, lanes), lambda i: (0, i, 0)),
            pl.BlockSpec((block, HEAD), lambda i: (i, 0)),
        ],
        out_shape=[jax.ShapeDtypeStruct((chips, size, lanes), BF), jax.ShapeDtypeStruct((size, HEAD), BF)],
        name="gate_back",
    )(grad, result, logits)


def join_rows_kernel(count, which_ref, *refs):
    out_ref = refs[2 * count]
    size = refs[0].shape[1]
    own_half = pl.program_id(0) == which_ref[0]

    def put(parts):
        for k in range(count):
            out_ref[:, k * size : (k + 1) * size] = parts[k][...].astype(F32)

    pl.when(own_half)(lambda: put(refs[:count]))
    pl.when(jnp.logical_not(own_half))(lambda: put(refs[count : 2 * count]))


def join_rows(mine, other, core, blocks, block):
    count = len(mine)
    height, size = mine[0].shape
    steps = height // block

    def source(side):
        def index(h, i, which):
            active = (h == which[0]) if side == 0 else (h != which[0])
            return (jnp.where(active, i, jnp.where(h == 0, 0, steps - 1)), 0)

        return pl.BlockSpec((block, size), index)

    def target(h, i, which):
        per = which[1]
        return ((i // per) * 2 * per + h * per + i % per, 0)

    return pl.pallas_call(
        functools.partial(join_rows_kernel, count),
        grid_spec=pltpu.PrefetchScalarGridSpec(
            num_scalar_prefetch=1,
            grid=(CORES, steps),
            in_specs=[source(0)] * count + [source(1)] * count,
            out_specs=pl.BlockSpec((block, count * size), target),
        ),
        out_shape=jax.ShapeDtypeStruct((CORES * height, count * size), F32),
        name="join_rows",
    )(jnp.stack([core, blocks.astype(jnp.int32)]), *mine, *other)


def join_cols_kernel(count, per, which_ref, *refs):
    out_ref = refs[2 * count]
    u = pl.program_id(0)
    own_half = pl.program_id(1) == which_ref[0]

    def put(ref):
        out_ref[...] = ref[...].astype(F32)

    for k in range(count):
        here = u // per == k
        pl.when(here & own_half)(functools.partial(put, refs[k]))
        pl.when(here & jnp.logical_not(own_half))(functools.partial(put, refs[count + k]))


def join_cols(mine, other, core, unit):
    count = len(mine)
    height, size = mine[0].shape
    per = size // unit

    def source(k):
        return pl.BlockSpec((height, unit), lambda u, h, which: (0, jnp.clip(u - k * per, 0, per - 1)))

    sources = [source(k) for k in range(count)]
    return pl.pallas_call(
        functools.partial(join_cols_kernel, count, per),
        grid_spec=pltpu.PrefetchScalarGridSpec(
            num_scalar_prefetch=1,
            grid=(count * per, CORES),
            in_specs=sources + sources,
            out_specs=pl.BlockSpec((height, unit), lambda u, h, which: (0, u * CORES + h)),
        ),
        out_shape=jax.ShapeDtypeStruct((height, CORES * count * size), F32),
        name="join_cols",
    )(core[None], *mine, *other)


def join_units_kernel(which_ref, keep_ref, keep_other_ref, sent_ref, sent_other_ref, out_ref):
    kept = pl.program_id(0) == which_ref[1]
    mine = pl.program_id(1) == which_ref[0]
    for side, pair in ((True, (keep_ref, keep_other_ref)), (False, (sent_ref, sent_other_ref))):
        for here, ref in ((True, pair[0]), (False, pair[1])):

            @pl.when((kept == side) & (mine == here))
            def _(ref=ref):
                out_ref[...] = ref[...].astype(F32)


def join_units(mine, other, core, upper):
    height, width = mine[0].shape
    block = 256
    steps = height // block
    sources = []
    for side in (0, 1):
        for half in (0, 1):

            def index(p, h, i, which, side=side, half=half):
                at_side = (p == which[1]) if side == 0 else (p != which[1])
                at_half = (h == which[0]) if half == 0 else (h != which[0])
                side_p = which[1] if side == 0 else 1 - which[1]
                side_h = which[0] if half == 0 else 1 - which[0]
                before = (p * 2 + h) < (side_p * 2 + side_h)
                return (jnp.where(at_side & at_half, i, jnp.where(before, 0, steps - 1)), 0)

            sources.append(pl.BlockSpec((block, width), index))
    return pl.pallas_call(
        join_units_kernel,
        grid_spec=pltpu.PrefetchScalarGridSpec(
            num_scalar_prefetch=1,
            grid=(2, CORES, steps),
            in_specs=sources,
            out_specs=pl.BlockSpec((block, width), lambda p, h, i, which: ((p * CORES + h) * steps + i, 0)),
        ),
        out_shape=jax.ShapeDtypeStruct((2 * CORES * height, width), F32),
        name="join_units",
    )(jnp.stack([core, upper]), mine[0], other[0], mine[1], other[1])


def join_blocks_kernel(which_ref, mine_ref, other_ref, out_ref):
    own_half = pl.program_id(0) == which_ref[0]
    for here, ref in ((True, mine_ref), (False, other_ref)):

        @pl.when(own_half == here)
        def _(ref=ref):
            out_ref[...] = ref[0].astype(F32)


def join_blocks(mine, other, core, order):
    count, height, size = mine.shape
    source = pl.BlockSpec((1, height, size), lambda h, b, which, where: (where[b], 0, 0))
    return pl.pallas_call(
        lambda which_ref, where_ref, *refs: join_blocks_kernel(which_ref, *refs),
        grid_spec=pltpu.PrefetchScalarGridSpec(
            num_scalar_prefetch=2,
            grid=(CORES, count),
            in_specs=[source, source],
            out_specs=pl.BlockSpec((height, size), lambda h, b, which, where: (h, b)),
        ),
        out_shape=jax.ShapeDtypeStruct((CORES * height, count * size), F32),
        name="join_blocks",
    )(core[None], jnp.stack(order).astype(jnp.int32), mine, other)


class Halving:
    def __init__(self, x, dp, flip):
        self.dp = dp
        self.mine = lax.axis_index("dp")
        bits = dp.bit_length() - 1
        self.left = list(range(bits))
        self.order = self.left[::-1] if flip else self.left[:]
        self.x = x.reshape((2,) * bits + (x.shape[0] // dp, x.shape[1]))

    def send(self):
        bit = self.order.pop(0)
        axis = sum(1 for b in self.left if b > bit)
        self.left.remove(bit)
        low, high = lax.index_in_dim(self.x, 0, axis, False), lax.index_in_dim(self.x, 1, axis, False)
        mark = (self.mine >> bit) % 2 == 1
        pairs = [(d, d ^ (1 << bit)) for d in range(self.dp)]
        self.keep = jnp.where(mark, high, low)
        return lax.ppermute(jnp.where(mark, low, high), "dp", pairs)

    def add(self, moved):
        self.x = self.keep + moved


class Line:
    def __init__(self, chips, chip):
        self.chips = chips
        self.inner = (chip == 1) | (chip == 2)
        ends = lambda pairs: [(a * CORES + c, b * CORES + c) for a, b in pairs for c in range(CORES)]
        self.stages = [ends([(0, 1), (3, 2)]), ends([(1, 2), (2, 1)]), ends([(1, 0), (2, 3)])]
        self.groups = [[z * CORES + c for z in range(chips)] for c in range(CORES)]

    def send(self, x, stage):
        if self.chips != 4:
            return (x, lax.psum(x, "seq", axis_index_groups=self.groups) if stage == 0 else x)
        return (x, lax.ppermute(x, "seq", self.stages[stage]))

    def begin(self, x):
        return (0,) + self.send(x, 0)

    def next(self, state):
        stage, x, moved = state
        if self.chips != 4:
            return (stage + 1, moved, moved)
        return (stage + 1,) + self.send(x + moved, stage + 1)

    def end(self, state):
        stage, x, moved = state
        return moved if self.chips != 4 else jnp.where(self.inner, x, moved)

    def pipeline(self, parts, fillers):
        if self.chips != 4:
            done = lax.psum(parts, "seq", axis_index_groups=self.groups)
            made = []
            for filler in fillers.values():
                made.append(filler(done, made))
            return done, made
        count = len(parts)
        states = [None] * count
        made = []
        for step in range(count + 2):
            for k in range(count):
                if k == step:
                    states[k] = self.begin(parts[k])
                elif k < step <= k + 2:
                    states[k] = self.next(states[k])
            done = [self.end(states[k]) if k + 3 <= step else None for k in range(count)]
            extra = fillers[step](done, made) if step in fillers else []
            live = [k for k in range(count) if states[k] is not None]
            later = [k for k in range(step + 1, min(step + 2, count))]
            moved, extra = lax.optimization_barrier(
                ([states[k][1:] for k in live] + [parts[k] for k in later], extra)
            )
            if step in fillers:
                made.append(extra)
            for k, value in zip(live + later, moved):
                if k in later:
                    parts[k] = value
                else:
                    states[k] = (states[k][0], *value)
        return [self.end(state) for state in states], made


def tie_all(values, work):
    return lax.optimization_barrier((values, work))


def tie(value, work):
    leaves, tree = jax.tree.flatten(work)
    moving = [x for x in leaves if not isinstance(x, int)]
    value, *moving = lax.optimization_barrier((value, *moving))
    moving = iter(moving)
    return value, jax.tree.unflatten(tree, [x if isinstance(x, int) else next(moving) for x in leaves])


def shards(
    layer_input,
    doc_lengths,
    attn_norm,
    q_norm,
    k_norm,
    ffn_norm,
    w_qkv,
    w_gate,
    w_out,
    w_gu,
    w_down,
    cotangent,
):
    rows, tok, width = layer_input.shape
    seq = lax.axis_size("seq")
    dp = lax.axis_size("dp")
    chips = seq // CORES
    place = lax.axis_index("seq")
    core = place % CORES
    chip = place // CORES
    first = core == 0
    chip_tok = tok * CORES
    length = tok * seq
    tokens = rows * chip_tok
    pair = [(s, s ^ 1) for s in range(seq)]
    groups = [[z * CORES + c for z in range(chips)] for c in range(CORES)]
    q_shard = lax.axis_index("dp") * w_qkv.shape[0] < QUERY_HEADS * HEAD

    def swap(x):
        return lax.ppermute(x, "seq", pair)

    def pick(a, b):
        return jnp.where(first, a, b)

    def both(x):
        other = swap(x)
        return jnp.concatenate([pick(x, other), pick(other, x)], axis=1).reshape(tokens, width)

    def exchange(x):
        return lax.all_to_all(x, "seq", 0, 0, axis_index_groups=groups, tiled=True)

    def total_sum(x, names=("seq", "dp")):
        for name in names:
            size = lax.axis_size(name)
            step = 1
            while step < size:
                x = x + lax.ppermute(x, name, [(s, s ^ step) for s in range(size)])
                step *= 2
        return x

    def scatter(x):
        return lax.psum_scatter(x, "dp", scatter_dimension=0, tiled=True)

    def gather(x):
        return lax.all_gather(x, "dp", axis=0, tiled=True)

    def core_rows(w, unit):
        return jnp.concatenate(
            [pick(w[a : a + unit], w[a + unit : a + 2 * unit]) for a in range(0, w.shape[0], 2 * unit)], axis=0
        )

    def core_cols(w, unit):
        return jnp.concatenate(
            [pick(w[:, a : a + unit], w[:, a + unit : a + 2 * unit]) for a in range(0, w.shape[1], 2 * unit)],
            axis=1,
        )

    def trade_blocks(x):
        mine = lax.axis_index("dp")
        found = [(mine, lax.dynamic_index_in_dim(x, mine, 0, keepdims=False))]
        for k in range(1, dp):
            out = lax.dynamic_index_in_dim(x, mine ^ k, 0, keepdims=False)
            found.append((mine ^ k, lax.ppermute(out, "dp", [(d, d ^ k) for d in range(dp)])))
        return found

    half_dp = dp // 2
    me = lax.axis_index("dp")
    upper = me >= half_dp
    trade = [(d, d ^ half_dp) for d in range(dp)]
    units = w_gu.shape[0] // 2
    owned = rows * tok

    qkv_half = jnp.where(q_shard, core_rows(w_qkv, GROUP * HEAD), core_rows(w_qkv, HEAD))
    qkv_full = gather(qkv_half)
    out_full = gather(core_cols(w_out, GROUP * HEAD))
    ctg = cotangent.reshape(owned, width)
    gate_count = w_gate.shape[0]
    gate_full = lax.dynamic_update_slice_in_dim(jnp.zeros((QUERY_HEADS, width), BF), w_gate, me * gate_count, 0)
    gate_full = total_sum(gate_full, ("dp",))
    gate_core = jnp.pad(core_rows(gate_full, GROUP), ((0, HEAD - CORE_Q), (0, 0)))

    gu_keep = jnp.where(upper, w_gu[units:], w_gu[:units])
    quarter = units // 2
    gu_send = jnp.where(
        upper, pick(w_gu[:quarter], w_gu[quarter:units]), pick(w_gu[units : units + quarter], w_gu[units + quarter :])
    )
    out_rows = w_down.shape[0] // 2
    down_core = pick(w_down[:out_rows], w_down[out_rows:])
    unit_block = [(d % half_dp) * 2 + d // half_dp for d in range(dp)]
    down_send = jnp.stack([down_core[:, b * units : (b + 1) * units] for b in unit_block])
    (qkv_full, gu_send, down_send) = lax.optimization_barrier((qkv_full, gu_send, down_send))
    gu_pair = lax.all_gather(gu_send, "dp", axis_index_groups=[[d, d + half_dp] for d in range(half_dp)])
    gu_half = jnp.where(upper, gu_pair[0], gu_pair[1])
    down_half = jnp.zeros_like(down_send)
    for other, moved in trade_blocks(down_send):
        down_half = lax.dynamic_update_index_in_dim(down_half, moved, other, 0)

    start, position = doc_positions(doc_lengths, length)
    low = start.reshape(rows, chips, chip_tok)[:, :, 0] // chip_tok
    local = lax.dynamic_slice_in_dim(position, chip * chip_tok, chip_tok, 1).reshape(tokens)
    freq = jnp.power(theta_base, -(jnp.arange(HEAD // 2, dtype=F32) * 2.0) / HEAD)
    angle = local.astype(F32)[:, None] * freq
    cos = jnp.cos(angle)
    sin = jnp.sin(angle)
    cos = jnp.concatenate([cos, cos], axis=1)
    sin = jnp.concatenate([-sin, sin], axis=1)

    inputs = both(layer_input).astype(F32)
    factor_a = lax.rsqrt(jnp.mean(inputs * inputs, axis=-1, keepdims=True) + epsilon)
    normed_a = (inputs * factor_a * attn_norm).astype(BF)
    logits = dot_nt(normed_a, gate_core)
    proj = dot_nt(normed_a, qkv_full)
    q_gain = q_norm[None, :]
    k_gain = k_norm[None, :]

    packed, results, logs, gated, mid = [], [], [], [], []
    for row in range(rows):
        cos_row = cos
        if row:
            cos_row, logits = tie(cos, logits)
        packed.append(exchange(pack_heads(proj, cos_row, sin, q_gain, k_gain, row, chips, chip_tok)))
    packed[0], down_half = tie(packed[0], down_half)
    packed[-1], ctg_late = tie(packed[-1], ctg)
    ctg_all = gather(ctg_late)
    for row in range(rows):
        head_out, log = attend(packed[row], start[row : row + 1], low[row])
        results.append(head_out)
        logs.append(log)
    tok_results = [exchange(r) for r in results]
    gu_other = swap(gu_half)
    down_other = swap(down_half)
    for row in range(rows):
        gated.append(gate_rows(tok_results[row], logits, row))
        part = dot_nt(gated[row], out_full, BF).reshape(CORES, tok, width)
        other = swap(pick(part[1], part[0]))
        mid.append(layer_input[row].astype(F32) + pick(part[0], part[1]).astype(F32) + other.astype(F32))
    mid = jnp.concatenate(mid, axis=0)
    gated = jnp.concatenate(gated, axis=0)

    factor_f = lax.rsqrt(jnp.mean(mid * mid, axis=-1, keepdims=True) + epsilon)
    normed_f = (mid * factor_f * ffn_norm).astype(BF)
    normed_all = gather(normed_f)
    gu_recv = jnp.concatenate([pick(gu_half, gu_other), pick(gu_other, gu_half)], axis=0)
    down_full = jnp.concatenate([pick(down_half, down_other), pick(down_other, down_half)], axis=1)
    down_full = down_full.reshape(width, units)
    d_hidden = dot_nn(ctg_all, down_full, BF)
    normed_all, (d_hidden, gu_recv) = tie(normed_all, (d_hidden, gu_recv))
    keep_part = dot_nt(normed_all, gu_keep, BF)
    recv_part = dot_nt(normed_all, gu_recv, BF)
    gate_part = jnp.where(upper, recv_part, keep_part).astype(F32)
    up_part = jnp.where(upper, keep_part, recv_part).astype(F32)
    d_hid = d_hidden.astype(F32)
    gate_act = jax.nn.sigmoid(gate_part)
    silu = gate_part * gate_act
    hidden = (silu * up_part).astype(BF)
    d_gate = d_hid * up_part * gate_act * (1.0 + gate_part * (1.0 - gate_act))
    d_up = d_hid * silu
    d_keep = jnp.where(upper, d_up, d_gate).astype(BF)
    d_recv = jnp.where(upper, d_gate, d_up).astype(BF)
    d_normed = scatter((dot_nn(d_keep, gu_keep) + dot_nn(d_recv, gu_recv)).astype(BF))

    part_keep = dot_tn(d_keep, normed_all, BF)
    part_recv = dot_tn(d_recv, normed_all, BF)
    part_down = dot_tn(ctg_all, hidden, BF).reshape(dp, CORES, out_rows, units)
    keep_swap = swap(pick(part_keep[quarter:], part_keep[:quarter]))
    recv_swap = swap(pick(part_recv[quarter:], part_recv[:quarter]))
    down_swap = swap(pick(part_down[:, 1], part_down[:, 0]))
    d_normed, (part_keep, part_recv, part_down, keep_swap, recv_swap) = tie(
        d_normed, (part_keep, part_recv, part_down, keep_swap, recv_swap)
    )
    keep_sum = pick(part_keep[:quarter], part_keep[quarter:]) + keep_swap
    recv_sum = pick(part_recv[:quarter], part_recv[quarter:]) + recv_swap
    d_normed, gu_sum = tie(d_normed, jnp.concatenate([keep_sum, recv_sum], axis=0))
    third = gu_sum.shape[0] // 3
    gu_first = lax.psum(gu_sum[:third], "seq", axis_index_groups=groups)
    gu_sum = gu_sum[third:]

    d_normed = d_normed.astype(F32)
    part_ffn = jnp.sum(d_normed * mid * factor_f, axis=0)
    weighted = d_normed * ffn_norm
    inner = jnp.mean(weighted * mid, axis=-1, keepdims=True)
    d_mid = ctg.astype(F32) + factor_f * weighted - mid * factor_f**3 * inner
    low_mine = d_mid.astype(BF).reshape(rows, tok, width)
    low_other = swap(low_mine)
    low_other, down_swap = tie(low_other, down_swap)
    down_sum = pick(part_down[:, 0], part_down[:, 1]) + down_swap
    down_sum = jnp.stack([moved for _, moved in trade_blocks(down_sum)])

    d_mid_low = jnp.concatenate([pick(low_mine, low_other), pick(low_other, low_mine)], axis=1).reshape(tokens, width)
    part_out = dot_tn(d_mid_low, gated, BF)
    d_proj, d_logit, d_heads = [], [], []
    q_sum = 0.0
    k_sum = 0.0
    for row in range(rows):
        low_row = d_mid_low[row * chip_tok : (row + 1) * chip_tok]
        if row == 1:
            out_part = dot_nt(hidden, down_full, BF)
            low_row, (part_out, out_part) = tie(low_row, (part_out, out_part))
        d_gated = dot_nn(low_row, out_full)
        d_attn, dl = gate_back(d_gated, tok_results[row], logits, row)
        if row == 0:
            d_attn, hidden = tie(d_attn, hidden)
        d_logit.append(dl)
        d_heads.append(exchange(d_attn))
    d_heads[0], (gu_first, gu_sum) = tie(d_heads[0], (gu_first, gu_sum))
    gu_sum = lax.psum(gu_sum, "seq", axis_index_groups=groups)
    back = []
    for row in range(rows):
        grads = attend_back(packed[row], d_heads[row], results[row], logs[row], start[row : row + 1], low[row])
        back.append(exchange(grads))
    shard_out = scatter(part_out)
    back[1], down_sum = tie(back[1], down_sum)
    for row in range(rows):
        dpr, qs, ks = unpack_heads(back[row], proj, cos, sin, q_gain, k_gain, row, chips, chip_tok)
        d_proj.append(dpr)
        q_sum = q_sum + qs
        k_sum = k_sum + ks
    d_proj = jnp.concatenate(d_proj, axis=0)
    d_logit = jnp.concatenate(d_logit, axis=0)
    half = width // 2
    part_qkv = [dot_tn(d_proj, normed_a[:, a : a + half], BF) for a in (0, half)]
    part_qkv, (gu_sum, out_part, d_proj, down_sum) = tie_all(part_qkv, (gu_sum, out_part, d_proj, down_sum))
    trading = [Halving(p, dp, flip) for p, flip in zip(part_qkv, (False, True))]
    moved = [t.send() for t in trading]
    while trading[0].order:
        for t, m in zip(trading, moved):
            t.add(m)
        moved = [t.send() for t in trading]
    for t, m in zip(trading, moved):
        t.add(m)
    shard_qkv = [t.x for t in trading]
    d_norm_part = (dot_nn(d_proj, qkv_full) + dot_nn(d_logit, gate_core)).astype(BF)
    d_norm_part = d_norm_part.reshape(rows, CORES, tok, width)
    d_norm_other = swap(pick(d_norm_part[:, 1], d_norm_part[:, 0]))
    d_normed_a = pick(d_norm_part[:, 0], d_norm_part[:, 1]).astype(F32) + d_norm_other.astype(F32)
    own_in = layer_input.astype(F32)
    own_factor = lax.rsqrt(jnp.mean(own_in * own_in, axis=-1, keepdims=True) + epsilon)
    part_attn = jnp.sum(d_normed_a * own_in * own_factor, axis=(0, 1))
    weighted_a = d_normed_a * attn_norm
    inner_a = jnp.mean(weighted_a * own_in, axis=-1, keepdims=True)
    grad_input = (
        d_mid.reshape(rows, tok, width) + own_factor * weighted_a - own_in * own_factor**3 * inner_a
    ).astype(BF)

    heads = jnp.concatenate([jnp.sum(q_sum, axis=0), jnp.sum(k_sum, axis=0)])
    heads = jnp.pad(heads, (0, width - heads.shape[0]))

    def norm_done(done, made):
        return [part_attn, grad_input]

    part_gate = dot_tn(d_logit, normed_a)[:CORE_Q]
    zero = jnp.zeros_like(part_gate)
    part_gate = jnp.stack(
        [pick(part_gate, zero).reshape(-1, GROUP, width), pick(zero, part_gate).reshape(-1, GROUP, width)], 1
    )
    part_gate = part_gate.reshape(QUERY_HEADS, width)
    small = jnp.concatenate([part_gate, part_ffn[None], part_attn[None], heads[None], jnp.zeros((5, width), F32)], axis=0)
    hops = [("seq", 1)] + [("dp", 1 << k) for k in range(dp.bit_length() - 1)]
    mid_cut = down_sum.shape[1] // 2
    parts = [down_sum[:, :mid_cut], down_sum[:, mid_cut:], shard_out, *shard_qkv]

    def hop(x, some):
        for name, bit in some:
            x = x + lax.ppermute(x, name, [(p, p ^ bit) for p in range(lax.axis_size(name))])
        return x

    def near_sum(done, made):
        return [hop(small, hops[:2]), out_part]

    def far_sum(done, made):
        total = hop(made[-1][0], hops[2:])
        if chips == 4:
            wide = total.astype(BF)
            parts[4] = jnp.concatenate([parts[4], wide[:, :half], wide[:, half:]], axis=0)
        else:
            total = lax.psum(total, "seq", axis_index_groups=groups)
        return [total, made[-1][1]]

    line = Line(chips, chip)
    keep = jnp.concatenate([gu_first, gu_sum[: quarter - third]], axis=0)
    sent = lax.ppermute(gu_sum[quarter - third :], "dp", trade)

    def join_early(done, made):
        down_done = jnp.concatenate(done[:2], axis=1)
        places = [unit_block.index(b) ^ me for b in range(dp)]
        return [
            join_units([keep, sent], [swap(keep), swap(sent)], core, upper.astype(jnp.int32)),
            join_blocks(down_done, swap(down_done), core, places),
        ]

    def join_late(done, made):
        output = (mid + scatter(made[2][1]).astype(F32)).astype(BF).reshape(rows, tok, width)
        return [join_cols([done[2]], [swap(done[2])], core, GROUP * HEAD), output]

    sums, ((_, grad_input), _, (small, _), (grad_gu, grad_down), (grad_out, output)) = line.pipeline(
        parts, {1: norm_done, 2: near_sum, 3: far_sum, 5: join_early, 6: join_late}
    )
    if chips == 4:
        body = shard_qkv[0].shape[0]
        count = (sums[4].shape[0] - body) // 2
        small = jnp.concatenate([sums[4][body : body + count], sums[4][body + count :]], axis=1).astype(F32)
    grad_w_gate = lax.dynamic_slice_in_dim(small, me * gate_count, gate_count, 0)
    qkv_sum = sums[3:]
    grad_qkv = join_rows(qkv_sum, [swap(p) for p in qkv_sum], core, jnp.where(q_shard, GROUP, 1), HEAD)
    return (
        output,
        grad_input,
        small[QUERY_HEADS + 1],
        small[QUERY_HEADS + 2, :HEAD],
        small[QUERY_HEADS + 2, HEAD : 2 * HEAD],
        small[QUERY_HEADS],
        grad_qkv,
        grad_w_gate,
        grad_out,
        grad_gu,
        grad_down,
    )


def solution(mesh):
    token = P("dp", "seq", None)
    shard = P("dp", None)
    in_specs = (token, shard, P(), P(), P(), P(), shard, shard, shard, shard, shard, token)
    out_specs = (token, token, P(), P(), P(), P(), shard, shard, shard, shard, shard)
    return jax.shard_map(shards, mesh=mesh, in_specs=in_specs, out_specs=out_specs, check_vma=False)
```

```python
import functools
import math

import jax
import jax.numpy as jnp
from jax import lax
from jax.experimental import pallas as pl
from jax.experimental.pallas import tpu as pltpu
from jax.sharding import PartitionSpec as P

QUERY_HEADS = 16
KEY_VALUE_HEADS = 8
HEAD = 128
FF = 6144
CORES = 2

GROUP = QUERY_HEADS // KEY_VALUE_HEADS
CORE_Q = QUERY_HEADS // CORES
CORE_KV = KEY_VALUE_HEADS // CORES
epsilon = 1e-06
theta_base = 1000000.0
SCALE = 1.0 / math.sqrt(HEAD)
SCALE2 = SCALE * math.log2(math.e)
BF = jnp.bfloat16
F32 = jnp.float32


def dot_nt(left, right, out=F32):
    return lax.dot_general(left, right, (((1,), (1,)), ((), ())), preferred_element_type=F32).astype(out)


def dot_nn(left, right, out=F32):
    return lax.dot_general(left, right, (((1,), (0,)), ((), ())), preferred_element_type=F32).astype(out)


def dot_tn(left, right, out=F32):
    return lax.dot_general(left, right, (((0,), (0,)), ((), ())), preferred_element_type=F32).astype(out)


def doc_positions(lengths, total):
    ends = jnp.cumsum(lengths, axis=-1)
    starts = ends - lengths
    places = jnp.arange(total, dtype=jnp.int32)
    segment = jnp.sum((places[:, None] >= ends[..., None, :]).astype(jnp.int32), axis=-1)
    owners = segment[..., None] == jnp.arange(lengths.shape[-1], dtype=jnp.int32)
    first = jnp.sum(jnp.where(owners, starts[..., None, :], 0), axis=-1)
    return first, places - first


def pack_kernel(chips, proj_ref, cos_ref, sin_ref, qg_ref, kg_ref, out_ref):
    per = CORE_Q // chips
    copies = max(1, chips // CORE_KV)
    cos = cos_ref[...]
    sin = sin_ref[...]

    def head(index, gain):
        u = proj_ref[:, index * HEAD : (index + 1) * HEAD]
        factor = lax.rsqrt(jnp.mean(u * u, axis=-1, keepdims=True) + epsilon)
        n = u * factor * gain
        return (n * cos + pltpu.roll(n, HEAD // 2, 1) * sin).astype(BF)

    for z in range(chips):
        for h in range(per):
            out_ref[z, :, h * HEAD : (h + 1) * HEAD] = head(z * per + h, qg_ref[...])
        if z % copies == 0:
            kv = z // copies
            key = head(CORE_Q + kv, kg_ref[...])
            base = (CORE_Q + CORE_KV + kv) * HEAD
            value = proj_ref[:, base : base + HEAD].astype(BF)
        out_ref[z, :, per * HEAD : (per + 1) * HEAD] = key
        out_ref[z, :, (per + 1) * HEAD : (per + 2) * HEAD] = value


def pack_heads(proj, cos, sin, q_gain, k_gain, row, chips, chip_tok):
    per = CORE_Q // chips
    lanes = (per + 2) * HEAD
    block = min(256, chip_tok)
    steps = chip_tok // block
    width = proj.shape[1]
    tok = lambda i: (row * steps + i, 0)
    return pl.pallas_call(
        functools.partial(pack_kernel, chips),
        grid=(steps,),
        in_specs=[
            pl.BlockSpec((block, width), tok),
            pl.BlockSpec((block, HEAD), tok),
            pl.BlockSpec((block, HEAD), tok),
            pl.BlockSpec((1, HEAD), lambda i: (0, 0)),
            pl.BlockSpec((1, HEAD), lambda i: (0, 0)),
        ],
        out_specs=pl.BlockSpec((chips, block, lanes), lambda i: (0, i, 0)),
        out_shape=jax.ShapeDtypeStruct((chips, chip_tok, lanes), BF),
        name="pack_heads",
    )(proj, cos, sin, q_gain, k_gain)


def unpack_kernel(chips, grad_ref, proj_ref, cos_ref, sin_ref, qg_ref, kg_ref, out_ref, qs_ref, ks_ref):
    per = CORE_Q // chips
    copies = max(1, chips // CORE_KV)
    cos = cos_ref[...]
    sin = sin_ref[...]

    @pl.when(pl.program_id(0) == 0)
    def _():
        qs_ref[...] = jnp.zeros_like(qs_ref)
        ks_ref[...] = jnp.zeros_like(ks_ref)

    def head(e, index, gain, sum_ref):
        e = e * cos + pltpu.roll(e * sin, HEAD // 2, 1)
        u = proj_ref[:, index * HEAD : (index + 1) * HEAD]
        factor = lax.rsqrt(jnp.mean(u * u, axis=-1, keepdims=True) + epsilon)
        n = u * factor
        sum_ref[...] += jnp.sum((e * n).reshape(-1, 8, HEAD), axis=0)
        weighted = e * gain
        inner = jnp.mean(weighted * n, axis=-1, keepdims=True)
        out_ref[:, index * HEAD : (index + 1) * HEAD] = (factor * (weighted - n * inner)).astype(BF)

    def part(z, lane):
        return grad_ref[z, :, lane * HEAD : (lane + 1) * HEAD].astype(F32)

    for z in range(chips):
        for h in range(per):
            head(part(z, h), z * per + h, qg_ref[...], qs_ref)
    for kv in range(CORE_KV):
        spread = range(kv * copies, (kv + 1) * copies)
        head(sum(part(z, per) for z in spread), CORE_Q + kv, kg_ref[...], ks_ref)
        base = (CORE_Q + CORE_KV + kv) * HEAD
        out_ref[:, base : base + HEAD] = sum(part(z, per + 1) for z in spread).astype(BF)


def unpack_heads(grads, proj, cos, sin, q_gain, k_gain, row, chips, chip_tok):
    lanes = grads.shape[2]
    block = min(256, chip_tok)
    steps = chip_tok // block
    width = proj.shape[1]
    tok = lambda i: (row * steps + i, 0)
    small = pl.BlockSpec((8, HEAD), lambda i: (0, 0))
    return pl.pallas_call(
        functools.partial(unpack_kernel, chips),
        grid=(steps,),
        in_specs=[
            pl.BlockSpec((chips, block, lanes), lambda i: (0, i, 0)),
            pl.BlockSpec((block, width), tok),
            pl.BlockSpec((block, HEAD), tok),
            pl.BlockSpec((block, HEAD), tok),
            pl.BlockSpec((1, HEAD), lambda i: (0, 0)),
            pl.BlockSpec((1, HEAD), lambda i: (0, 0)),
        ],
        out_specs=[pl.BlockSpec((block, width), lambda i: (i, 0)), small, small],
        out_shape=[
            jax.ShapeDtypeStruct((chip_tok, width), BF),
            jax.ShapeDtypeStruct((8, HEAD), F32),
            jax.ShapeDtypeStruct((8, HEAD), F32),
        ],
        name="unpack_heads",
    )(grads, proj, cos, sin, q_gain, k_gain)


def visible(j, size, start, diagonal):
    inner = lax.broadcasted_iota(jnp.int32, (size, size), 0)
    allowed = inner >= start - j * size
    if diagonal:
        allowed = allowed & (inner <= lax.broadcasted_iota(jnp.int32, (size, size), 1))
    return allowed


def attend_kernel(per, low_ref, q_ref, k_ref, v_ref, start_ref, out_ref, log_ref, acc_ref, sum_ref):
    i = pl.program_id(0)
    size = q_ref.shape[1]
    start = start_ref[...]
    acc_ref[...] = jnp.zeros_like(acc_ref)
    sum_ref[...] = jnp.zeros_like(sum_ref)

    def one(j, diagonal):
        key = k_ref[j]
        value = v_ref[j]
        allowed = visible(j, size, start, diagonal)
        for h in range(per):
            scores = dot_nt(key, q_ref[0, :, h * HEAD : (h + 1) * HEAD])
            p = jnp.where(allowed, jnp.exp2(scores * SCALE2), 0.0)
            sum_ref[h : h + 1, :] += jnp.sum(p, axis=0, keepdims=True)
            acc_ref[h] += dot_tn(value, p.astype(BF))

    def step(j, carry):
        one(j, False)
        return carry

    lax.fori_loop(low_ref[i], i, step, 0)
    one(i, True)
    for h in range(per):
        total = sum_ref[h : h + 1, :]
        out_ref[0, :, h * HEAD : (h + 1) * HEAD] = (acc_ref[h] / total).T.astype(BF)
        log_ref[h : h + 1, :] = jnp.log2(total)


def attend(packed, start, low):
    chips, size, lanes = packed.shape
    per = lanes // HEAD - 2
    return pl.pallas_call(
        functools.partial(attend_kernel, per),
        grid_spec=pltpu.PrefetchScalarGridSpec(
            num_scalar_prefetch=1,
            grid=(chips,),
            in_specs=[
                pl.BlockSpec((1, size, per * HEAD), lambda i, low: (i, 0, 0)),
                pl.BlockSpec((chips, size, HEAD), lambda i, low: (0, 0, per)),
                pl.BlockSpec((chips, size, HEAD), lambda i, low: (0, 0, per + 1)),
                pl.BlockSpec((1, size), lambda i, low: (0, i)),
            ],
            out_specs=[
                pl.BlockSpec((1, size, per * HEAD), lambda i, low: (i, 0, 0)),
                pl.BlockSpec((per, size), lambda i, low: (0, i)),
            ],
            scratch_shapes=[pltpu.VMEM((per, HEAD, size), F32), pltpu.VMEM((per, size), F32)],
        ),
        out_shape=[
            jax.ShapeDtypeStruct((chips, size, per * HEAD), BF),
            jax.ShapeDtypeStruct((per, chips * size), F32),
        ],
        name="attend",
    )(low, packed, packed, packed, start)


def attend_back_kernel(
    per, low_ref, q_ref, k_ref, v_ref, grad_ref, res_ref, log_ref, start_ref, out_ref, dq_ref, dk_ref, dv_ref
):
    i = pl.program_id(0)
    size = q_ref.shape[1]
    start = start_ref[...]

    @pl.when(i == 0)
    def _():
        dk_ref[...] = jnp.zeros_like(dk_ref)
        dv_ref[...] = jnp.zeros_like(dv_ref)

    dq_ref[...] = jnp.zeros_like(dq_ref)
    ones = jnp.ones((8, HEAD), F32)
    inner = []
    for h in range(per):
        cols = slice(h * HEAD, (h + 1) * HEAD)
        both = grad_ref[0, :, cols].astype(F32) * res_ref[0, :, cols].astype(F32)
        sums = lax.dot_general(
            ones, both, (((1,), (1,)), ((), ())), precision=lax.Precision.HIGHEST, preferred_element_type=F32
        )
        inner.append(sums[0:1, :])

    def one(j, diagonal):
        key = k_ref[j]
        value = v_ref[j]
        allowed = visible(j, size, start, diagonal)
        for h in range(per):
            query = q_ref[0, :, h * HEAD : (h + 1) * HEAD]
            grad = grad_ref[0, :, h * HEAD : (h + 1) * HEAD]
            scores = dot_nt(key, query)
            p = jnp.where(allowed, jnp.exp2(scores * SCALE2 - log_ref[h : h + 1, :]), 0.0)
            dp = dot_nt(value, grad)
            ds = (p * (dp - inner[h])).astype(BF)
            dv_ref[j] += dot_nn(p.astype(BF), grad)
            dk_ref[j] += dot_nn(ds, query)
            dq_ref[h] += dot_tn(ds, key)

    def step(j, carry):
        one(j, False)
        return carry

    lax.fori_loop(low_ref[i], i, step, 0)
    one(i, True)
    for h in range(per):
        out_ref[i, :, h * HEAD : (h + 1) * HEAD] = (dq_ref[h] * SCALE).astype(BF)

    @pl.when(i == pl.num_programs(0) - 1)
    def _():
        out_ref[:, :, per * HEAD : (per + 1) * HEAD] = (dk_ref[...] * SCALE).astype(BF)
        out_ref[:, :, (per + 1) * HEAD : (per + 2) * HEAD] = dv_ref[...].astype(BF)


def attend_back(packed, grad, result, logs, start, low):
    chips, size, lanes = packed.shape
    per = lanes // HEAD - 2
    one = pl.BlockSpec((1, size, per * HEAD), lambda i, low: (i, 0, 0))
    return pl.pallas_call(
        functools.partial(attend_back_kernel, per),
        grid_spec=pltpu.PrefetchScalarGridSpec(
            num_scalar_prefetch=1,
            grid=(chips,),
            in_specs=[
                one,
                pl.BlockSpec((chips, size, HEAD), lambda i, low: (0, 0, per)),
                pl.BlockSpec((chips, size, HEAD), lambda i, low: (0, 0, per + 1)),
                one,
                one,
                pl.BlockSpec((per, size), lambda i, low: (0, i)),
                pl.BlockSpec((1, size), lambda i, low: (0, i)),
            ],
            out_specs=pl.BlockSpec((chips, size, lanes), lambda i, low: (0, 0, 0)),
            scratch_shapes=[
                pltpu.VMEM((per, size, HEAD), F32),
                pltpu.VMEM((chips, size, HEAD), F32),
                pltpu.VMEM((chips, size, HEAD), F32),
            ],
        ),
        out_shape=jax.ShapeDtypeStruct((chips, size, lanes), BF),
        name="attend_back",
    )(low, packed, packed, packed, grad, result, logs, start)


def gate_kernel(res_ref, logit_ref, out_ref):
    chips, _, lanes = res_ref.shape
    per = lanes // HEAD
    sig = jax.nn.sigmoid(logit_ref[...])
    for z in range(chips):
        for h in range(per):
            head = z * per + h
            value = res_ref[z, :, h * HEAD : (h + 1) * HEAD].astype(F32)
            out_ref[:, head * HEAD : (head + 1) * HEAD] = (value * sig[:, head : head + 1]).astype(BF)


def gate_rows(result, logits, row):
    chips, size, lanes = result.shape
    block = min(256, size)
    steps = size // block
    return pl.pallas_call(
        gate_kernel,
        grid=(steps,),
        in_specs=[
            pl.BlockSpec((chips, block, lanes), lambda i: (0, i, 0)),
            pl.BlockSpec((block, HEAD), lambda i: (row * steps + i, 0)),
        ],
        out_specs=pl.BlockSpec((block, chips * lanes), lambda i: (i, 0)),
        out_shape=jax.ShapeDtypeStruct((size, chips * lanes), BF),
        name="gate_rows",
    )(result, logits)


def gate_back_kernel(grad_ref, res_ref, logit_ref, out_ref, dlogit_ref):
    chips, size, lanes = res_ref.shape
    per = lanes // HEAD
    sig = jax.nn.sigmoid(logit_ref[...])
    lane = lax.broadcasted_iota(jnp.int32, sig.shape, 1)
    sums = jnp.zeros(sig.shape, F32)
    for z in range(chips):
        for h in range(per):
            head = z * per + h
            e = grad_ref[:, head * HEAD : (head + 1) * HEAD]
            value = res_ref[z, :, h * HEAD : (h + 1) * HEAD].astype(F32)
            out_ref[z, :, h * HEAD : (h + 1) * HEAD] = (e * sig[:, head : head + 1]).astype(BF)
            sums = jnp.where(lane == head, jnp.sum(e * value, axis=-1, keepdims=True), sums)
    dlogit_ref[...] = (sums * sig * (1.0 - sig)).astype(BF)


def gate_back(grad, result, logits, row):
    chips, size, lanes = result.shape
    block = min(256, size)
    steps = size // block
    return pl.pallas_call(
        gate_back_kernel,
        grid=(steps,),
        in_specs=[
            pl.BlockSpec((block, chips * lanes), lambda i: (i, 0)),
            pl.BlockSpec((chips, block, lanes), lambda i: (0, i, 0)),
            pl.BlockSpec((block, HEAD), lambda i: (row * steps + i, 0)),
        ],
        out_specs=[
            pl.BlockSpec((chips, block, lanes), lambda i: (0, i, 0)),
            pl.BlockSpec((block, HEAD), lambda i: (i, 0)),
        ],
        out_shape=[jax.ShapeDtypeStruct((chips, size, lanes), BF), jax.ShapeDtypeStruct((size, HEAD), BF)],
        name="gate_back",
    )(grad, result, logits)


def join_rows_kernel(count, which_ref, *refs):
    out_ref = refs[2 * count]
    size = refs[0].shape[1]
    own_half = pl.program_id(0) == which_ref[0]

    def put(parts):
        for k in range(count):
            out_ref[:, k * size : (k + 1) * size] = parts[k][...].astype(F32)

    pl.when(own_half)(lambda: put(refs[:count]))
    pl.when(jnp.logical_not(own_half))(lambda: put(refs[count : 2 * count]))


def join_rows(mine, other, core, blocks, block):
    count = len(mine)
    height, size = mine[0].shape
    steps = height // block

    def source(side):
        def index(h, i, which):
            active = (h == which[0]) if side == 0 else (h != which[0])
            return (jnp.where(active, i, jnp.where(h == 0, 0, steps - 1)), 0)

        return pl.BlockSpec((block, size), index)

    def target(h, i, which):
        per = which[1]
        return ((i // per) * 2 * per + h * per + i % per, 0)

    return pl.pallas_call(
        functools.partial(join_rows_kernel, count),
        grid_spec=pltpu.PrefetchScalarGridSpec(
            num_scalar_prefetch=1,
            grid=(CORES, steps),
            in_specs=[source(0)] * count + [source(1)] * count,
            out_specs=pl.BlockSpec((block, count * size), target),
        ),
        out_shape=jax.ShapeDtypeStruct((CORES * height, count * size), F32),
        name="join_rows",
    )(jnp.stack([core, blocks.astype(jnp.int32)]), *mine, *other)


def join_cols_kernel(count, per, which_ref, *refs):
    out_ref = refs[2 * count]
    u = pl.program_id(0)
    own_half = pl.program_id(1) == which_ref[0]

    def put(ref):
        out_ref[...] = ref[...].astype(F32)

    for k in range(count):
        here = u // per == k
        pl.when(here & own_half)(functools.partial(put, refs[k]))
        pl.when(here & jnp.logical_not(own_half))(functools.partial(put, refs[count + k]))


def join_cols(mine, other, core, unit):
    count = len(mine)
    height, size = mine[0].shape
    per = size // unit

    def source(k):
        return pl.BlockSpec((height, unit), lambda u, h, which: (0, jnp.clip(u - k * per, 0, per - 1)))

    sources = [source(k) for k in range(count)]
    return pl.pallas_call(
        functools.partial(join_cols_kernel, count, per),
        grid_spec=pltpu.PrefetchScalarGridSpec(
            num_scalar_prefetch=1,
            grid=(count * per, CORES),
            in_specs=sources + sources,
            out_specs=pl.BlockSpec((height, unit), lambda u, h, which: (0, u * CORES + h)),
        ),
        out_shape=jax.ShapeDtypeStruct((height, CORES * count * size), F32),
        name="join_cols",
    )(core[None], *mine, *other)


def join_units_kernel(which_ref, keep_ref, keep_other_ref, sent_ref, sent_other_ref, out_ref):
    kept = pl.program_id(0) == which_ref[1]
    mine = pl.program_id(1) == which_ref[0]
    for side, pair in ((True, (keep_ref, keep_other_ref)), (False, (sent_ref, sent_other_ref))):
        for here, ref in ((True, pair[0]), (False, pair[1])):

            @pl.when((kept == side) & (mine == here))
            def _(ref=ref):
                out_ref[...] = ref[...].astype(F32)


def join_units(mine, other, core, upper):
    height, width = mine[0].shape
    block = 256
    steps = height // block
    sources = []
    for side in (0, 1):
        for half in (0, 1):

            def index(p, h, i, which, side=side, half=half):
                at_side = (p == which[1]) if side == 0 else (p != which[1])
                at_half = (h == which[0]) if half == 0 else (h != which[0])
                side_p = which[1] if side == 0 else 1 - which[1]
                side_h = which[0] if half == 0 else 1 - which[0]
                before = (p * 2 + h) < (side_p * 2 + side_h)
                return (jnp.where(at_side & at_half, i, jnp.where(before, 0, steps - 1)), 0)

            sources.append(pl.BlockSpec((block, width), index))
    return pl.pallas_call(
        join_units_kernel,
        grid_spec=pltpu.PrefetchScalarGridSpec(
            num_scalar_prefetch=1,
            grid=(2, CORES, steps),
            in_specs=sources,
            out_specs=pl.BlockSpec((block, width), lambda p, h, i, which: ((p * CORES + h) * steps + i, 0)),
        ),
        out_shape=jax.ShapeDtypeStruct((2 * CORES * height, width), F32),
        name="join_units",
    )(jnp.stack([core, upper]), mine[0], other[0], mine[1], other[1])


def join_blocks_kernel(which_ref, mine_ref, other_ref, out_ref):
    own_half = pl.program_id(0) == which_ref[0]
    for here, ref in ((True, mine_ref), (False, other_ref)):

        @pl.when(own_half == here)
        def _(ref=ref):
            out_ref[...] = ref[0].astype(F32)


def join_blocks(mine, other, core, order):
    count, height, size = mine.shape
    source = pl.BlockSpec((1, height, size), lambda h, b, which, where: (where[b], 0, 0))
    return pl.pallas_call(
        lambda which_ref, where_ref, *refs: join_blocks_kernel(which_ref, *refs),
        grid_spec=pltpu.PrefetchScalarGridSpec(
            num_scalar_prefetch=2,
            grid=(CORES, count),
            in_specs=[source, source],
            out_specs=pl.BlockSpec((height, size), lambda h, b, which, where: (h, b)),
        ),
        out_shape=jax.ShapeDtypeStruct((CORES * height, count * size), F32),
        name="join_blocks",
    )(core[None], jnp.stack(order).astype(jnp.int32), mine, other)


class Halving:
    def __init__(self, x, dp, flip):
        self.dp = dp
        self.mine = lax.axis_index("dp")
        bits = dp.bit_length() - 1
        self.left = list(range(bits))
        self.order = self.left[::-1] if flip else self.left[:]
        self.x = x.reshape((2,) * bits + (x.shape[0] // dp, x.shape[1]))

    def send(self):
        bit = self.order.pop(0)
        axis = sum(1 for b in self.left if b > bit)
        self.left.remove(bit)
        low, high = lax.index_in_dim(self.x, 0, axis, False), lax.index_in_dim(self.x, 1, axis, False)
        mark = (self.mine >> bit) % 2 == 1
        pairs = [(d, d ^ (1 << bit)) for d in range(self.dp)]
        self.keep = jnp.where(mark, high, low)
        return lax.ppermute(jnp.where(mark, low, high), "dp", pairs)

    def add(self, moved):
        self.x = self.keep + moved


class Line:
    def __init__(self, chips, chip):
        self.chips = chips
        self.inner = (chip == 1) | (chip == 2)
        ends = lambda pairs: [(a * CORES + c, b * CORES + c) for a, b in pairs for c in range(CORES)]
        self.stages = [ends([(0, 1), (3, 2)]), ends([(1, 2), (2, 1)]), ends([(1, 0), (2, 3)])]
        self.groups = [[z * CORES + c for z in range(chips)] for c in range(CORES)]

    def send(self, x, stage):
        if self.chips != 4:
            return (x, lax.psum(x, "seq", axis_index_groups=self.groups) if stage == 0 else x)
        return (x, lax.ppermute(x, "seq", self.stages[stage]))

    def begin(self, x):
        return (0,) + self.send(x, 0)

    def next(self, state):
        stage, x, moved = state
        if self.chips != 4:
            return (stage + 1, moved, moved)
        return (stage + 1,) + self.send(x + moved, stage + 1)

    def end(self, state):
        stage, x, moved = state
        return moved if self.chips != 4 else jnp.where(self.inner, x, moved)

    def pipeline(self, parts, fillers):
        if self.chips != 4:
            done = lax.psum(parts, "seq", axis_index_groups=self.groups)
            made = []
            for filler in fillers.values():
                made.append(filler(done, made))
            return done, made
        count = len(parts)
        states = [None] * count
        made = []
        for step in range(count + 2):
            for k in range(count):
                if k == step:
                    states[k] = self.begin(parts[k])
                elif k < step <= k + 2:
                    states[k] = self.next(states[k])
            done = [self.end(states[k]) if k + 3 <= step else None for k in range(count)]
            extra = fillers[step](done, made) if step in fillers else []
            live = [k for k in range(count) if states[k] is not None]
            later = [k for k in range(step + 1, min(step + 2, count))]
            moved, extra = lax.optimization_barrier(
                ([states[k][1:] for k in live] + [parts[k] for k in later], extra)
            )
            if step in fillers:
                made.append(extra)
            for k, value in zip(live + later, moved):
                if k in later:
                    parts[k] = value
                else:
                    states[k] = (states[k][0], *value)
        return [self.end(state) for state in states], made


def tie_all(values, work):
    return lax.optimization_barrier((values, work))


def tie(value, work):
    leaves, tree = jax.tree.flatten(work)
    moving = [x for x in leaves if not isinstance(x, int)]
    value, *moving = lax.optimization_barrier((value, *moving))
    moving = iter(moving)
    return value, jax.tree.unflatten(tree, [x if isinstance(x, int) else next(moving) for x in leaves])


def shards(
    layer_input,
    doc_lengths,
    attn_norm,
    q_norm,
    k_norm,
    ffn_norm,
    w_qkv,
    w_gate,
    w_out,
    w_gu,
    w_down,
    cotangent,
):
    rows, tok, width = layer_input.shape
    seq = lax.axis_size("seq")
    dp = lax.axis_size("dp")
    chips = seq // CORES
    place = lax.axis_index("seq")
    core = place % CORES
    chip = place // CORES
    first = core == 0
    chip_tok = tok * CORES
    length = tok * seq
    tokens = rows * chip_tok
    pair = [(s, s ^ 1) for s in range(seq)]
    groups = [[z * CORES + c for z in range(chips)] for c in range(CORES)]
    q_shard = lax.axis_index("dp") * w_qkv.shape[0] < QUERY_HEADS * HEAD

    def swap(x):
        return lax.ppermute(x, "seq", pair)

    def pick(a, b):
        return jnp.where(first, a, b)

    def both(x):
        other = swap(x)
        return jnp.concatenate([pick(x, other), pick(other, x)], axis=1).reshape(tokens, width)

    def exchange(x):
        return lax.all_to_all(x, "seq", 0, 0, axis_index_groups=groups, tiled=True)

    def total_sum(x, names=("seq", "dp")):
        for name in names:
            size = lax.axis_size(name)
            step = 1
            while step < size:
                x = x + lax.ppermute(x, name, [(s, s ^ step) for s in range(size)])
                step *= 2
        return x

    def scatter(x):
        return lax.psum_scatter(x, "dp", scatter_dimension=0, tiled=True)

    def gather(x):
        return lax.all_gather(x, "dp", axis=0, tiled=True)

    def core_rows(w, unit):
        return jnp.concatenate(
            [pick(w[a : a + unit], w[a + unit : a + 2 * unit]) for a in range(0, w.shape[0], 2 * unit)], axis=0
        )

    def core_cols(w, unit):
        return jnp.concatenate(
            [pick(w[:, a : a + unit], w[:, a + unit : a + 2 * unit]) for a in range(0, w.shape[1], 2 * unit)],
            axis=1,
        )

    def trade_blocks(x):
        mine = lax.axis_index("dp")
        found = [(mine, lax.dynamic_index_in_dim(x, mine, 0, keepdims=False))]
        for k in range(1, dp):
            out = lax.dynamic_index_in_dim(x, mine ^ k, 0, keepdims=False)
            found.append((mine ^ k, lax.ppermute(out, "dp", [(d, d ^ k) for d in range(dp)])))
        return found

    half_dp = dp // 2
    me = lax.axis_index("dp")
    upper = me >= half_dp
    trade = [(d, d ^ half_dp) for d in range(dp)]
    units = w_gu.shape[0] // 2
    owned = rows * tok

    qkv_half = jnp.where(q_shard, core_rows(w_qkv, GROUP * HEAD), core_rows(w_qkv, HEAD))
    qkv_full = gather(qkv_half)
    out_full = gather(core_cols(w_out, GROUP * HEAD))
    ctg = cotangent.reshape(owned, width)
    gate_count = w_gate.shape[0]
    gate_full = lax.dynamic_update_slice_in_dim(jnp.zeros((QUERY_HEADS, width), BF), w_gate, me * gate_count, 0)
    gate_full = total_sum(gate_full, ("dp",))
    gate_core = jnp.pad(core_rows(gate_full, GROUP), ((0, HEAD - CORE_Q), (0, 0)))

    gu_keep = jnp.where(upper, w_gu[units:], w_gu[:units])
    quarter = units // 2
    gu_send = jnp.where(
        upper, pick(w_gu[:quarter], w_gu[quarter:units]), pick(w_gu[units : units + quarter], w_gu[units + quarter :])
    )
    out_rows = w_down.shape[0] // 2
    down_core = pick(w_down[:out_rows], w_down[out_rows:])
    unit_block = [(d % half_dp) * 2 + d // half_dp for d in range(dp)]
    down_send = jnp.stack([down_core[:, b * units : (b + 1) * units] for b in unit_block])
    (qkv_full, gu_send, down_send) = lax.optimization_barrier((qkv_full, gu_send, down_send))
    gu_pair = lax.all_gather(gu_send, "dp", axis_index_groups=[[d, d + half_dp] for d in range(half_dp)])
    gu_half = jnp.where(upper, gu_pair[0], gu_pair[1])
    down_half = jnp.zeros_like(down_send)
    for other, moved in trade_blocks(down_send):
        down_half = lax.dynamic_update_index_in_dim(down_half, moved, other, 0)

    start, position = doc_positions(doc_lengths, length)
    low = start.reshape(rows, chips, chip_tok)[:, :, 0] // chip_tok
    local = lax.dynamic_slice_in_dim(position, chip * chip_tok, chip_tok, 1).reshape(tokens)
    freq = jnp.power(theta_base, -(jnp.arange(HEAD // 2, dtype=F32) * 2.0) / HEAD)
    angle = local.astype(F32)[:, None] * freq
    cos = jnp.cos(angle)
    sin = jnp.sin(angle)
    cos = jnp.concatenate([cos, cos], axis=1)
    sin = jnp.concatenate([-sin, sin], axis=1)

    inputs = both(layer_input).astype(F32)
    factor_a = lax.rsqrt(jnp.mean(inputs * inputs, axis=-1, keepdims=True) + epsilon)
    normed_a = (inputs * factor_a * attn_norm).astype(BF)
    logits = dot_nt(normed_a, gate_core)
    proj = dot_nt(normed_a, qkv_full)
    q_gain = q_norm[None, :]
    k_gain = k_norm[None, :]

    packed, results, logs, gated, mid = [], [], [], [], []
    for row in range(rows):
        cos_row = cos
        if row:
            cos_row, logits = tie(cos, logits)
        packed.append(exchange(pack_heads(proj, cos_row, sin, q_gain, k_gain, row, chips, chip_tok)))
    packed[0], down_half = tie(packed[0], down_half)
    packed[-1], ctg_late = tie(packed[-1], ctg)
    ctg_all = gather(ctg_late)
    for row in range(rows):
        head_out, log = attend(packed[row], start[row : row + 1], low[row])
        results.append(head_out)
        logs.append(log)
    tok_results = [exchange(r) for r in results]
    gu_other = swap(gu_half)
    down_other = swap(down_half)
    for row in range(rows):
        gated.append(gate_rows(tok_results[row], logits, row))
        part = dot_nt(gated[row], out_full, BF).reshape(CORES, tok, width)
        other = swap(pick(part[1], part[0]))
        mid.append(layer_input[row].astype(F32) + pick(part[0], part[1]).astype(F32) + other.astype(F32))
    mid = jnp.concatenate(mid, axis=0)
    gated = jnp.concatenate(gated, axis=0)

    factor_f = lax.rsqrt(jnp.mean(mid * mid, axis=-1, keepdims=True) + epsilon)
    normed_f = (mid * factor_f * ffn_norm).astype(BF)
    normed_all = gather(normed_f)
    gu_recv = jnp.concatenate([pick(gu_half, gu_other), pick(gu_other, gu_half)], axis=0)
    down_full = jnp.concatenate([pick(down_half, down_other), pick(down_other, down_half)], axis=1)
    down_full = down_full.reshape(width, units)
    d_hidden = dot_nn(ctg_all, down_full, BF)
    normed_all, (d_hidden, gu_recv) = tie(normed_all, (d_hidden, gu_recv))
    keep_part = dot_nt(normed_all, gu_keep, BF)
    recv_part = dot_nt(normed_all, gu_recv, BF)
    gate_part = jnp.where(upper, recv_part, keep_part).astype(F32)
    up_part = jnp.where(upper, keep_part, recv_part).astype(F32)
    d_hid = d_hidden.astype(F32)
    gate_act = jax.nn.sigmoid(gate_part)
    silu = gate_part * gate_act
    hidden = (silu * up_part).astype(BF)
    d_gate = d_hid * up_part * gate_act * (1.0 + gate_part * (1.0 - gate_act))
    d_up = d_hid * silu
    d_keep = jnp.where(upper, d_up, d_gate).astype(BF)
    d_recv = jnp.where(upper, d_gate, d_up).astype(BF)
    d_normed = scatter((dot_nn(d_keep, gu_keep) + dot_nn(d_recv, gu_recv)).astype(BF))

    part_keep = dot_tn(d_keep, normed_all, BF)
    part_recv = dot_tn(d_recv, normed_all, BF)
    part_down = dot_tn(ctg_all, hidden, BF).reshape(dp, CORES, out_rows, units)
    keep_swap = swap(pick(part_keep[quarter:], part_keep[:quarter]))
    recv_swap = swap(pick(part_recv[quarter:], part_recv[:quarter]))
    down_swap = swap(pick(part_down[:, 1], part_down[:, 0]))
    d_normed, (part_keep, part_recv, part_down, keep_swap, recv_swap) = tie(
        d_normed, (part_keep, part_recv, part_down, keep_swap, recv_swap)
    )
    keep_sum = pick(part_keep[:quarter], part_keep[quarter:]) + keep_swap
    recv_sum = pick(part_recv[:quarter], part_recv[quarter:]) + recv_swap
    d_normed, gu_sum = tie(d_normed, jnp.concatenate([keep_sum, recv_sum], axis=0))
    third = gu_sum.shape[0] // 3
    gu_first = lax.psum(gu_sum[:third], "seq", axis_index_groups=groups)
    gu_sum = gu_sum[third:]

    d_normed = d_normed.astype(F32)
    part_ffn = jnp.sum(d_normed * mid * factor_f, axis=0)
    weighted = d_normed * ffn_norm
    inner = jnp.mean(weighted * mid, axis=-1, keepdims=True)
    d_mid = ctg.astype(F32) + factor_f * weighted - mid * factor_f**3 * inner
    low_mine = d_mid.astype(BF).reshape(rows, tok, width)
    low_other = swap(low_mine)
    low_other, down_swap = tie(low_other, down_swap)
    down_sum = pick(part_down[:, 0], part_down[:, 1]) + down_swap
    down_sum = jnp.stack([moved for _, moved in trade_blocks(down_sum)])

    d_mid_low = jnp.concatenate([pick(low_mine, low_other), pick(low_other, low_mine)], axis=1).reshape(tokens, width)
    part_out = dot_tn(d_mid_low, gated, BF)
    d_proj, d_logit, d_heads = [], [], []
    q_sum = 0.0
    k_sum = 0.0
    for row in range(rows):
        low_row = d_mid_low[row * chip_tok : (row + 1) * chip_tok]
        if row == 1:
            out_part = dot_nt(hidden, down_full, BF)
            low_row, (part_out, out_part) = tie(low_row, (part_out, out_part))
        d_gated = dot_nn(low_row, out_full)
        d_attn, dl = gate_back(d_gated, tok_results[row], logits, row)
        if row == 0:
            d_attn, hidden = tie(d_attn, hidden)
        d_logit.append(dl)
        d_heads.append(exchange(d_attn))
    d_heads[0], (gu_first, gu_sum) = tie(d_heads[0], (gu_first, gu_sum))
    gu_sum = lax.psum(gu_sum, "seq", axis_index_groups=groups)
    back = []
    for row in range(rows):
        grads = attend_back(packed[row], d_heads[row], results[row], logs[row], start[row : row + 1], low[row])
        back.append(exchange(grads))
    shard_out = scatter(part_out)
    back[1], down_sum = tie(back[1], down_sum)
    for row in range(rows):
        dpr, qs, ks = unpack_heads(back[row], proj, cos, sin, q_gain, k_gain, row, chips, chip_tok)
        d_proj.append(dpr)
        q_sum = q_sum + qs
        k_sum = k_sum + ks
    d_proj = jnp.concatenate(d_proj, axis=0)
    d_logit = jnp.concatenate(d_logit, axis=0)
    half = width // 2
    part_qkv = [dot_tn(d_proj, normed_a[:, a : a + half], BF) for a in (0, half)]
    part_qkv, (gu_sum, out_part, d_proj, down_sum) = tie_all(part_qkv, (gu_sum, out_part, d_proj, down_sum))
    trading = [Halving(p, dp, flip) for p, flip in zip(part_qkv, (False, True))]
    moved = [t.send() for t in trading]
    while trading[0].order:
        for t, m in zip(trading, moved):
            t.add(m)
        moved = [t.send() for t in trading]
    for t, m in zip(trading, moved):
        t.add(m)
    shard_qkv = [t.x for t in trading]
    d_norm_part = (dot_nn(d_proj, qkv_full) + dot_nn(d_logit, gate_core)).astype(BF)
    d_norm_part = d_norm_part.reshape(rows, CORES, tok, width)
    d_norm_other = swap(pick(d_norm_part[:, 1], d_norm_part[:, 0]))
    d_normed_a = pick(d_norm_part[:, 0], d_norm_part[:, 1]).astype(F32) + d_norm_other.astype(F32)
    own_in = layer_input.astype(F32)
    own_factor = lax.rsqrt(jnp.mean(own_in * own_in, axis=-1, keepdims=True) + epsilon)
    part_attn = jnp.sum(d_normed_a * own_in * own_factor, axis=(0, 1))
    weighted_a = d_normed_a * attn_norm
    inner_a = jnp.mean(weighted_a * own_in, axis=-1, keepdims=True)
    grad_input = (
        d_mid.reshape(rows, tok, width) + own_factor * weighted_a - own_in * own_factor**3 * inner_a
    ).astype(BF)

    heads = jnp.concatenate([jnp.sum(q_sum, axis=0), jnp.sum(k_sum, axis=0)])
    heads = jnp.pad(heads, (0, width - heads.shape[0]))

    def norm_done(done, made):
        return [part_attn, grad_input]

    part_gate = dot_tn(d_logit, normed_a)[:CORE_Q]
    zero = jnp.zeros_like(part_gate)
    part_gate = jnp.stack(
        [pick(part_gate, zero).reshape(-1, GROUP, width), pick(zero, part_gate).reshape(-1, GROUP, width)], 1
    )
    part_gate = part_gate.reshape(QUERY_HEADS, width)
    small = jnp.concatenate([part_gate, part_ffn[None], part_attn[None], heads[None], jnp.zeros((5, width), F32)], axis=0)
    hops = [("seq", 1)] + [("dp", 1 << k) for k in range(dp.bit_length() - 1)]
    mid_cut = down_sum.shape[1] // 2
    parts = [down_sum[:, :mid_cut], down_sum[:, mid_cut:], shard_out, *shard_qkv]

    def hop(x, some):
        for name, bit in some:
            x = x + lax.ppermute(x, name, [(p, p ^ bit) for p in range(lax.axis_size(name))])
        return x

    keep = jnp.concatenate([gu_first, gu_sum[: quarter - third]], axis=0)
    sent = lax.ppermute(gu_sum[quarter - third :], "dp", trade)

    def near_sum(done, made):
        return [hop(small, hops[:2]), out_part]

    def far_sum(done, made):
        total = hop(made[-1][0], hops[2:])
        if chips == 4:
            wide = total.astype(BF)
            parts[4] = jnp.concatenate([parts[4], wide[:, :half], wide[:, half:]], axis=0)
        else:
            total = lax.psum(total, "seq", axis_index_groups=groups)
        return [total, made[-1][1], sent]

    line = Line(chips, chip)
    def join_early(done, made):
        down_done = jnp.concatenate(done[:2], axis=1)
        sent = made[2][2]
        places = [unit_block.index(b) ^ me for b in range(dp)]
        return [
            join_units([keep, sent], [swap(keep), swap(sent)], core, upper.astype(jnp.int32)),
            join_blocks(down_done, swap(down_done), core, places),
        ]

    def join_late(done, made):
        output = (mid + scatter(made[2][1]).astype(F32)).astype(BF).reshape(rows, tok, width)
        return [join_cols([done[2]], [swap(done[2])], core, GROUP * HEAD), output]

    sums, ((_, grad_input), _, (small, *_), (grad_gu, grad_down), (grad_out, output)) = line.pipeline(
        parts, {1: norm_done, 2: near_sum, 3: far_sum, 5: join_early, 6: join_late}
    )
    if chips == 4:
        body = shard_qkv[0].shape[0]
        count = (sums[4].shape[0] - body) // 2
        small = jnp.concatenate([sums[4][body : body + count], sums[4][body + count :]], axis=1).astype(F32)
    grad_w_gate = lax.dynamic_slice_in_dim(small, me * gate_count, gate_count, 0)
    qkv_sum = sums[3:]
    grad_qkv = join_rows(qkv_sum, [swap(p) for p in qkv_sum], core, jnp.where(q_shard, GROUP, 1), HEAD)
    return (
        output,
        grad_input,
        small[QUERY_HEADS + 1],
        small[QUERY_HEADS + 2, :HEAD],
        small[QUERY_HEADS + 2, HEAD : 2 * HEAD],
        small[QUERY_HEADS],
        grad_qkv,
        grad_w_gate,
        grad_out,
        grad_gu,
        grad_down,
    )


def solution(mesh):
    token = P("dp", "seq", None)
    shard = P("dp", None)
    in_specs = (token, shard, P(), P(), P(), P(), shard, shard, shard, shard, shard, token)
    out_specs = (token, token, P(), P(), P(), P(), shard, shard, shard, shard, shard)
    return jax.shard_map(shards, mesh=mesh, in_specs=in_specs, out_specs=out_specs, check_vma=False)
```
